32 devices in a mesh: groups: 2 (over x), space: 16 (over z, y, core).
Axes of the slice: x: 2, y: 2, z: 4, core: 2. Of those that a mesh axis runs over, the one named last changes fastest.
Arguments:
- noisy: bfloat16 [16384, 512], P(('groups', 'space')), parts along dimension 0, may hold values from -6 to 6
- matches: int32 [3072, 16], P(('groups', 'space')), parts along dimension 0, may hold values from 0 to 8191, as said below
- cube_home: int32 [16384], P('groups'), parts along dimension 0, may hold values from 0 to 8191, as said below
- sigma_coef: float32 [512], replicated, may hold values from 0.3 to 1.5
Outputs:
- basic: bfloat16 [16384, 512], P(('groups', 'space')), parts along dimension 0
- final: bfloat16 [16384, 512], P(('groups', 'space')), parts along dimension 0
The draws below stay inside these ranges and needn't reach their ends.
There are 2 independent parts, one for each index of `groups`. The reference program is written for one: setup_inputs(seed, part) draws one part's arguments, and reference() takes and returns one part's arrays. A program takes and returns all parts, laid end to end along the dimension named above; an argument that names none is the same for every part. Nothing has to cross between parts.
Inputs may be any that keep to these rules, and one draw needn't show every extreme that they name: `matches`: each device's 16 * 96 list entries name at most 192 cubes whose table rows lie in any one device's block of 512 rows; in every draw one block receives exactly 192 from every device. `cube_home`: A permutation of the table rows.
All inputs are finite; a program needn't handle non-finite values.
Results may differ from the reference program's by a relative error of at most 0.0079.
Values may be sent and summed in bfloat16 or wider, within the bound.
A program may use at most 64 MiB of HBM per device.

```python
import math
import jax
import jax.numpy as jnp
from jax import lax

CUBE = 512
M = 16
REF_DEV = 96
CUBES_DEV = 512
CUBES = 8192
CAP = 192
N_SPACE = 16


def make_plan(key):
    base = jax.random.fold_in(key, 7)
    key_home, key_hot, key_slots, key_mix, key_local = jax.random.split(base, 5)
    entries = M * REF_DEV
    places = N_SPACE * CAP
    home = jax.random.permutation(key_home, CUBES_DEV * N_SPACE)
    hotter = jax.random.randint(key_hot, (), 0, N_SPACE)
    slot_keys = jax.random.split(key_slots, N_SPACE)
    orders = jax.vmap(lambda k: jax.random.permutation(k, places))(slot_keys)
    holder = jnp.arange(places, dtype=jnp.int32) // CAP
    scores = orders + jnp.where(holder == hotter, 0, places)[None, :]
    chosen = jnp.argsort(scores, axis=1, stable=True)[:, :entries]
    mix_keys = jax.random.split(key_mix, N_SPACE)
    mixing = jax.vmap(lambda k: jax.random.permutation(k, entries))(mix_keys)
    chosen = jnp.take_along_axis(chosen, mixing, axis=1)
    owner = chosen // CAP
    local = jax.random.randint(key_local, (N_SPACE, entries), 0, CUBES_DEV)
    table_row = owner * CUBES_DEV + local
    identity = jnp.argsort(home, stable=True).astype(jnp.int32)
    ids = identity[table_row.reshape(-1)].reshape(N_SPACE * REF_DEV, M)
    return (home.astype(jnp.int32), ids.astype(jnp.int32))


def draw_cube_home(key, part):
    return make_plan(key)[0]


def draw_matches(key, part):
    return make_plan(key)[1]


def level_of(own_key, extent, shards, smallest, high):
    def one(position, blocks):
        heights = jax.random.uniform(jax.random.fold_in(jax.random.fold_in(own_key, 6), position), (blocks,), jnp.float32, smallest / len(shards), high / len(shards))
        return jnp.repeat(jnp.exp(heights), extent[position] // blocks).reshape((-1,) + (1,) * (len(extent) - position - 1))

    loudness = one(*shards[0])
    for cut in shards[1:]:
        loudness = loudness * one(*cut)
    return loudness


def gaussian(rng, dims, deviation, reach, cuts=(), kind=jnp.bfloat16):
    drawn = deviation * jax.random.normal(rng, dims, jnp.float32)
    if cuts:
        drawn = drawn * level_of(rng, dims, cuts, -0.22, 0.18)
    return jnp.clip(drawn, -reach, reach).astype(kind)


def setup_inputs(seed: int = 0, part: int = 0) -> dict:
    arg_keys = jax.random.split(jax.random.key(seed), 5)
    own_keys = jax.random.split(jax.random.fold_in(arg_keys[4], part), 5)
    return {
        "noisy": gaussian(own_keys[0], (CUBES, CUBE), 1.0, 6.0, ((0, 16),)),
        "matches": draw_matches(jax.random.fold_in(jax.random.fold_in(arg_keys[4], part), 71), part),
        "cube_home": draw_cube_home(jax.random.fold_in(jax.random.fold_in(arg_keys[4], part), 71), part),
        "sigma_coef": jnp.clip(jnp.exp(jax.random.uniform(arg_keys[3], (CUBE,), jnp.float32, math.log(0.3), math.log(1.5))), 0.3, 1.5),
    }


shrink_level = 2.7
prior_weight = 0.5

def dct_matrix(length):
    index = jnp.arange(length, dtype=jnp.float32)
    freq = index[:, None]
    table = jnp.cos(jnp.pi * (2.0 * index[None, :] + 1.0) * freq / (2.0 * length)) * jnp.sqrt(2.0 / length)
    return jnp.where(freq == 0, table / jnp.sqrt(2.0), table)

def make_tables(group):
    small = dct_matrix(8)
    cube_table = jnp.einsum('ad,be,cf->abcdef', small, small, small).reshape(512, 512).astype(jnp.bfloat16)
    return (cube_table, dct_matrix(group))

def forward(members, cube_table, group_table):
    spec = jnp.dot(members.reshape(-1, members.shape[-1]), cube_table.T, preferred_element_type=jnp.float32)
    spec = spec.reshape(members.shape)
    return jnp.einsum('jm,rmk->rjk', group_table, spec, precision=lax.Precision.HIGHEST)

def backward(coeffs, cube_table, group_table):
    back = jnp.einsum('jm,rjk->rmk', group_table, coeffs, precision=lax.Precision.HIGHEST).astype(jnp.bfloat16)
    out = jnp.dot(back.reshape(-1, back.shape[-1]), cube_table, preferred_element_type=jnp.float32)
    return out.reshape(coeffs.shape)

def aggregate(parts, weights, targets, noisy, count):
    numer = jax.ops.segment_sum(parts.astype(jnp.float32), targets, count)
    denom = jax.ops.segment_sum(weights.astype(jnp.float32), targets, count)
    return ((numer + prior_weight * noisy.astype(jnp.float32)) / (denom[:, None] + prior_weight)).astype(jnp.bfloat16)

def first_phase(coeffs, sigma_coef, cube_table, group_table):
    level = (shrink_level * sigma_coef) ** 2
    square = coeffs * coeffs
    gain = square / (square + level)
    weight = 1.0 / (0.25 + lax.optimization_barrier(jnp.mean(gain * gain, axis=(1, 2))))
    out = backward(gain * coeffs, cube_table, group_table)
    part = (weight[:, None, None] * out).astype(jnp.bfloat16)
    wcopy = jnp.broadcast_to(weight[:, None], out.shape[:2]).astype(jnp.bfloat16)
    return (part, wcopy)

def second_phase(coeffs, gcoeffs, sigma_coef, cube_table, group_table):
    noise = sigma_coef * sigma_coef
    square = gcoeffs * gcoeffs
    wiener = square / (square + noise)
    weight = 1.0 / (0.25 + lax.optimization_barrier(jnp.mean(wiener * wiener * noise, axis=(1, 2))))
    out = backward(wiener * coeffs, cube_table, group_table)
    part = (weight[:, None, None] * out).astype(jnp.bfloat16)
    wcopy = jnp.broadcast_to(weight[:, None], out.shape[:2]).astype(jnp.bfloat16)
    return (part, wcopy)

def reference(noisy, matches, cube_home, sigma_coef):
    cube_table, group_table = make_tables(matches.shape[1])
    rows = cube_home[matches]
    flat_rows = rows.reshape(-1)
    count = noisy.shape[0]
    width = noisy.shape[1]
    members = noisy[rows]
    coeffs = forward(members, cube_table, group_table)
    part, wcopy = first_phase(coeffs, sigma_coef, cube_table, group_table)
    basic = aggregate(part.reshape(-1, width), wcopy.reshape(-1), flat_rows, noisy, count)
    guide = basic[rows]
    gcoeffs = forward(guide, cube_table, group_table)
    part2, wcopy2 = second_phase(coeffs, gcoeffs, sigma_coef, cube_table, group_table)
    final = aggregate(part2.reshape(-1, width), wcopy2.reshape(-1), flat_rows, noisy, count)
    return (basic, final)
```

```python
import functools

import jax
import jax.numpy as jnp
import numpy as np
from jax import lax
from jax.experimental import pallas as pl
from jax.experimental.pallas import tpu as pltpu
from jax.sharding import PartitionSpec as P

shrink_level = 2.7
prior_weight = 0.5
LANES = 128
SUBS = 8
PIECES = 2
STREAMS = 4
TOGETHER = 2
LIMIT = 60 * 1024 * 1024
MESH = pl.DeviceIdType.MESH
VMEM = pl.BlockSpec(memory_space=pltpu.VMEM)
SMEM = pl.BlockSpec(memory_space=pltpu.SMEM)
HBM = pl.BlockSpec(memory_space=pltpu.HBM)
SEMS = pltpu.SemaphoreType.DMA


def dct_matrix(length):
    index = np.arange(length, dtype=np.float64)
    table = np.cos(np.pi * (2.0 * index[None, :] + 1.0) * index[:, None] / (2.0 * length))
    table = table * np.sqrt(2.0 / length)
    table[0] /= np.sqrt(2.0)
    return table


def cube_tables():
    small = dct_matrix(8)
    cube = np.kron(np.kron(small, small), small).astype(np.float32)
    return cube.astype(jnp.bfloat16), cube.T.astype(jnp.bfloat16)


def half_cosines(n):
    return [float(2.0 * np.cos(np.pi * (2 * i + 1) / (2 * n))) for i in range(n // 2)]


def cosine_sums(x):
    n = len(x)
    if n == 2:
        return [x[0] + x[1], (x[0] - x[1]) * float(np.cos(np.pi / 4))]
    half = n // 2
    even = cosine_sums([x[i] + x[n - 1 - i] for i in range(half)])
    turned = cosine_sums([(x[i] - x[n - 1 - i]) * f for i, f in enumerate(half_cosines(n))])
    out = [None] * n
    for k in range(half):
        out[2 * k] = even[k]
        out[2 * k + 1] = turned[k] - out[2 * k - 1] if k else 0.5 * turned[0]
    return out


def cosine_sums_transposed(y):
    n = len(y)
    if n == 2:
        odd = y[1] * float(np.cos(np.pi / 4))
        return [y[0] + odd, y[0] - odd]
    half = n // 2
    even = cosine_sums_transposed(y[0::2])
    tail = [None] * half
    for k in reversed(range(half)):
        tail[k] = y[2 * k + 1] - tail[k + 1] if k + 1 < half else y[2 * k + 1]
    tail[0] = 0.5 * tail[0]
    odd = [o * f for o, f in zip(cosine_sums_transposed(tail), half_cosines(n))]
    return [even[i] + odd[i] for i in range(half)] + [even[i] - odd[i] for i in reversed(range(half))]


def scales(n):
    return [float(np.sqrt((1.0 if k == 0 else 2.0) / n)) for k in range(n)]


def flip(value, mask):
    bit = 1
    while bit <= mask:
        if mask & bit:
            value = value + bit - 2 * bit * lax.rem(value // bit, 2)
        bit *= 2
    return value


def lowest(d, count):
    return d & -d if d else count


class Place:
    def __init__(self, count, parts):
        self.parts, self.ranks = parts, count // parts
        me = lax.axis_index("space")
        self.part, self.rank = me // self.ranks, lax.rem(me, self.ranks)
        self.bits = [1 << b for b in range(self.ranks.bit_length() - 1)]

    def index(self, off, d):
        return flip(self.part, off) * self.ranks + flip(self.rank, d)

    def device(self, off, d):
        return {"space": self.index(off, d)}

    def greet(self):
        barrier = pltpu.get_barrier_semaphore()
        peers = [(off, 0) for off in range(1, self.parts)] + [(0, d) for d in range(1, self.ranks)]
        for off, d in peers:
            pl.semaphore_signal(barrier, inc=1, device_id=self.device(off, d), device_id_type=MESH)
        pl.semaphore_wait(barrier, len(peers))


def remote(src, dst, send, recv, device):
    return pltpu.make_async_remote_copy(
        src_ref=src, dst_ref=dst, send_sem=send, recv_sem=recv, device_id=device, device_id_type=MESH
    )


def piece_of(ref, h):
    size = ref.shape[0] // PIECES
    return ref.at[pl.ds(h * size, size), :]


class Spread:
    def __init__(self, place, stage, got, table, send, recv):
        self.place, self.stage, self.got, self.table = place, stage, got, table
        self.send, self.recv, self.started = send, recv, []

    def block(self, off, d):
        return self.stage.at[0] if off == 0 and d == 0 else self.got.at[off, d]

    def pass_on(self, off, d, h):
        place = self.place
        for bit in reversed(place.bits):
            if bit < lowest(d, place.ranks):
                copy = remote(
                    piece_of(self.block(off, d), h),
                    piece_of(self.got.at[off, d | bit], h),
                    self.send.at[off, d | bit, h],
                    self.recv.at[off, d | bit, h],
                    place.device(0, bit),
                )
                copy.start()
                self.started.append(copy)

    def begin(self, rows, cube_t):
        place = self.place
        for off in list(range(place.parts - 1, 0, -1)) + [0]:
            columns = pl.ds(pl.multiple_of(flip(place.part, off) * LANES, LANES), LANES)
            spec = jnp.dot(rows, cube_t[:, columns], preferred_element_type=jnp.float32)
            self.stage[off] = spec.astype(self.stage.dtype)
            for h in range(PIECES):
                if off == 0:
                    self.pass_on(0, 0, h)
                    continue
                copy = remote(
                    piece_of(self.stage.at[off], h),
                    piece_of(self.got.at[off, 0], h),
                    self.send.at[off, 0, h],
                    self.recv.at[off, 0, h],
                    place.device(off, 0),
                )
                copy.start()
                self.started.append(copy)

    def widen(self, off, d, h):
        source = piece_of(self.block(off, d), h)
        held = self.stage.shape[1]
        size = held // PIECES
        first = self.place.index(off, d) * held + h * size
        rows = pl.ds(pl.multiple_of(first, size), size)
        self.table[rows, :] = source[...].astype(jnp.float32)

    def finish(self):
        place = self.place

        def when(key):
            off, d, h = key
            return (place.parts - off if off else 0) + 0.5 * h + sum(0.3 if b == 1 else 1.0 for b in place.bits if d & b)

        keys = [
            (off, d, h)
            for off in range(place.parts)
            for d in range(place.ranks)
            for h in range(PIECES)
            if off or d
        ]
        for h in range(PIECES):
            self.widen(0, 0, h)
        for off, d, h in sorted(keys, key=when):
            piece = piece_of(self.got.at[off, d], h)
            remote(
                piece, piece, self.send.at[off, d, h], self.recv.at[off, d, h], place.device(off, d)
            ).wait_recv()
            self.pass_on(off, d, h)
            self.widen(off, d, h)

    def close(self):
        for copy in self.started:
            copy.wait_send()


def spread_scratch(count, parts, held, dtype):
    ranks = count // parts
    return [
        pltpu.VMEM((parts, held, LANES), dtype),
        pltpu.VMEM((parts, ranks, held, LANES), dtype),
        pltpu.VMEM((count * held, LANES), jnp.float32),
        SEMS((parts, ranks, PIECES)),
        SEMS((parts, ranks, PIECES)),
    ]


def pick_rows(table, lists, members, some):
    parts, group = lists.shape[:2]
    for src in range(parts):

        def step(q, carry):
            for m in range(group):
                members[m, pl.ds(src * some + q, 1), :] = table[pl.ds(lists[src, m, q], 1), :]
            return carry

        lax.fori_loop(0, some, step, 0, unroll=4)


def diagonal(rows):
    shape = (rows, LANES)
    return lax.broadcasted_iota(jnp.int32, shape, 0) == lax.broadcasted_iota(jnp.int32, shape, 1)


def shrink_groups(place, second, width, some, sigma, members, coeffs, back, energy, ebuf, egot, weights, send, recv):
    group, refs = members.shape[:2]
    factor = scales(group)
    columns = pl.ds(pl.multiple_of(place.part * LANES, LANES), LANES)
    own = sigma[:, columns]
    level = own * own if second else (shrink_level * own) * (shrink_level * own)

    def forward(b, carry):
        rows = pl.ds(pl.multiple_of(b * SUBS, SUBS), SUBS)
        values = cosine_sums([members[m, rows, :] for m in range(group)])
        total = None
        for j in range(group):
            value = values[j] * factor[j]
            square = value * value
            gain = square / (square + level)
            power = gain * gain
            total = power if total is None else total + power
            if second:
                members[j, rows, :] = gain * coeffs[j, rows, :]
            else:
                coeffs[j, rows, :] = value
                members[j, rows, :] = gain * value
        energy[rows, :] = total * level if second else total
        return carry

    lax.fori_loop(0, refs // SUBS, forward, 0)
    parts = refs // some
    for src in range(parts):
        column = jnp.sum(energy[src * some : (src + 1) * some, :], axis=1, keepdims=True)
        ebuf[src : src + 1, :] = jnp.sum(jnp.where(diagonal(some), column, 0.0), axis=0, keepdims=True)
    started = []
    for off in range(1, place.parts):
        copy = remote(ebuf, egot.at[off], send.at[off], recv.at[off], place.device(off, 0))
        copy.start()
        started.append(copy)

    def inverse(b, carry):
        rows = pl.ds(pl.multiple_of(b * 2 * SUBS, 2 * SUBS), 2 * SUBS)
        values = cosine_sums_transposed([members[j, rows, :] * factor[j] for j in range(group)])
        for m in range(group):
            back[m, rows, :] = values[m].astype(back.dtype)
        return carry

    lax.fori_loop(0, refs // (2 * SUBS), inverse, 0)
    total = ebuf[...]
    for off in range(1, place.parts):
        remote(ebuf, egot.at[off], send.at[off], recv.at[off], place.device(off, 0)).wait_recv()
        total = total + egot[off]
    weights[...] = 1.0 / (0.25 + total / (group * width))
    for copy in started:
        copy.wait_send()


def shrink_scratch(parts, group, refs):
    assert parts <= SUBS
    return [
        pltpu.VMEM((group, refs, LANES), jnp.float32),
        pltpu.VMEM((refs, LANES), jnp.float32),
        pltpu.VMEM((SUBS, LANES), jnp.float32),
        pltpu.VMEM((parts, SUBS, LANES), jnp.float32),
        SEMS((parts,)),
        SEMS((parts,)),
    ]


def first_kernel(count, x, home, ids, sigma, cube_t, coeffs, back, weights, lists_out, *scratch):
    stage, got, table, send, recv = scratch[:5]
    members, energy, ebuf, egot, esend, erecv = scratch[5:11]
    named, lists_v, lists_s, lsend, lrecv, lsem = scratch[11:]
    parts = stage.shape[0]
    group, some = ids.shape
    place = Place(count, parts)
    place.greet()
    spread = Spread(place, stage, got, table, send, recv)
    spread.begin(x[...], cube_t)

    def look_up(m, carry):
        for q in range(some):
            named[m, q] = home[ids[m, q]]
        for q in range(some, LANES):
            named[m, q] = 0
        return carry

    lax.fori_loop(0, group, look_up, 0)
    ebuf[...] = jnp.zeros(ebuf.shape, ebuf.dtype)
    mine = pltpu.make_async_copy(named, lists_v.at[place.part], lsem.at[0])
    mine.start()
    mine.wait()
    started = []
    for off in range(1, parts):
        copy = remote(
            lists_v.at[place.part],
            lists_v.at[place.part],
            lsend.at[off],
            lrecv.at[off],
            place.device(off, 0),
        )
        copy.start()
        started.append(copy)
    spread.finish()
    copies = []
    for off in range(parts):
        source = lists_v.at[flip(place.part, off)]
        if off:
            remote(source, source, lsend.at[off], lrecv.at[off], place.device(off, 0)).wait_recv()
        copy = pltpu.make_async_copy(source, lists_s.at[flip(place.part, off)], lsem.at[off])
        copy.start()
        copies.append(copy)
    for copy in copies:
        copy.wait()
    lists_out[...] = lists_v[...]
    pick_rows(table, lists_s, members, some)
    shrink_groups(
        place, False, x.shape[1], some, sigma, members, coeffs, back, energy, ebuf, egot, weights, esend, erecv
    )
    for copy in started:
        copy.wait_send()
    spread.close()


class Collect:
    def __init__(self, place, acc, own, got, sent, zgot, local, send, recv):
        self.place, self.acc, self.own, self.got, self.sent, self.zgot = place, acc, own, got, sent, zgot
        self.local, self.send, self.recv, self.started = local, send, recv, []
        self.order = list(range(place.parts - 1, -1, -1))

    def start(self, copy):
        copy.start()
        self.started.append(copy)

    def fetch(self, off, d):
        return pltpu.make_async_copy(
            self.acc.at[self.place.index(off, d)], self.own.at[off, d // 2], self.local.at[off, d // 2]
        )

    def open(self):
        place = self.place
        for d in sorted(range(0, place.ranks, 2), key=lambda d: lowest(d, place.ranks)):
            for off in self.order:
                self.fetch(off, d).start()

    def begin(self):
        place = self.place
        for d in sorted(range(1, place.ranks, 2), key=lambda d: lowest(d - 1, place.ranks)):
            for off in self.order:
                for h in range(PIECES):
                    self.start(
                        remote(
                            piece_of(self.acc.at[place.index(off, d)], h),
                            piece_of(self.got.at[off, d], h),
                            self.send.at[off, d, h],
                            self.recv.at[off, d, h],
                            place.device(0, 1),
                        )
                    )

    def value(self, off, d, h):
        place = self.place
        if h == 0:
            self.fetch(off, d).wait()
        total = piece_of(self.own.at[off, d // 2], h)[...].astype(jnp.float32)
        for bit in place.bits:
            if bit < lowest(d, place.ranks):
                piece = piece_of(self.got.at[off, d | bit], h)
                remote(
                    piece, piece, self.send.at[off, d | bit, h], self.recv.at[off, d | bit, h], place.device(0, bit)
                ).wait_recv()
                total = total + piece[...].astype(jnp.float32)
        return total

    def run(self):
        place = self.place
        for d in sorted(range(0, place.ranks, 2), key=lambda d: lowest(d, place.ranks)):
            for off in self.order:
                for h in range(PIECES):
                    piece = piece_of(self.sent.at[off, d // 2], h)
                    piece[...] = self.value(off, d, h).astype(self.sent.dtype)
                    if d == 0 and off == 0:
                        continue
                    bit = lowest(d, 0)
                    self.start(
                        remote(
                            piece,
                            piece_of(self.got.at[off, d] if d else self.zgot.at[off], h),
                            self.send.at[off, d, h],
                            self.recv.at[off, d, h],
                            place.device(0, bit) if d else place.device(off, 0),
                        )
                    )

    def slices(self, h):
        place = self.place
        yield 0, piece_of(self.sent.at[0, 0], h)[...]
        for off in self.order[:-1]:
            piece = piece_of(self.zgot.at[off], h)
            remote(
                piece, piece, self.send.at[off, 0, h], self.recv.at[off, 0, h], place.device(off, 0)
            ).wait_recv()
            yield off, piece[...]

    def close(self):
        for copy in self.started:
            copy.wait_send()


def settle(place, acc, wsum, noisy, cube, out, own, got, sent, zgot, wgot, local, send, recv, wsend, wrecv):
    held = noisy.shape[0]
    collect = Collect(place, acc, own, got, sent, zgot, local, send, recv)
    collect.open()
    place.greet()
    collect.begin()
    for d in range(1, place.ranks):
        collect.start(
            remote(wsum.at[flip(place.rank, d)], wgot.at[d], wsend.at[d], wrecv.at[d], place.device(0, d))
        )
    collect.run()
    denom = wsum[place.rank]
    for d in range(1, place.ranks):
        remote(wgot.at[d], wgot.at[d], wsend.at[d], wrecv.at[d], place.device(0, d)).wait_recv()
        denom = denom + wgot[d]
    size = held // PIECES
    for h in range(PIECES):
        numer = prior_weight * noisy[pl.ds(h * size, size), :].astype(jnp.float32)
        for off, part in collect.slices(h):
            rows = pl.ds(pl.multiple_of(flip(place.part, off) * LANES, LANES), LANES)
            numer = numer + jnp.dot(part, cube[rows, :], preferred_element_type=jnp.float32)
        for j in range(size // LANES):
            row = h * (size // LANES) + j
            spread = jnp.broadcast_to(denom[row : row + 1, :], (LANES, LANES))
            column = jnp.sum(jnp.where(diagonal(LANES), spread, 0.0), axis=1, keepdims=True)
            out[pl.ds(row * LANES, LANES), :] = (
                numer[j * LANES : (j + 1) * LANES, :] / (column + prior_weight)
            ).astype(out.dtype)
    return collect


def settle_scratch(count, parts, held, dtype):
    ranks = count // parts
    half = (parts, ranks // 2, held, LANES)
    return [
        pltpu.VMEM(half, dtype),
        pltpu.VMEM((parts, ranks, held, LANES), dtype),
        pltpu.VMEM(half, dtype),
        pltpu.VMEM((parts, held, LANES), dtype),
        pltpu.VMEM((ranks, SUBS, LANES), jnp.float32),
        SEMS((parts, ranks // 2)),
        SEMS((parts, ranks, PIECES)),
        SEMS((parts, ranks, PIECES)),
        SEMS((ranks,)),
        SEMS((ranks,)),
    ]


def second_kernel(count, some, acc, wsum, noisy, cube, cube_t, sigma, lists, coeffs_in, basic, back, weights, *scratch):
    stage, got, table, send, recv = scratch[:5]
    members, energy, ebuf, egot, esend, erecv = scratch[5:11]
    coeffs, csem = scratch[11:13]
    parts = stage.shape[0]
    place = Place(count, parts)
    fetch = pltpu.make_async_copy(coeffs_in, coeffs, csem.at[0])
    fetch.start()
    collect = settle(place, acc, wsum, noisy, cube, basic, *scratch[13:])
    spread = Spread(place, stage, got, table, send, recv)
    spread.begin(basic[...], cube_t)
    ebuf[...] = jnp.zeros(ebuf.shape, ebuf.dtype)
    spread.finish()
    pick_rows(table, lists, members, some)
    fetch.wait()
    shrink_groups(
        place, True, noisy.shape[1], some, sigma, members, coeffs, back, energy, ebuf, egot, weights, esend, erecv
    )
    collect.close()
    spread.close()


def third_kernel(count, parts, acc, wsum, noisy, cube, out, *scratch):
    settle(Place(count, parts), acc, wsum, noisy, cube, out, *scratch).close()


def add_kernel(count, some, lists, lists_v, weights, back, acc, wsum, members, *sums):
    parts, group = lists.shape[:2]
    place = Place(count, parts)
    blocks, held = acc.shape[:2]

    def clear(i, carry):
        rows = pl.ds(pl.multiple_of(i * LANES, LANES), LANES)
        for each in sums:
            each[rows, :] = jnp.zeros((LANES, LANES), jnp.float32)
        return carry

    lax.fori_loop(0, blocks * held // LANES, clear, 0)
    for src in range(parts):
        row = jnp.broadcast_to(weights[src : src + 1, :], (some, LANES))
        column = jnp.sum(jnp.where(diagonal(some), row, 0.0), axis=1, keepdims=True)
        spread = jnp.broadcast_to(column, (some, LANES))
        rows = pl.ds(src * some, some)

        def scale(m, carry):
            members[m, rows, :] = back[m, rows, :].astype(jnp.float32) * spread
            return carry

        lax.fori_loop(0, group, scale, 0)

    many = wsum.shape[0] * (held // LANES)
    lane = lax.broadcasted_iota(jnp.int32, (1, LANES), 1)
    heavy = [jnp.where(lane < some, weights[src : src + 1, :], 0.0) for src in range(parts)]
    tall = lax.broadcasted_iota(jnp.int32, (many, LANES), 0)
    low = lax.broadcasted_iota(jnp.int32, (LANES, LANES), 0)
    first = place.part * (many * LANES)

    def weigh(m, total):
        ones, loads = [], []
        for src in range(parts):
            spots = lists_v[src, pl.ds(m, 1), :] - first
            loads.append(jnp.where((spots >> 7) == tall, heavy[src], 0.0).astype(jnp.bfloat16))
            ones.append(jnp.where((spots & (LANES - 1)) == low, 1.0, 0.0).astype(jnp.bfloat16))
        return total + lax.dot_general(
            jnp.concatenate(loads, axis=1),
            jnp.concatenate(ones, axis=1),
            (((1,), (1,)), ((), ())),
            preferred_element_type=jnp.float32,
        )

    total = lax.fori_loop(0, group, weigh, jnp.zeros((many, LANES), jnp.float32))
    per = held // LANES
    for b in range(wsum.shape[0]):
        wsum[b, :per, :] = total[b * per : (b + 1) * per, :]
        if per < SUBS:
            wsum[b, per:, :] = jnp.zeros((SUBS - per, LANES), jnp.float32)

    for src in range(parts):

        def step(q, carry):
            for base in range(0, group, STREAMS * TOGETHER):
                spots, news = [], []
                for s in range(STREAMS):
                    ms = [base + s * TOGETHER + t for t in range(TOGETHER)]
                    where = [lists[src, m, q] for m in ms]
                    extra = [members[m, pl.ds(src * some + q, 1), :] for m in ms]
                    fresh = [sums[s][pl.ds(w, 1), :] + e for w, e in zip(where, extra)]
                    for t in range(TOGETHER):
                        for u in range(t):
                            fresh[t] = fresh[t] + jnp.where(where[u] == where[t], extra[u], 0.0)
                    spots.append(where)
                    news.append(fresh)
                for s in range(STREAMS):
                    for w, n in zip(spots[s], news[s]):
                        sums[s][pl.ds(w, 1), :] = n
            return carry

        lax.fori_loop(0, some, step, 0, unroll=2)

    def store(b, carry):
        for i in range(held // LANES):
            rows = pl.ds(pl.multiple_of(b * held + i * LANES, LANES), LANES)
            whole = sums[0][rows, :]
            for each in sums[1:]:
                whole = whole + each[rows, :]
            acc[b, i * LANES : (i + 1) * LANES, :] = whole.astype(acc.dtype)
        return carry

    lax.fori_loop(0, blocks, store, 0)


def shape(*dims, dtype=jnp.float32):
    return jax.ShapeDtypeStruct(dims, dtype)


def params(collective_id=None):
    return pltpu.CompilerParams(
        collective_id=collective_id, has_side_effects=collective_id is not None, vmem_limit_bytes=LIMIT
    )


def add_up(count, some, held, lists, weights, back):
    parts, group = lists.shape[:2]
    ranks = count // parts
    return pl.pallas_call(
        functools.partial(add_kernel, count, some),
        out_shape=[shape(count, held, LANES, dtype=back.dtype), shape(ranks, SUBS, LANES)],
        in_specs=[SMEM, VMEM, VMEM, VMEM],
        out_specs=[VMEM, VMEM],
        scratch_shapes=[pltpu.VMEM((group, parts * some, LANES), jnp.float32)]
        + [pltpu.VMEM((count * held, LANES), jnp.float32)] * STREAMS,
        compiler_params=params(),
        name="add_up",
    )(lists, lists, weights, back)


def body(noisy, matches, cube_home, sigma_coef):
    count = lax.axis_size("space")
    some, group = matches.shape
    held, width = noisy.shape
    parts = width // LANES
    refs = parts * some
    cube, cube_t = cube_tables()
    sigma = sigma_coef[None, :]
    dtype = noisy.dtype
    shared = spread_scratch(count, parts, held, dtype) + shrink_scratch(parts, group, refs)
    coeffs, back, weights, lists = pl.pallas_call(
        functools.partial(first_kernel, count),
        out_shape=[
            shape(group, refs, LANES),
            shape(group, refs, LANES, dtype=dtype),
            shape(SUBS, LANES),
            shape(parts, group, LANES, dtype=jnp.int32),
        ],
        in_specs=[VMEM, SMEM, SMEM, VMEM, VMEM],
        out_specs=[VMEM] * 4,
        scratch_shapes=shared
        + [
            pltpu.SMEM((group, LANES), jnp.int32),
            pltpu.VMEM((parts, group, LANES), jnp.int32),
            pltpu.SMEM((parts, group, LANES), jnp.int32),
            SEMS((parts,)),
            SEMS((parts,)),
            SEMS((parts,)),
        ],
        compiler_params=params(0),
        name="shrink",
    )(noisy, cube_home, matches.T, sigma, cube_t)
    acc, wsum = add_up(count, some, held, lists, weights, back)
    basic, back, weights = pl.pallas_call(
        functools.partial(second_kernel, count, some),
        out_shape=[
            shape(held, width, dtype=dtype),
            shape(group, refs, LANES, dtype=dtype),
            shape(SUBS, LANES),
        ],
        in_specs=[HBM] + [VMEM] * 5 + [SMEM, HBM],
        out_specs=[VMEM] * 3,
        scratch_shapes=shared
        + [pltpu.VMEM((group, refs, LANES), jnp.float32), SEMS((1,))]
        + settle_scratch(count, parts, held, dtype),
        compiler_params=params(1),
        name="wiener",
    )(acc, wsum, noisy, cube, cube_t, sigma, lists, coeffs)
    acc, wsum = add_up(count, some, held, lists, weights, back)
    final = pl.pallas_call(
        functools.partial(third_kernel, count, parts),
        out_shape=shape(held, width, dtype=dtype),
        in_specs=[HBM] + [VMEM] * 3,
        out_specs=VMEM,
        scratch_shapes=settle_scratch(count, parts, held, dtype),
        compiler_params=params(2),
        name="settle",
    )(acc, wsum, noisy, cube)
    return basic, final


def solution(mesh):
    in_specs = (P(("groups", "space"), None), P(("groups", "space"), None), P("groups"), P())
    out_specs = (P(("groups", "space"), None), P(("groups", "space"), None))
    return jax.shard_map(body, mesh=mesh, in_specs=in_specs, out_specs=out_specs, check_vma=False)
```

```python
import functools
import itertools

import jax
import jax.numpy as jnp
import numpy as np
from jax import lax
from jax.experimental import pallas as pl
from jax.experimental.pallas import tpu as pltpu
from jax.sharding import PartitionSpec as P

shrink_level = 2.7
prior_weight = 0.5
LANES = 128
SUBS = 8
PIECES = 2
STREAMS = 4
LIMIT = 60 * 1024 * 1024
MESH = pl.DeviceIdType.MESH
VMEM = pl.BlockSpec(memory_space=pltpu.VMEM)
SMEM = pl.BlockSpec(memory_space=pltpu.SMEM)
HBM = pl.BlockSpec(memory_space=pltpu.HBM)
SEMS = pltpu.SemaphoreType.DMA


def dct_matrix(length):
    index = np.arange(length, dtype=np.float64)
    table = np.cos(np.pi * (2.0 * index[None, :] + 1.0) * index[:, None] / (2.0 * length))
    table = table * np.sqrt(2.0 / length)
    table[0] /= np.sqrt(2.0)
    return table


def cube_tables():
    small = dct_matrix(8)
    cube = np.kron(np.kron(small, small), small).astype(np.float32)
    return cube.astype(jnp.bfloat16), cube.T.astype(jnp.bfloat16)


def half_cosines(n):
    return [float(2.0 * np.cos(np.pi * (2 * i + 1) / (2 * n))) for i in range(n // 2)]


def cosine_sums(x):
    n = len(x)
    if n == 2:
        return [x[0] + x[1], (x[0] - x[1]) * float(np.cos(np.pi / 4))]
    half = n // 2
    even = cosine_sums([x[i] + x[n - 1 - i] for i in range(half)])
    turned = cosine_sums([(x[i] - x[n - 1 - i]) * f for i, f in enumerate(half_cosines(n))])
    out = [None] * n
    for k in range(half):
        out[2 * k] = even[k]
        out[2 * k + 1] = turned[k] - out[2 * k - 1] if k else 0.5 * turned[0]
    return out


def cosine_sums_transposed(y):
    n = len(y)
    if n == 2:
        odd = y[1] * float(np.cos(np.pi / 4))
        return [y[0] + odd, y[0] - odd]
    half = n // 2
    even = cosine_sums_transposed(y[0::2])
    tail = [None] * half
    for k in reversed(range(half)):
        tail[k] = y[2 * k + 1] - tail[k + 1] if k + 1 < half else y[2 * k + 1]
    tail[0] = 0.5 * tail[0]
    odd = [o * f for o, f in zip(cosine_sums_transposed(tail), half_cosines(n))]
    return [even[i] + odd[i] for i in range(half)] + [even[i] - odd[i] for i in reversed(range(half))]


def scales(n):
    return [float(np.sqrt((1.0 if k == 0 else 2.0) / n)) for k in range(n)]


def flip(value, mask):
    if isinstance(mask, int):
        for bit in (1 << b for b in range(mask.bit_length())):
            if mask & bit:
                value = value + bit - 2 * bit * lax.rem(value // bit, 2)
        return value
    for bit in (1, 2):
        value = value + bit * lax.rem(mask // bit, 2) * (1 - 2 * lax.rem(value // bit, 2))
    return value


def lowest(d, count):
    return d & -d if d else count


class Place:
    def __init__(self, count, parts):
        self.parts, self.ranks = parts, count // parts
        me = lax.axis_index("space")
        self.part, self.rank = me // self.ranks, lax.rem(me, self.ranks)
        self.bits = [1 << b for b in range(self.ranks.bit_length() - 1)]

    def index(self, off, d):
        return flip(self.part, off) * self.ranks + flip(self.rank, d)

    def device(self, off, d):
        return {"space": self.index(off, d)}

    def greet(self):
        barrier = pltpu.get_barrier_semaphore()
        peers = [(off, 0) for off in range(1, self.parts)] + [(0, d) for d in range(1, self.ranks)]
        for off, d in peers:
            pl.semaphore_signal(barrier, inc=1, device_id=self.device(off, d), device_id_type=MESH)
        pl.semaphore_wait(barrier, len(peers))


def remote(src, dst, send, recv, device):
    return pltpu.make_async_remote_copy(
        src_ref=src, dst_ref=dst, send_sem=send, recv_sem=recv, device_id=device, device_id_type=MESH
    )


def piece_of(ref, h):
    size = ref.shape[0] // PIECES
    return ref.at[pl.ds(h * size, size), :]


class Spread:
    def __init__(self, place, stage, got, table, send, recv):
        self.place, self.stage, self.got, self.table = place, stage, got, table
        self.send, self.recv, self.started = send, recv, []

    def block(self, off, d):
        return self.stage.at[0] if off == 0 and d == 0 else self.got.at[off, d]

    def pass_on(self, off, d, h):
        place = self.place
        for bit in reversed(place.bits):
            if bit < lowest(d, place.ranks):
                copy = remote(
                    piece_of(self.block(off, d), h),
                    piece_of(self.got.at[off, d | bit], h),
                    self.send.at[off, d | bit, h],
                    self.recv.at[off, d | bit, h],
                    place.device(0, bit),
                )
                copy.start()
                self.started.append(copy)

    def begin(self, h, rows, cube_t):
        place = self.place
        for off in list(range(1, place.parts)) + [0]:
            columns = pl.ds(pl.multiple_of(flip(place.part, off) * LANES, LANES), LANES)
            spec = jnp.dot(rows, cube_t[:, columns], preferred_element_type=jnp.float32)
            piece = piece_of(self.stage.at[off], h)
            piece[...] = spec.astype(self.stage.dtype)
            if off == 0:
                self.pass_on(0, 0, h)
                continue
            copy = remote(
                piece,
                piece_of(self.got.at[off, 0], h),
                self.send.at[off, 0, h],
                self.recv.at[off, 0, h],
                place.device(off, 0),
            )
            copy.start()
            self.started.append(copy)

    def widen(self, off, d, h):
        source = piece_of(self.block(off, d), h)
        held = self.stage.shape[1]
        size = held // PIECES
        first = self.place.index(off, d) * held + h * size
        rows = pl.ds(pl.multiple_of(first, size), size)
        self.table[rows, :] = source[...].astype(jnp.float32)

    def finish(self):
        place = self.place

        def when(key):
            off, d, h = key
            return off + place.parts * h + sum(0.3 if b == 1 else 1.0 for b in place.bits if d & b)

        keys = [
            (off, d, h)
            for off in range(place.parts)
            for d in range(place.ranks)
            for h in range(PIECES)
            if off or d
        ]
        for h in range(PIECES):
            self.widen(0, 0, h)
        for off, d, h in sorted(keys, key=when):
            piece = piece_of(self.got.at[off, d], h)
            remote(
                piece, piece, self.send.at[off, d, h], self.recv.at[off, d, h], place.device(off, d)
            ).wait_recv()
            self.pass_on(off, d, h)
            self.widen(off, d, h)

    def close(self):
        for copy in self.started:
            copy.wait_send()


def spread_scratch(count, parts, held, dtype):
    ranks = count // parts
    return [
        pltpu.VMEM((parts, held, LANES), dtype),
        pltpu.VMEM((parts, ranks, held, LANES), dtype),
        pltpu.VMEM((count * held, LANES), jnp.float32),
        SEMS((parts, ranks, PIECES)),
        SEMS((parts, ranks, PIECES)),
    ]


def pick_rows(table, lists, first, members, some):
    group = members.shape[0]
    each = LANES // group

    def step(t, carry):
        src, row = t // (some // each), lax.rem(t, some // each)
        for q in range(each):
            for m in range(group):
                spot = lists[src, first + row, q * group + m]
                members[m, pl.ds(t * each + q, 1), :] = table[pl.ds(spot, 1), :]
        return carry

    lax.fori_loop(0, lists.shape[0] * some // each, step, 0)


def find_equals(lists, same, group, some):
    for src in range(lists.shape[0]):
        rows = lists[src, :group, :]
        equal = [jnp.where(rows == pltpu.roll(rows, back, 0), 1.0, 0.0) for back in range(1, group // STREAMS)]
        equal.append(jnp.zeros((LANES - group * len(equal), LANES), jnp.float32))
        same[src * some : (src + 1) * some, :] = jnp.concatenate(equal, axis=0).T[:some, :]


def diagonal(rows):
    shape = (rows, LANES)
    return lax.broadcasted_iota(jnp.int32, shape, 0) == lax.broadcasted_iota(jnp.int32, shape, 1)


def shrink_groups(place, second, width, some, sigma, members, coeffs, back, same, energy, ebuf, egot, weights, send, recv, then=None):
    group, refs = members.shape[:2]
    factor = scales(group)
    columns = pl.ds(pl.multiple_of(place.part * LANES, LANES), LANES)
    own = sigma[:, columns]
    level = own * own if second else (shrink_level * own) * (shrink_level * own)

    def forward(b, carry):
        rows = pl.ds(pl.multiple_of(b * SUBS, SUBS), SUBS)
        values = cosine_sums([members[m, rows, :] for m in range(group)])
        total = None
        for j in range(group):
            value = values[j] * factor[j]
            square = value * value
            gain = square / (square + level)
            power = gain * gain
            total = power if total is None else total + power
            if second:
                members[j, rows, :] = gain * coeffs[j, rows, :]
            else:
                coeffs[j, rows, :] = value
                members[j, rows, :] = gain * value
        energy[rows, :] = total * level if second else total
        return carry

    lax.fori_loop(0, refs // SUBS, forward, 0)
    if then is not None:
        then()
    parts = refs // some
    for src in range(parts):
        column = jnp.sum(energy[src * some : (src + 1) * some, :], axis=1, keepdims=True)
        ebuf[src : src + 1, :] = jnp.sum(jnp.where(diagonal(some), column, 0.0), axis=0, keepdims=True)
    started = []
    for off in range(1, place.parts):
        copy = remote(ebuf, egot.at[off], send.at[off], recv.at[off], place.device(off, 0))
        copy.start()
        started.append(copy)

    def inverse(b, carry):
        rows = pl.ds(pl.multiple_of(b * 2 * SUBS, 2 * SUBS), 2 * SUBS)
        values = cosine_sums_transposed([members[j, rows, :] * factor[j] for j in range(group)])
        for m in range(group):
            merged = values[m]
            for before in range(1, m % (group // STREAMS) + 1):
                lane = (before - 1) * group + m
                merged = merged + same[rows, lane : lane + 1] * values[m - before]
            back[m, rows, :] = merged.astype(back.dtype)
        return carry

    lax.fori_loop(0, refs // (2 * SUBS), inverse, 0)
    total = ebuf[...]
    for off in range(1, place.parts):
        remote(ebuf, egot.at[off], send.at[off], recv.at[off], place.device(off, 0)).wait_recv()
        total = total + egot[off]
    weights[...] = 1.0 / (0.25 + total / (group * width))
    for copy in started:
        copy.wait_send()


def shrink_scratch(parts, group, refs):
    assert parts <= SUBS
    return [
        pltpu.VMEM((group, refs, LANES), jnp.float32),
        pltpu.VMEM((refs, LANES), jnp.float32),
        pltpu.VMEM((refs, LANES), jnp.float32),
        pltpu.VMEM((SUBS, LANES), jnp.float32),
        pltpu.VMEM((parts, SUBS, LANES), jnp.float32),
        SEMS((parts,)),
        SEMS((parts,)),
    ]


def first_kernel(count, x, home, ids, sigma, cube_t, coeffs_out, back, weights, lists_out, *scratch):
    stage, got, table, send, recv = scratch[:5]
    members, same, energy, ebuf, egot, esend, erecv = scratch[5:12]
    coeffs, csem, named, lists_v, lists_s, lsend, lrecv, lsem = scratch[12:]
    parts = stage.shape[0]
    group, some = ids.shape
    each = LANES // group
    size = x.shape[0] // PIECES
    place = Place(count, parts)
    place.greet()
    spread = Spread(place, stage, got, table, send, recv)
    spread.begin(0, x[:size, :], cube_t)

    def look_up(row, carry):
        for q in range(each):
            for m in range(group):
                spot = home[ids[m, row * each + q]]
                named[m, row * each + q] = spot
                named[group + row, q * group + m] = spot
        return carry

    lax.fori_loop(0, some // each, look_up, 0)

    def fill(m, carry):
        for q in range(some, LANES):
            named[m, q] = 0
        return carry

    lax.fori_loop(0, group, fill, 0)

    def fill_rows(row, carry):
        for q in range(LANES):
            named[row, q] = 0
        return carry

    lax.fori_loop(group + some // each, named.shape[0], fill_rows, 0)
    ebuf[...] = jnp.zeros(ebuf.shape, ebuf.dtype)
    mine = pltpu.make_async_copy(named, lists_v.at[place.part], lsem.at[0])
    mine.start()
    mine.wait()
    started = []
    for off in range(1, parts):
        copy = remote(
            lists_v.at[place.part],
            lists_v.at[place.part],
            lsend.at[off],
            lrecv.at[off],
            place.device(off, 0),
        )
        copy.start()
        started.append(copy)
    for h in range(1, PIECES):
        spread.begin(h, x[h * size : (h + 1) * size, :], cube_t)
    spread.finish()
    copies = []
    for off in range(parts):
        source = lists_v.at[flip(place.part, off)]
        if off:
            remote(source, source, lsend.at[off], lrecv.at[off], place.device(off, 0)).wait_recv()
        copy = pltpu.make_async_copy(source, lists_s.at[flip(place.part, off)], lsem.at[off])
        copy.start()
        copies.append(copy)
    lists_out[...] = lists_v[...]
    find_equals(lists_v, same, group, some)
    for copy in copies:
        copy.wait()
    pick_rows(table, lists_s, group, members, some)
    store = pltpu.make_async_copy(coeffs, coeffs_out, csem.at[0])
    shrink_groups(
        place, False, x.shape[1], some, sigma, members, coeffs, back, same, energy, ebuf, egot, weights, esend, erecv, store.start
    )
    store.wait()
    for copy in started:
        copy.wait_send()
    spread.close()


class Collect:
    def __init__(self, place, acc, own, got, sent, zgot, local, send, recv):
        self.place, self.acc, self.own, self.got, self.sent, self.zgot = place, acc, own, got, sent, zgot
        self.local, self.send, self.recv, self.started = local, send, recv, []
        last = place.parts - 1
        inner = jnp.where((place.part == 0) | (place.part == last), 0, 1)
        self.order = [inner * (i + 1) + (1 - inner) * (last - i) for i in range(last)] + [0]

    def start(self, copy):
        copy.start()
        self.started.append(copy)

    def fetch(self, off, d):
        return pltpu.make_async_copy(
            self.acc.at[self.place.index(off, d)], self.own.at[off, d // 2], self.local.at[off, d // 2]
        )

    def open(self):
        place = self.place
        for d in sorted(range(0, place.ranks, 2), key=lambda d: lowest(d, place.ranks)):
            for off in self.order:
                self.fetch(off, d).start()

    def begin(self):
        place = self.place
        for h in range(PIECES):
            for d in sorted(range(1, place.ranks, 2), key=lambda d: lowest(d - 1, place.ranks)):
                for off in self.order:
                    self.start(
                        remote(
                            piece_of(self.acc.at[place.index(off, d)], h),
                            piece_of(self.got.at[off, d], h),
                            self.send.at[off, d, h],
                            self.recv.at[off, d, h],
                            place.device(0, 1),
                        )
                    )

    def value(self, off, d, h):
        place = self.place
        if h == 0:
            self.fetch(off, d).wait()
        total = piece_of(self.own.at[off, d // 2], h)[...].astype(jnp.float32)
        for bit in place.bits:
            if bit < lowest(d, place.ranks):
                piece = piece_of(self.got.at[off, d | bit], h)
                remote(
                    piece, piece, self.send.at[off, d | bit, h], self.recv.at[off, d | bit, h], place.device(0, bit)
                ).wait_recv()
                total = total + piece[...].astype(jnp.float32)
        return total

    def run(self):
        place = self.place
        for level in place.bits[1:] + [place.ranks]:
            ds = [d for d in range(0, place.ranks, 2) if lowest(d, place.ranks) == level]
            for h, d, i in itertools.product(range(PIECES), ds, range(place.parts)):
                    off = self.order[i]
                    piece = piece_of(self.sent.at[off, d // 2], h)
                    piece[...] = self.value(off, d, h).astype(self.sent.dtype)
                    if d == 0 and i == place.parts - 1:
                        continue
                    bit = lowest(d, 0)
                    self.start(
                        remote(
                            piece,
                            piece_of(self.got.at[off, d] if d else self.zgot.at[off], h),
                            self.send.at[off, d, h],
                            self.recv.at[off, d, h],
                            place.device(0, bit) if d else place.device(off, 0),
                        )
                    )

    def slices(self, h):
        place = self.place
        yield 0, piece_of(self.sent.at[0, 0], h)[...]
        for off in range(1, place.parts):
            piece = piece_of(self.zgot.at[off], h)
            remote(
                piece, piece, self.send.at[off, 0, h], self.recv.at[off, 0, h], place.device(off, 0)
            ).wait_recv()
            yield off, piece[...]

    def close(self):
        for copy in self.started:
            copy.wait_send()


def settle(place, acc, wsum, noisy, cube, out, own, got, sent, zgot, wgot, local, send, recv, wsend, wrecv, then=None):
    held = noisy.shape[0]
    collect = Collect(place, acc, own, got, sent, zgot, local, send, recv)
    collect.open()
    place.greet()
    collect.begin()
    for d in range(1, place.ranks):
        collect.start(
            remote(wsum.at[flip(place.rank, d)], wgot.at[d], wsend.at[d], wrecv.at[d], place.device(0, d))
        )
    collect.run()
    denom = wsum[place.rank]
    for d in range(1, place.ranks):
        remote(wgot.at[d], wgot.at[d], wsend.at[d], wrecv.at[d], place.device(0, d)).wait_recv()
        denom = denom + wgot[d]
    size = held // PIECES
    for h in range(PIECES):
        numer = prior_weight * noisy[pl.ds(h * size, size), :].astype(jnp.float32)
        for off, part in collect.slices(h):
            rows = pl.ds(pl.multiple_of(flip(place.part, off) * LANES, LANES), LANES)
            numer = numer + jnp.dot(part, cube[rows, :], preferred_element_type=jnp.float32)
        for j in range(size // LANES):
            row = h * (size // LANES) + j
            spread = jnp.broadcast_to(denom[row : row + 1, :], (LANES, LANES))
            column = jnp.sum(jnp.where(diagonal(LANES), spread, 0.0), axis=1, keepdims=True)
            out[pl.ds(row * LANES, LANES), :] = (
                numer[j * LANES : (j + 1) * LANES, :] / (column + prior_weight)
            ).astype(out.dtype)
        if then is not None:
            then(h)
    return collect


def settle_scratch(count, parts, held, dtype):
    ranks = count // parts
    half = (parts, ranks // 2, held, LANES)
    return [
        pltpu.VMEM(half, dtype),
        pltpu.VMEM((parts, ranks, held, LANES), dtype),
        pltpu.VMEM(half, dtype),
        pltpu.VMEM((parts, held, LANES), dtype),
        pltpu.VMEM((ranks, SUBS, LANES), jnp.float32),
        SEMS((parts, ranks // 2)),
        SEMS((parts, ranks, PIECES)),
        SEMS((parts, ranks, PIECES)),
        SEMS((ranks,)),
        SEMS((ranks,)),
    ]


def second_kernel(count, some, acc, wsum, noisy, cube, cube_t, sigma, lists, lists_v, coeffs_in, basic, back, weights, *scratch):
    stage, got, table, send, recv = scratch[:5]
    members, same, energy, ebuf, egot, esend, erecv = scratch[5:12]
    coeffs, csem = scratch[12:14]
    group = members.shape[0]
    size = noisy.shape[0] // PIECES
    parts = stage.shape[0]
    place = Place(count, parts)
    fetch = pltpu.make_async_copy(coeffs_in, coeffs, csem.at[0])
    fetch.start()
    spread = Spread(place, stage, got, table, send, recv)
    ebuf[...] = jnp.zeros(ebuf.shape, ebuf.dtype)
    find_equals(lists_v, same, group, some)
    collect = settle(
        place,
        acc,
        wsum,
        noisy,
        cube,
        basic,
        *scratch[14:],
        then=lambda h: spread.begin(h, basic[h * size : (h + 1) * size, :], cube_t),
    )
    spread.finish()
    pick_rows(table, lists, group, members, some)
    fetch.wait()
    shrink_groups(
        place, True, noisy.shape[1], some, sigma, members, coeffs, back, same, energy, ebuf, egot, weights, esend, erecv
    )
    collect.close()
    spread.close()


def third_kernel(count, parts, acc, wsum, noisy, cube, out, *scratch):
    settle(Place(count, parts), acc, wsum, noisy, cube, out, *scratch).close()


def add_kernel(count, some, lists, lists_v, weights, back, acc, wsum, members, *sums):
    parts, group = lists.shape[0], members.shape[0]
    each = LANES // group
    place = Place(count, parts)
    blocks, held = acc.shape[:2]

    def clear(i, carry):
        rows = pl.ds(pl.multiple_of(i * LANES, LANES), LANES)
        for each in sums:
            each[rows, :] = jnp.zeros((LANES, LANES), jnp.float32)
        return carry

    lax.fori_loop(0, blocks * held // LANES, clear, 0)
    for src in range(parts):
        row = jnp.broadcast_to(weights[src : src + 1, :], (some, LANES))
        column = jnp.sum(jnp.where(diagonal(some), row, 0.0), axis=1, keepdims=True)
        spread = jnp.broadcast_to(column, (some, LANES))
        rows = pl.ds(src * some, some)

        def scale(m, carry):
            members[m, rows, :] = back[m, rows, :].astype(jnp.float32) * spread
            return carry

        lax.fori_loop(0, group, scale, 0)

    many = wsum.shape[0] * (held // LANES)
    lane = lax.broadcasted_iota(jnp.int32, (1, LANES), 1)
    heavy = [jnp.where(lane < some, weights[src : src + 1, :], 0.0) for src in range(parts)]
    tall = lax.broadcasted_iota(jnp.int32, (many, LANES), 0)
    low = lax.broadcasted_iota(jnp.int32, (LANES, LANES), 0)
    first = place.part * (many * LANES)

    def weigh(m, total):
        ones, loads = [], []
        for src in range(parts):
            spots = lists_v[src, pl.ds(m, 1), :] - first
            loads.append(jnp.where((spots >> 7) == tall, heavy[src], 0.0).astype(jnp.bfloat16))
            ones.append(jnp.where((spots & (LANES - 1)) == low, 1.0, 0.0).astype(jnp.bfloat16))
        return total + lax.dot_general(
            jnp.concatenate(loads, axis=1),
            jnp.concatenate(ones, axis=1),
            (((1,), (1,)), ((), ())),
            preferred_element_type=jnp.float32,
        )

    total = lax.fori_loop(0, group, weigh, jnp.zeros((many, LANES), jnp.float32), unroll=True)
    per = held // LANES
    for b in range(wsum.shape[0]):
        wsum[b, :per, :] = total[b * per : (b + 1) * per, :]
        if per < SUBS:
            wsum[b, per:, :] = jnp.zeros((SUBS - per, LANES), jnp.float32)

    together = group // STREAMS

    def step(t, carry):
        src, row = t // (some // each), lax.rem(t, some // each)
        for q in range(each):
            spots, news = [], []
            for m in range(group):
                spot = lists[src, group + row, q * group + m]
                spots.append(spot)
                news.append(sums[m // together][pl.ds(spot, 1), :] + members[m, pl.ds(t * each + q, 1), :])
            for m in range(group):
                sums[m // together][pl.ds(spots[m], 1), :] = news[m]
        return carry

    lax.fori_loop(0, parts * some // each, step, 0)

    def store(b, carry):
        for i in range(held // LANES):
            rows = pl.ds(pl.multiple_of(b * held + i * LANES, LANES), LANES)
            whole = sums[0][rows, :]
            for each in sums[1:]:
                whole = whole + each[rows, :]
            acc[b, i * LANES : (i + 1) * LANES, :] = whole.astype(acc.dtype)
        return carry

    lax.fori_loop(0, blocks, store, 0)


def shape(*dims, dtype=jnp.float32):
    return jax.ShapeDtypeStruct(dims, dtype)


def params(collective_id=None):
    return pltpu.CompilerParams(
        collective_id=collective_id, has_side_effects=collective_id is not None, vmem_limit_bytes=LIMIT
    )


def add_up(count, some, held, lists, weights, back):
    parts, group = lists.shape[0], back.shape[0]
    ranks = count // parts
    return pl.pallas_call(
        functools.partial(add_kernel, count, some),
        out_shape=[shape(count, held, LANES, dtype=back.dtype), shape(ranks, SUBS, LANES)],
        in_specs=[SMEM, VMEM, VMEM, VMEM],
        out_specs=[VMEM, VMEM],
        scratch_shapes=[pltpu.VMEM((group, parts * some, LANES), jnp.float32)]
        + [pltpu.VMEM((count * held, LANES), jnp.float32)] * STREAMS,
        compiler_params=params(),
        name="add_up",
    )(lists, lists, weights, back)


def body(noisy, matches, cube_home, sigma_coef):
    count = lax.axis_size("space")
    some, group = matches.shape
    held, width = noisy.shape
    parts = width // LANES
    refs = parts * some
    cube, cube_t = cube_tables()
    sigma = sigma_coef[None, :]
    dtype = noisy.dtype
    shared = spread_scratch(count, parts, held, dtype) + shrink_scratch(parts, group, refs)
    coeffs, back, weights, lists = pl.pallas_call(
        functools.partial(first_kernel, count),
        out_shape=[
            shape(group, refs, LANES),
            shape(group, refs, LANES, dtype=dtype),
            shape(SUBS, LANES),
            shape(parts, 2 * group, LANES, dtype=jnp.int32),
        ],
        in_specs=[VMEM, SMEM, SMEM, VMEM, VMEM],
        out_specs=[HBM] + [VMEM] * 3,
        scratch_shapes=shared
        + [
            pltpu.VMEM((group, refs, LANES), jnp.float32),
            SEMS((1,)),
            pltpu.SMEM((2 * group, LANES), jnp.int32),
            pltpu.VMEM((parts, 2 * group, LANES), jnp.int32),
            pltpu.SMEM((parts, 2 * group, LANES), jnp.int32),
            SEMS((parts,)),
            SEMS((parts,)),
            SEMS((parts,)),
        ],
        compiler_params=params(0),
        name="shrink",
    )(noisy, cube_home, matches.T, sigma, cube_t)
    acc, wsum = add_up(count, some, held, lists, weights, back)
    basic, back, weights = pl.pallas_call(
        functools.partial(second_kernel, count, some),
        out_shape=[
            shape(held, width, dtype=dtype),
            shape(group, refs, LANES, dtype=dtype),
            shape(SUBS, LANES),
        ],
        in_specs=[HBM] + [VMEM] * 5 + [SMEM, VMEM, HBM],
        out_specs=[VMEM] * 3,
        scratch_shapes=shared
        + [pltpu.VMEM((group, refs, LANES), jnp.float32), SEMS((1,))]
        + settle_scratch(count, parts, held, dtype),
        compiler_params=params(1),
        name="wiener",
    )(acc, wsum, noisy, cube, cube_t, sigma, lists, lists, coeffs)
    acc, wsum = add_up(count, some, held, lists, weights, back)
    final = pl.pallas_call(
        functools.partial(third_kernel, count, parts),
        out_shape=shape(held, width, dtype=dtype),
        in_specs=[HBM] + [VMEM] * 3,
        out_specs=VMEM,
        scratch_shapes=settle_scratch(count, parts, held, dtype),
        compiler_params=params(2),
        name="settle",
    )(acc, wsum, noisy, cube)
    return basic, final


def solution(mesh):
    in_specs = (P(("groups", "space"), None), P(("groups", "space"), None), P("groups"), P())
    out_specs = (P(("groups", "space"), None), P(("groups", "space"), None))
    return jax.shard_map(body, mesh=mesh, in_specs=in_specs, out_specs=out_specs, check_vma=False)
```

```python
import functools
import itertools

import jax
import jax.numpy as jnp
import numpy as np
from jax import lax
from jax.experimental import pallas as pl
from jax.experimental.pallas import tpu as pltpu
from jax.sharding import PartitionSpec as P

shrink_level = 2.7
prior_weight = 0.5
LANES = 128
SUBS = 8
PIECES = 2
STREAMS = 4
MESH = pl.DeviceIdType.MESH
VMEM = pl.BlockSpec(memory_space=pltpu.VMEM)
SMEM = pl.BlockSpec(memory_space=pltpu.SMEM)
HBM = pl.BlockSpec(memory_space=pltpu.HBM)
SEMS = pltpu.SemaphoreType.DMA


def dct_matrix(length):
    index = np.arange(length, dtype=np.float64)
    table = np.cos(np.pi * (2.0 * index[None, :] + 1.0) * index[:, None] / (2.0 * length))
    table = table * np.sqrt(2.0 / length)
    table[0] /= np.sqrt(2.0)
    return table


def cube_tables():
    small = dct_matrix(8)
    cube = np.kron(np.kron(small, small), small).astype(np.float32)
    return cube.astype(jnp.bfloat16), cube.T.astype(jnp.bfloat16)


def half_cosines(n):
    return [float(2.0 * np.cos(np.pi * (2 * i + 1) / (2 * n))) for i in range(n // 2)]


def cosine_sums(x):
    n = len(x)
    if n == 2:
        return [x[0] + x[1], (x[0] - x[1]) * float(np.cos(np.pi / 4))]
    half = n // 2
    even = cosine_sums([x[i] + x[n - 1 - i] for i in range(half)])
    turned = cosine_sums([(x[i] - x[n - 1 - i]) * f for i, f in enumerate(half_cosines(n))])
    out = [None] * n
    for k in range(half):
        out[2 * k] = even[k]
        out[2 * k + 1] = turned[k] - out[2 * k - 1] if k else 0.5 * turned[0]
    return out


def cosine_sums_transposed(y):
    n = len(y)
    if n == 2:
        odd = y[1] * float(np.cos(np.pi / 4))
        return [y[0] + odd, y[0] - odd]
    half = n // 2
    even = cosine_sums_transposed(y[0::2])
    tail = [None] * half
    for k in reversed(range(half)):
        tail[k] = y[2 * k + 1] - tail[k + 1] if k + 1 < half else y[2 * k + 1]
    tail[0] = 0.5 * tail[0]
    odd = [o * f for o, f in zip(cosine_sums_transposed(tail), half_cosines(n))]
    return [even[i] + odd[i] for i in range(half)] + [even[i] - odd[i] for i in reversed(range(half))]


def scales(n):
    return [float(np.sqrt((1.0 if k == 0 else 2.0) / n)) for k in range(n)]


def flip(value, mask):
    if isinstance(mask, int):
        for bit in (1 << b for b in range(mask.bit_length())):
            if mask & bit:
                value = value + bit - 2 * bit * lax.rem(value // bit, 2)
        return value
    for bit in (1, 2):
        value = value + bit * lax.rem(mask // bit, 2) * (1 - 2 * lax.rem(value // bit, 2))
    return value


def lowest(d, count):
    return d & -d if d else count


class Place:
    def __init__(self, count, parts):
        self.parts, self.ranks = parts, count // parts
        me = lax.axis_index("space")
        self.part, self.rank = me // self.ranks, lax.rem(me, self.ranks)
        self.bits = [1 << b for b in range(self.ranks.bit_length() - 1)]

    def index(self, off, d):
        return flip(self.part, off) * self.ranks + flip(self.rank, d)

    def device(self, off, d):
        return {"space": self.index(off, d)}

    def greet(self):
        barrier = pltpu.get_barrier_semaphore()
        peers = [(off, 0) for off in range(1, self.parts)] + [(0, d) for d in range(1, self.ranks)]
        for off, d in peers:
            pl.semaphore_signal(barrier, inc=1, device_id=self.device(off, d), device_id_type=MESH)
        pl.semaphore_wait(barrier, len(peers))


def remote(src, dst, send, recv, device):
    return pltpu.make_async_remote_copy(
        src_ref=src, dst_ref=dst, send_sem=send, recv_sem=recv, device_id=device, device_id_type=MESH
    )


def piece_of(ref, h):
    size = ref.shape[0] // PIECES
    return ref.at[pl.ds(h * size, size), :]


class Spread:
    def __init__(self, place, stage, got, table, send, recv):
        self.place, self.stage, self.got, self.table = place, stage, got, table
        self.send, self.recv, self.started = send, recv, []

    def block(self, off, d):
        return self.stage.at[0] if off == 0 and d == 0 else self.got.at[off, d]

    def pass_on(self, off, d, h):
        place = self.place
        for bit in reversed(place.bits):
            if bit < lowest(d, place.ranks):
                copy = remote(
                    piece_of(self.block(off, d), h),
                    piece_of(self.got.at[off, d | bit], h),
                    self.send.at[off, d | bit, h],
                    self.recv.at[off, d | bit, h],
                    place.device(0, bit),
                )
                copy.start()
                self.started.append(copy)

    def begin(self, h, rows, cube_t):
        place = self.place
        for off in list(range(1, place.parts)) + [0]:
            columns = pl.ds(pl.multiple_of(flip(place.part, off) * LANES, LANES), LANES)
            spec = jnp.dot(rows, cube_t[:, columns], preferred_element_type=jnp.float32)
            piece = piece_of(self.stage.at[off], h)
            piece[...] = spec.astype(self.stage.dtype)
            if off == 0:
                self.pass_on(0, 0, h)
                continue
            copy = remote(
                piece,
                piece_of(self.got.at[off, 0], h),
                self.send.at[off, 0, h],
                self.recv.at[off, 0, h],
                place.device(off, 0),
            )
            copy.start()
            self.started.append(copy)

    def widen(self, off, d, h):
        source = piece_of(self.block(off, d), h)
        held = self.stage.shape[1]
        size = held // PIECES
        first = self.place.index(off, d) * held + h * size
        rows = pl.ds(pl.multiple_of(first, size), size)
        self.table[rows, :] = source[...].astype(jnp.float32)

    def finish(self):
        place = self.place

        def when(key):
            off, d, h = key
            return off + 0.5 * h + sum(2.2 if b == 1 else 1.6 for b in place.bits if d & b)

        keys = [
            (off, d, h)
            for off in range(place.parts)
            for d in range(place.ranks)
            for h in range(PIECES)
            if off or d
        ]
        for h in range(PIECES):
            self.widen(0, 0, h)
        for off, d, h in sorted(keys, key=when):
            piece = piece_of(self.got.at[off, d], h)
            remote(
                piece, piece, self.send.at[off, d, h], self.recv.at[off, d, h], place.device(off, d)
            ).wait_recv()
            self.pass_on(off, d, h)
            self.widen(off, d, h)

    def close(self):
        for copy in self.started:
            copy.wait_send()


def spread_scratch(count, parts, held, dtype):
    ranks = count // parts
    return [
        pltpu.VMEM((parts, held, LANES), dtype),
        pltpu.VMEM((parts, ranks, held, LANES), dtype),
        pltpu.VMEM((count * held, LANES), jnp.float32),
        SEMS((parts, ranks, PIECES)),
        SEMS((parts, ranks, PIECES)),
    ]


def pick_rows(table, lists, first, members, some):
    group = members.shape[0]
    each = LANES // group

    def step(t, carry):
        src, row = t // (some // each), lax.rem(t, some // each)
        for q in range(each):
            for m in range(group):
                spot = lists[src, first + row, q * group + m]
                members[m, pl.ds(t * each + q, 1), :] = table[pl.ds(spot, 1), :]
        return carry

    lax.fori_loop(0, lists.shape[0] * some // each, step, 0)


def find_equals(lists, same, group, some):
    for src in range(lists.shape[0]):
        rows = lists[src, :group, :]
        equal = [jnp.where(rows == pltpu.roll(rows, back, 0), 1.0, 0.0) for back in range(1, group // STREAMS)]
        equal.append(jnp.zeros((LANES - group * len(equal), LANES), jnp.float32))
        same[src * some : (src + 1) * some, :] = jnp.concatenate(equal, axis=0).T[:some, :]


def diagonal(rows):
    shape = (rows, LANES)
    return lax.broadcasted_iota(jnp.int32, shape, 0) == lax.broadcasted_iota(jnp.int32, shape, 1)


def shrink_groups(place, second, width, some, sigma, members, coeffs, back, lists_v, same, energy, ebuf, egot, weights, send, recv, then=None):
    group, refs = members.shape[:2]
    factor = scales(group)
    columns = pl.ds(pl.multiple_of(place.part * LANES, LANES), LANES)
    own = sigma[:, columns]
    level = own * own if second else (shrink_level * own) * (shrink_level * own)

    def forward(b, carry):
        rows = pl.ds(pl.multiple_of(b * SUBS, SUBS), SUBS)
        values = cosine_sums([members[m, rows, :] for m in range(group)])
        total = None
        for j in range(group):
            value = values[j] * factor[j]
            square = value * value
            gain = square / (square + level)
            power = gain * gain
            total = power if total is None else total + power
            if second:
                members[j, rows, :] = gain * coeffs[j, rows, :]
            else:
                coeffs[j, rows, :] = value
                members[j, rows, :] = gain * value
        energy[rows, :] = total * level if second else total
        return carry

    lax.fori_loop(0, refs // SUBS, forward, 0)
    if then is not None:
        then()
    parts = refs // some
    for src in range(parts):
        column = jnp.sum(energy[src * some : (src + 1) * some, :], axis=1, keepdims=True)
        ebuf[src : src + 1, :] = jnp.sum(jnp.where(diagonal(some), column, 0.0), axis=0, keepdims=True)
    started = []
    for off in range(1, place.parts):
        copy = remote(ebuf, egot.at[off], send.at[off], recv.at[off], place.device(off, 0))
        copy.start()
        started.append(copy)

    find_equals(lists_v, same, group, some)

    def inverse(b, carry):
        rows = pl.ds(pl.multiple_of(b * 2 * SUBS, 2 * SUBS), 2 * SUBS)
        values = cosine_sums_transposed([members[j, rows, :] * factor[j] for j in range(group)])
        for m in range(group):
            merged = values[m]
            for before in range(1, m % (group // STREAMS) + 1):
                lane = (before - 1) * group + m
                merged = merged + same[rows, lane : lane + 1] * values[m - before]
            back[m, rows, :] = merged.astype(back.dtype)
        return carry

    lax.fori_loop(0, refs // (2 * SUBS), inverse, 0)
    total = ebuf[...]
    for off in range(1, place.parts):
        remote(ebuf, egot.at[off], send.at[off], recv.at[off], place.device(off, 0)).wait_recv()
        total = total + egot[off]
    weights[...] = 1.0 / (0.25 + total / (group * width))
    for copy in started:
        copy.wait_send()


def shrink_scratch(parts, group, refs):
    assert parts <= SUBS
    return [
        pltpu.VMEM((group, refs, LANES), jnp.float32),
        pltpu.VMEM((refs, LANES), jnp.float32),
        pltpu.VMEM((refs, LANES), jnp.float32),
        pltpu.VMEM((SUBS, LANES), jnp.float32),
        pltpu.VMEM((parts, SUBS, LANES), jnp.float32),
        SEMS((parts,)),
        SEMS((parts,)),
    ]


def first_kernel(count, x_in, home_in, ids_in, sigma_in, cube_in, coeffs_out, back, weights, lists_out, *scratch):
    stage, got, table, send, recv = scratch[:5]
    members, same, energy, ebuf, egot, esend, erecv = scratch[5:12]
    x, cube_t, sigma, ids, insem = scratch[12:17]
    coeffs, csem, home, named, lists_v, lists_s, lsend, lrecv, lsem = scratch[17:]
    parts = stage.shape[0]
    group, some = ids.shape
    each = LANES // group
    size = x.shape[0] // PIECES
    place = Place(count, parts)
    pairs = [(x_in, x), (cube_in, cube_t), (home_in, home), (ids_in, ids), (sigma_in, sigma)]
    fetches = [pltpu.make_async_copy(src, dst, insem.at[i]) for i, (src, dst) in enumerate(pairs)]
    for fetch in fetches:
        fetch.start()
    place.greet()
    for fetch in fetches[:2]:
        fetch.wait()
    spread = Spread(place, stage, got, table, send, recv)
    for h in range(PIECES):
        spread.begin(h, x[h * size : (h + 1) * size, :], cube_t)

    def look_up(row, carry):
        for q in range(each):
            for m in range(group):
                spot = home[ids[m, row * each + q]]
                named[m, row * each + q] = spot
                named[group + row, q * group + m] = spot
        return carry

    for fetch in fetches[2:]:
        fetch.wait()
    lax.fori_loop(0, some // each, look_up, 0)

    def fill(m, carry):
        for q in range(some, LANES):
            named[m, q] = 0
        return carry

    lax.fori_loop(0, group, fill, 0)

    def fill_rows(row, carry):
        for q in range(LANES):
            named[row, q] = 0
        return carry

    lax.fori_loop(group + some // each, named.shape[0], fill_rows, 0)
    ebuf[...] = jnp.zeros(ebuf.shape, ebuf.dtype)
    mine = pltpu.make_async_copy(named, lists_v.at[place.part], lsem.at[0])
    mine.start()
    mine.wait()
    started = []
    for off in range(1, parts):
        copy = remote(
            lists_v.at[place.part],
            lists_v.at[place.part],
            lsend.at[off],
            lrecv.at[off],
            place.device(off, 0),
        )
        copy.start()
        started.append(copy)
    spread.finish()
    copies = []
    for off in range(parts):
        source = lists_v.at[flip(place.part, off)]
        if off:
            remote(source, source, lsend.at[off], lrecv.at[off], place.device(off, 0)).wait_recv()
        copy = pltpu.make_async_copy(source, lists_s.at[flip(place.part, off)], lsem.at[off])
        copy.start()
        copies.append(copy)
    lists_out[...] = lists_v[...]
    for copy in copies:
        copy.wait()
    pick_rows(table, lists_s, group, members, some)
    store = pltpu.make_async_copy(coeffs, coeffs_out, csem.at[0])
    shrink_groups(
        place, False, x.shape[1], some, sigma, members, coeffs, back, lists_v, same, energy, ebuf, egot, weights, esend, erecv, store.start
    )
    store.wait()
    for copy in started:
        copy.wait_send()
    spread.close()


class Collect:
    def __init__(self, place, acc, own, got, sent, zgot, local, send, recv):
        self.place, self.acc, self.own, self.got, self.sent, self.zgot = place, acc, own, got, sent, zgot
        self.local, self.send, self.recv, self.started = local, send, recv, []
        last = place.parts - 1
        inner = jnp.where((place.part == 0) | (place.part == last), 0, 1)
        self.order = [inner * (i + 1) + (1 - inner) * (last - i) for i in range(last)] + [0]

    def start(self, copy):
        copy.start()
        self.started.append(copy)

    def fetch(self, off, d):
        return pltpu.make_async_copy(
            self.acc.at[self.place.index(off, d)], self.own.at[off, d // 2], self.local.at[off, d // 2]
        )

    def open(self):
        place = self.place
        for d in sorted(range(0, place.ranks, 2), key=lambda d: lowest(d, place.ranks)):
            for off in self.order:
                self.fetch(off, d).start()

    def begin(self):
        place = self.place
        for h in range(PIECES):
            for d in sorted(range(1, place.ranks, 2), key=lambda d: lowest(d - 1, place.ranks)):
                for off in self.order:
                    self.start(
                        remote(
                            piece_of(self.acc.at[place.index(off, d)], h),
                            piece_of(self.got.at[off, d], h),
                            self.send.at[off, d, h],
                            self.recv.at[off, d, h],
                            place.device(0, 1),
                        )
                    )

    def value(self, off, d, h):
        place = self.place
        if h == 0:
            self.fetch(off, d).wait()
        total = piece_of(self.own.at[off, d // 2], h)[...].astype(jnp.float32)
        for bit in place.bits:
            if bit < lowest(d, place.ranks):
                piece = piece_of(self.got.at[off, d | bit], h)
                remote(
                    piece, piece, self.send.at[off, d | bit, h], self.recv.at[off, d | bit, h], place.device(0, bit)
                ).wait_recv()
                total = total + piece[...].astype(jnp.float32)
        return total

    def run(self):
        place = self.place
        for level in place.bits[1:] + [place.ranks]:
            ds = [d for d in range(0, place.ranks, 2) if lowest(d, place.ranks) == level]
            for h, d, i in itertools.product(range(PIECES), ds, range(place.parts)):
                    off = self.order[i]
                    piece = piece_of(self.sent.at[off, d // 2], h)
                    piece[...] = self.value(off, d, h).astype(self.sent.dtype)
                    if d == 0 and i == place.parts - 1:
                        continue
                    bit = lowest(d, 0)
                    self.start(
                        remote(
                            piece,
                            piece_of(self.got.at[off, d] if d else self.zgot.at[off], h),
                            self.send.at[off, d, h],
                            self.recv.at[off, d, h],
                            place.device(0, bit) if d else place.device(off, 0),
                        )
                    )

    def slices(self, h):
        place = self.place
        yield 0, piece_of(self.sent.at[0, 0], h)[...]
        for off in range(1, place.parts):
            piece = piece_of(self.zgot.at[off], h)
            remote(
                piece, piece, self.send.at[off, 0, h], self.recv.at[off, 0, h], place.device(off, 0)
            ).wait_recv()
            yield off, piece[...]

    def close(self):
        for copy in self.started:
            copy.wait_send()


def settle(place, acc, wsum, noisy, cube, out, own, got, sent, zgot, wgot, local, send, recv, wsend, wrecv, then=None):
    held = noisy.shape[0]
    collect = Collect(place, acc, own, got, sent, zgot, local, send, recv)
    collect.open()
    place.greet()
    collect.begin()
    for d in range(1, place.ranks):
        collect.start(
            remote(wsum.at[flip(place.rank, d)], wgot.at[d], wsend.at[d], wrecv.at[d], place.device(0, d))
        )
    collect.run()
    denom = wsum[place.rank]
    for d in range(1, place.ranks):
        remote(wgot.at[d], wgot.at[d], wsend.at[d], wrecv.at[d], place.device(0, d)).wait_recv()
        denom = denom + wgot[d]
    size = held // PIECES
    for h in range(PIECES):
        numer = prior_weight * noisy[pl.ds(h * size, size), :].astype(jnp.float32)
        for off, part in collect.slices(h):
            rows = pl.ds(pl.multiple_of(flip(place.part, off) * LANES, LANES), LANES)
            numer = numer + jnp.dot(part, cube[rows, :], preferred_element_type=jnp.float32)
        for j in range(size // LANES):
            row = h * (size // LANES) + j
            spread = jnp.broadcast_to(denom[row : row + 1, :], (LANES, LANES))
            column = jnp.sum(jnp.where(diagonal(LANES), spread, 0.0), axis=1, keepdims=True)
            out[pl.ds(row * LANES, LANES), :] = (
                numer[j * LANES : (j + 1) * LANES, :] / (column + prior_weight)
            ).astype(out.dtype)
        if then is not None:
            then(h)
    return collect


def settle_scratch(count, parts, held, dtype):
    ranks = count // parts
    half = (parts, ranks // 2, held, LANES)
    return [
        pltpu.VMEM(half, dtype),
        pltpu.VMEM((parts, ranks, held, LANES), dtype),
        pltpu.VMEM(half, dtype),
        pltpu.VMEM((parts, held, LANES), dtype),
        pltpu.VMEM((ranks, SUBS, LANES), jnp.float32),
        SEMS((parts, ranks // 2)),
        SEMS((parts, ranks, PIECES)),
        SEMS((parts, ranks, PIECES)),
        SEMS((ranks,)),
        SEMS((ranks,)),
    ]


def second_kernel(count, some, acc, wsum, noisy, cube, cube_t, sigma, lists, lists_v, coeffs_in, basic, back, weights, *scratch):
    stage, got, table, send, recv = scratch[:5]
    members, same, energy, ebuf, egot, esend, erecv = scratch[5:12]
    coeffs, csem = scratch[12:14]
    group = members.shape[0]
    size = noisy.shape[0] // PIECES
    parts = stage.shape[0]
    place = Place(count, parts)
    fetch = pltpu.make_async_copy(coeffs_in, coeffs, csem.at[0])
    fetch.start()
    spread = Spread(place, stage, got, table, send, recv)
    ebuf[...] = jnp.zeros(ebuf.shape, ebuf.dtype)
    collect = settle(
        place,
        acc,
        wsum,
        noisy,
        cube,
        basic,
        *scratch[14:],
        then=lambda h: spread.begin(h, basic[h * size : (h + 1) * size, :], cube_t),
    )
    spread.finish()
    pick_rows(table, lists, group, members, some)
    fetch.wait()
    shrink_groups(
        place, True, noisy.shape[1], some, sigma, members, coeffs, back, lists_v, same, energy, ebuf, egot, weights, esend, erecv
    )
    collect.close()
    spread.close()


def third_kernel(count, parts, acc, wsum, noisy, cube, out, *scratch):
    settle(Place(count, parts), acc, wsum, noisy, cube, out, *scratch).close()


def add_kernel(count, some, lists, lists_v, weights, back, acc, wsum, members, *sums):
    parts, group = lists.shape[0], members.shape[0]
    each = LANES // group
    place = Place(count, parts)
    blocks, held = acc.shape[:2]

    def clear(i, carry):
        rows = pl.ds(pl.multiple_of(i * LANES, LANES), LANES)
        for each in sums:
            each[rows, :] = jnp.zeros((LANES, LANES), jnp.float32)
        return carry

    lax.fori_loop(0, blocks * held // LANES, clear, 0)
    for src in range(parts):
        row = jnp.broadcast_to(weights[src : src + 1, :], (some, LANES))
        column = jnp.sum(jnp.where(diagonal(some), row, 0.0), axis=1, keepdims=True)
        spread = jnp.broadcast_to(column, (some, LANES))
        rows = pl.ds(src * some, some)

        def scale(m, carry):
            members[m, rows, :] = back[m, rows, :].astype(jnp.float32) * spread
            return carry

        lax.fori_loop(0, group, scale, 0)

    many = wsum.shape[0] * (held // LANES)
    lane = lax.broadcasted_iota(jnp.int32, (1, LANES), 1)
    heavy = [jnp.where(lane < some, weights[src : src + 1, :], 0.0) for src in range(parts)]
    tall = lax.broadcasted_iota(jnp.int32, (many, LANES), 0)
    low = lax.broadcasted_iota(jnp.int32, (LANES, LANES), 0)
    first = place.part * (many * LANES)

    def weigh(m, total):
        ones, loads = [], []
        for src in range(parts):
            spots = lists_v[src, pl.ds(m, 1), :] - first
            loads.append(jnp.where((spots >> 7) == tall, heavy[src], 0.0).astype(jnp.bfloat16))
            ones.append(jnp.where((spots & (LANES - 1)) == low, 1.0, 0.0).astype(jnp.bfloat16))
        return total + lax.dot_general(
            jnp.concatenate(loads, axis=1),
            jnp.concatenate(ones, axis=1),
            (((1,), (1,)), ((), ())),
            preferred_element_type=jnp.float32,
        )

    total = lax.fori_loop(0, group, weigh, jnp.zeros((many, LANES), jnp.float32), unroll=True)
    per = held // LANES
    for b in range(wsum.shape[0]):
        wsum[b, :per, :] = total[b * per : (b + 1) * per, :]
        if per < SUBS:
            wsum[b, per:, :] = jnp.zeros((SUBS - per, LANES), jnp.float32)

    together = group // STREAMS

    def step(t, carry):
        src, row = t // (some // each), lax.rem(t, some // each)
        for q in range(each):
            spots, news = [], []
            for m in range(group):
                spot = lists[src, group + row, q * group + m]
                spots.append(spot)
                news.append(sums[m // together][pl.ds(spot, 1), :] + members[m, pl.ds(t * each + q, 1), :])
            for m in range(group):
                sums[m // together][pl.ds(spots[m], 1), :] = news[m]
        return carry

    lax.fori_loop(0, parts * some // each, step, 0)

    def store(b, carry):
        for i in range(held // LANES):
            rows = pl.ds(pl.multiple_of(b * held + i * LANES, LANES), LANES)
            whole = sums[0][rows, :]
            for each in sums[1:]:
                whole = whole + each[rows, :]
            acc[b, i * LANES : (i + 1) * LANES, :] = whole.astype(acc.dtype)
        return carry

    lax.fori_loop(0, blocks, store, 0)


def shape(*dims, dtype=jnp.float32):
    return jax.ShapeDtypeStruct(dims, dtype)


def params(rows, collective_id=None):
    limit = 5 * rows * LANES * 4 + (10 << 20)
    return pltpu.CompilerParams(
        collective_id=collective_id, has_side_effects=collective_id is not None, vmem_limit_bytes=limit
    )


def add_up(count, some, held, lists, weights, back):
    parts, group = lists.shape[0], back.shape[0]
    ranks = count // parts
    return pl.pallas_call(
        functools.partial(add_kernel, count, some),
        out_shape=[shape(count, held, LANES, dtype=back.dtype), shape(ranks, SUBS, LANES)],
        in_specs=[SMEM, VMEM, VMEM, VMEM],
        out_specs=[VMEM, VMEM],
        scratch_shapes=[pltpu.VMEM((group, parts * some, LANES), jnp.float32)]
        + [pltpu.VMEM((count * held, LANES), jnp.float32)] * STREAMS,
        compiler_params=params(count * held),
        name="add_up",
    )(lists, lists, weights, back)


def body(noisy, matches, cube_home, sigma_coef):
    count = lax.axis_size("space")
    some, group = matches.shape
    held, width = noisy.shape
    parts = width // LANES
    refs = parts * some
    cube, cube_t = cube_tables()
    sigma = sigma_coef[None, :]
    dtype = noisy.dtype
    shared = spread_scratch(count, parts, held, dtype) + shrink_scratch(parts, group, refs)
    coeffs, back, weights, lists = pl.pallas_call(
        functools.partial(first_kernel, count),
        out_shape=[
            shape(group, refs, LANES),
            shape(group, refs, LANES, dtype=dtype),
            shape(SUBS, LANES),
            shape(parts, 2 * group, LANES, dtype=jnp.int32),
        ],
        in_specs=[HBM] * 5,
        out_specs=[HBM] + [VMEM] * 3,
        scratch_shapes=shared
        + [
            pltpu.VMEM(noisy.shape, dtype),
            pltpu.VMEM(cube_t.shape, dtype),
            pltpu.VMEM(sigma.shape, jnp.float32),
            pltpu.SMEM((group, some), jnp.int32),
            SEMS((5,)),
            pltpu.VMEM((group, refs, LANES), jnp.float32),
            SEMS((1,)),
            pltpu.SMEM(cube_home.shape, jnp.int32),
            pltpu.SMEM((2 * group, LANES), jnp.int32),
            pltpu.VMEM((parts, 2 * group, LANES), jnp.int32),
            pltpu.SMEM((parts, 2 * group, LANES), jnp.int32),
            SEMS((parts,)),
            SEMS((parts,)),
            SEMS((parts,)),
        ],
        compiler_params=params(count * held, 0),
        name="shrink",
    )(*[pltpu.with_memory_space_constraint(v, pltpu.HBM) for v in (noisy, cube_home, matches.T, sigma, jnp.asarray(cube_t))])
    acc, wsum = add_up(count, some, held, lists, weights, back)
    basic, back, weights = pl.pallas_call(
        functools.partial(second_kernel, count, some),
        out_shape=[
            shape(held, width, dtype=dtype),
            shape(group, refs, LANES, dtype=dtype),
            shape(SUBS, LANES),
        ],
        in_specs=[HBM] + [VMEM] * 5 + [SMEM, VMEM, HBM],
        out_specs=[VMEM] * 3,
        scratch_shapes=shared
        + [pltpu.VMEM((group, refs, LANES), jnp.float32), SEMS((1,))]
        + settle_scratch(count, parts, held, dtype),
        compiler_params=params(count * held, 1),
        name="wiener",
    )(acc, wsum, noisy, cube, cube_t, sigma, lists, lists, coeffs)
    acc, wsum = add_up(count, some, held, lists, weights, back)
    final = pl.pallas_call(
        functools.partial(third_kernel, count, parts),
        out_shape=shape(held, width, dtype=dtype),
        in_specs=[HBM] + [VMEM] * 3,
        out_specs=VMEM,
        scratch_shapes=settle_scratch(count, parts, held, dtype),
        compiler_params=params(count * held, 2),
        name="settle",
    )(acc, wsum, noisy, cube)
    return basic, final


def solution(mesh):
    in_specs = (P(("groups", "space"), None), P(("groups", "space"), None), P("groups"), P())
    out_specs = (P(("groups", "space"), None), P(("groups", "space"), None))
    return jax.shard_map(body, mesh=mesh, in_specs=in_specs, out_specs=out_specs, check_vma=False)
```

```python
import functools
import itertools

import jax
import jax.numpy as jnp
import numpy as np
from jax import lax
from jax.experimental import pallas as pl
from jax.experimental.pallas import tpu as pltpu
from jax.sharding import PartitionSpec as P

shrink_level = 2.7
prior_weight = 0.5
LANES = 128
SUBS = 8
PIECES = 2
STREAMS = 4
MESH = pl.DeviceIdType.MESH
VMEM = pl.BlockSpec(memory_space=pltpu.VMEM)
SMEM = pl.BlockSpec(memory_space=pltpu.SMEM)
HBM = pl.BlockSpec(memory_space=pltpu.HBM)
SEMS = pltpu.SemaphoreType.DMA


def dct_matrix(length):
    index = np.arange(length, dtype=np.float64)
    table = np.cos(np.pi * (2.0 * index[None, :] + 1.0) * index[:, None] / (2.0 * length))
    table = table * np.sqrt(2.0 / length)
    table[0] /= np.sqrt(2.0)
    return table


def cube_tables():
    small = dct_matrix(8)
    cube = np.kron(np.kron(small, small), small).astype(np.float32)
    return cube.astype(jnp.bfloat16), cube.T.astype(jnp.bfloat16)


def half_cosines(n):
    return [float(2.0 * np.cos(np.pi * (2 * i + 1) / (2 * n))) for i in range(n // 2)]


def cosine_sums(x):
    n = len(x)
    if n == 2:
        return [x[0] + x[1], (x[0] - x[1]) * float(np.cos(np.pi / 4))]
    half = n // 2
    even = cosine_sums([x[i] + x[n - 1 - i] for i in range(half)])
    turned = cosine_sums([(x[i] - x[n - 1 - i]) * f for i, f in enumerate(half_cosines(n))])
    out = [None] * n
    for k in range(half):
        out[2 * k] = even[k]
        out[2 * k + 1] = turned[k] - out[2 * k - 1] if k else 0.5 * turned[0]
    return out


def cosine_sums_transposed(y):
    n = len(y)
    if n == 2:
        odd = y[1] * float(np.cos(np.pi / 4))
        return [y[0] + odd, y[0] - odd]
    half = n // 2
    even = cosine_sums_transposed(y[0::2])
    tail = [None] * half
    for k in reversed(range(half)):
        tail[k] = y[2 * k + 1] - tail[k + 1] if k + 1 < half else y[2 * k + 1]
    tail[0] = 0.5 * tail[0]
    odd = [o * f for o, f in zip(cosine_sums_transposed(tail), half_cosines(n))]
    return [even[i] + odd[i] for i in range(half)] + [even[i] - odd[i] for i in reversed(range(half))]


def scales(n):
    return [float(np.sqrt((1.0 if k == 0 else 2.0) / n)) for k in range(n)]


def flip(value, mask):
    if isinstance(mask, int):
        for bit in (1 << b for b in range(mask.bit_length())):
            if mask & bit:
                value = value + bit - 2 * bit * lax.rem(value // bit, 2)
        return value
    for bit in (1, 2):
        value = value + bit * lax.rem(mask // bit, 2) * (1 - 2 * lax.rem(value // bit, 2))
    return value


def lowest(d, count):
    return d & -d if d else count


class Place:
    def __init__(self, count, parts):
        self.parts, self.ranks = parts, count // parts
        me = lax.axis_index("space")
        self.part, self.rank = me // self.ranks, lax.rem(me, self.ranks)
        self.bits = [1 << b for b in range(self.ranks.bit_length() - 1)]

    def index(self, off, d):
        return flip(self.part, off) * self.ranks + flip(self.rank, d)

    def device(self, off, d):
        return {"space": self.index(off, d)}

    def greet(self):
        barrier = pltpu.get_barrier_semaphore()
        peers = [(off, 0) for off in range(1, self.parts)] + [(0, d) for d in range(1, self.ranks)]
        for off, d in peers:
            pl.semaphore_signal(barrier, inc=1, device_id=self.device(off, d), device_id_type=MESH)
        pl.semaphore_wait(barrier, len(peers))


def remote(src, dst, send, recv, device):
    return pltpu.make_async_remote_copy(
        src_ref=src, dst_ref=dst, send_sem=send, recv_sem=recv, device_id=device, device_id_type=MESH
    )


def piece_of(ref, h):
    size = ref.shape[0] // PIECES
    return ref.at[pl.ds(h * size, size), :]


class Spread:
    def __init__(self, place, stage, got, table, send, recv):
        self.place, self.stage, self.got, self.table = place, stage, got, table
        self.send, self.recv, self.started = send, recv, []

    def block(self, off, d):
        return self.stage.at[0] if off == 0 and d == 0 else self.got.at[off, d]

    def pass_on(self, off, d, h):
        place = self.place
        for bit in reversed(place.bits):
            if bit < lowest(d, place.ranks):
                copy = remote(
                    piece_of(self.block(off, d), h),
                    piece_of(self.got.at[off, d | bit], h),
                    self.send.at[off, d | bit, h],
                    self.recv.at[off, d | bit, h],
                    place.device(0, bit),
                )
                copy.start()
                self.started.append(copy)

    def begin(self, h, rows, cube_t):
        place = self.place
        for off in list(range(1, place.parts)) + [0]:
            columns = pl.ds(pl.multiple_of(flip(place.part, off) * LANES, LANES), LANES)
            spec = jnp.dot(rows, cube_t[:, columns], preferred_element_type=jnp.float32)
            piece = piece_of(self.stage.at[off], h)
            piece[...] = spec.astype(self.stage.dtype)
            if off == 0:
                self.pass_on(0, 0, h)
                continue
            copy = remote(
                piece,
                piece_of(self.got.at[off, 0], h),
                self.send.at[off, 0, h],
                self.recv.at[off, 0, h],
                place.device(off, 0),
            )
            copy.start()
            self.started.append(copy)

    def widen(self, off, d, h):
        source = piece_of(self.block(off, d), h)
        held = self.stage.shape[1]
        size = held // PIECES
        first = self.place.index(off, d) * held + h * size
        rows = pl.ds(pl.multiple_of(first, size), size)
        self.table[rows, :] = source[...].astype(jnp.float32)

    def finish(self):
        place = self.place

        def when(key):
            off, d, h = key
            return off + 0.5 * h + sum(2.2 if b == 1 else 1.6 for b in place.bits if d & b)

        keys = [
            (off, d, h)
            for off in range(place.parts)
            for d in range(place.ranks)
            for h in range(PIECES)
            if off or d
        ]
        for h in range(PIECES):
            self.widen(0, 0, h)
        for off, d, h in sorted(keys, key=when):
            piece = piece_of(self.got.at[off, d], h)
            remote(
                piece, piece, self.send.at[off, d, h], self.recv.at[off, d, h], place.device(off, d)
            ).wait_recv()
            self.pass_on(off, d, h)
            self.widen(off, d, h)

    def close(self):
        for copy in self.started:
            copy.wait_send()


def spread_scratch(count, parts, held, dtype):
    ranks = count // parts
    return [
        pltpu.VMEM((parts, held, LANES), dtype),
        pltpu.VMEM((parts, ranks, held, LANES), dtype),
        pltpu.VMEM((count * held, LANES), jnp.float32),
        SEMS((parts, ranks, PIECES)),
        SEMS((parts, ranks, PIECES)),
    ]


def pick_rows(table, lists, members, some):
    group = members.shape[0]

    def step(t, carry):
        src, row = t // (some // SUBS), lax.rem(t, some // SUBS)
        for q in range(SUBS):
            for m in range(group):
                spot = lists[m][src, row * SUBS + q]
                members[m, pl.ds(t * SUBS + q, 1), :] = table[pl.ds(spot, 1), :]
        return carry

    lax.fori_loop(0, members.shape[1] // SUBS, step, 0)


def to_scalars(lists, scalars, sem):
    copies = [pltpu.make_async_copy(lists.at[m], each, sem.at[m]) for m, each in enumerate(scalars)]
    for copy in copies:
        copy.start()
    return copies


def find_equals(lists, same, group, some):
    for src in range(lists.shape[0]):
        rows = lists[src]
        equal = [jnp.where(rows == pltpu.roll(rows, back, 0), 1.0, 0.0) for back in range(1, group // STREAMS)]
        equal.append(jnp.zeros((LANES - group * len(equal), LANES), jnp.float32))
        same[src * some : (src + 1) * some, :] = jnp.concatenate(equal, axis=0).T[:some, :]


def diagonal(rows):
    shape = (rows, LANES)
    return lax.broadcasted_iota(jnp.int32, shape, 0) == lax.broadcasted_iota(jnp.int32, shape, 1)


def shrink_groups(place, second, width, some, sigma, members, coeffs, back, lists_v, same, energy, ebuf, egot, weights, send, recv, then=None):
    group, refs = members.shape[:2]
    factor = scales(group)
    columns = pl.ds(pl.multiple_of(place.part * LANES, LANES), LANES)
    own = sigma[:, columns]
    level = own * own if second else (shrink_level * own) * (shrink_level * own)

    def forward(b, carry):
        rows = pl.ds(pl.multiple_of(b * SUBS, SUBS), SUBS)
        values = cosine_sums([members[m, rows, :] for m in range(group)])
        total = None
        for j in range(group):
            value = values[j] * factor[j]
            square = value * value
            gain = square / (square + level)
            power = gain * gain
            total = power if total is None else total + power
            if second:
                members[j, rows, :] = gain * coeffs[j, rows, :]
            else:
                coeffs[j, rows, :] = value
                members[j, rows, :] = gain * value
        energy[rows, :] = total * level if second else total
        return carry

    lax.fori_loop(0, refs // SUBS, forward, 0)
    if then is not None:
        then()
    parts = refs // some
    for src in range(parts):
        column = jnp.sum(energy[src * some : (src + 1) * some, :], axis=1, keepdims=True)
        ebuf[src : src + 1, :] = jnp.sum(jnp.where(diagonal(some), column, 0.0), axis=0, keepdims=True)
    started = []
    for off in range(1, place.parts):
        copy = remote(ebuf, egot.at[off], send.at[off], recv.at[off], place.device(off, 0))
        copy.start()
        started.append(copy)

    find_equals(lists_v, same, group, some)

    def inverse(b, carry):
        rows = pl.ds(pl.multiple_of(b * 2 * SUBS, 2 * SUBS), 2 * SUBS)
        values = cosine_sums_transposed([members[j, rows, :] * factor[j] for j in range(group)])
        for m in range(group):
            merged = values[m]
            for before in range(1, m % (group // STREAMS) + 1):
                lane = (before - 1) * group + m
                merged = merged + same[rows, lane : lane + 1] * values[m - before]
            back[m, rows, :] = merged.astype(back.dtype)
        return carry

    lax.fori_loop(0, refs // (2 * SUBS), inverse, 0)
    total = ebuf[...]
    for off in range(1, place.parts):
        remote(ebuf, egot.at[off], send.at[off], recv.at[off], place.device(off, 0)).wait_recv()
        total = total + egot[off]
    weights[...] = 1.0 / (0.25 + total / (group * width))
    for copy in started:
        copy.wait_send()


def shrink_scratch(parts, group, refs):
    assert parts <= SUBS
    return [
        pltpu.VMEM((group, refs, LANES), jnp.float32),
        pltpu.VMEM((refs, LANES), jnp.float32),
        pltpu.VMEM((refs, LANES), jnp.float32),
        pltpu.VMEM((SUBS, LANES), jnp.float32),
        pltpu.VMEM((parts, SUBS, LANES), jnp.float32),
        SEMS((parts,)),
        SEMS((parts,)),
    ]


def first_kernel(count, x_in, home_in, ids_in, sigma_in, cube_in, coeffs_out, back, weights, lists_out, turned, *scratch):
    stage, got, table, send, recv = scratch[:5]
    members, same, energy, ebuf, egot, esend, erecv = scratch[5:12]
    x, cube_t, sigma, ids, insem = scratch[12:17]
    coeffs, csem, home, named, lists_v, lsend, lrecv, lsem = scratch[17:25]
    scalars = scratch[25:]
    parts = stage.shape[0]
    group, some = ids.shape
    size = x.shape[0] // PIECES
    place = Place(count, parts)
    pairs = [(x_in, x), (cube_in, cube_t), (home_in, home), (ids_in, ids), (sigma_in, sigma)]
    fetches = [pltpu.make_async_copy(src, dst, insem.at[i]) for i, (src, dst) in enumerate(pairs)]
    for fetch in fetches:
        fetch.start()
    place.greet()
    for fetch in fetches[:2]:
        fetch.wait()
    spread = Spread(place, stage, got, table, send, recv)
    for h in range(PIECES):
        spread.begin(h, x[h * size : (h + 1) * size, :], cube_t)

    def look_up(row, carry):
        for q in range(SUBS):
            for m in range(group):
                named[m, row * SUBS + q] = home[ids[m, row * SUBS + q]]
        return carry

    for fetch in fetches[2:]:
        fetch.wait()
    lax.fori_loop(0, some // SUBS, look_up, 0)

    def fill(m, carry):
        for q in range(some, LANES):
            named[m, q] = 0
        return carry

    lax.fori_loop(0, group, fill, 0)

    ebuf[...] = jnp.zeros(ebuf.shape, ebuf.dtype)
    mine = pltpu.make_async_copy(named, lists_v.at[place.part], lsem.at[0])
    mine.start()
    mine.wait()
    started = []
    for off in range(1, parts):
        copy = remote(
            lists_v.at[place.part],
            lists_v.at[place.part],
            lsend.at[off],
            lrecv.at[off],
            place.device(off, 0),
        )
        copy.start()
        started.append(copy)
    spread.finish()
    for off in range(1, parts):
        source = lists_v.at[flip(place.part, off)]
        remote(source, source, lsend.at[off], lrecv.at[off], place.device(off, 0)).wait_recv()
    lists_out[...] = lists_v[...]
    turned[...] = jnp.zeros(turned.shape, turned.dtype)
    for m in range(group):
        for src in range(parts):
            turned[m, src : src + 1, :] = lists_v[src, m : m + 1, :]
    for copy in to_scalars(turned, scalars, lsem):
        copy.wait()
    pick_rows(table, scalars, members, some)
    store = pltpu.make_async_copy(coeffs, coeffs_out, csem.at[0])
    shrink_groups(
        place, False, x.shape[1], some, sigma, members, coeffs, back, lists_v, same, energy, ebuf, egot, weights, esend, erecv, store.start
    )
    store.wait()
    for copy in started:
        copy.wait_send()
    spread.close()


class Collect:
    def __init__(self, place, acc, own, got, sent, zgot, local, send, recv):
        self.place, self.acc, self.own, self.got, self.sent, self.zgot = place, acc, own, got, sent, zgot
        self.local, self.send, self.recv, self.started = local, send, recv, []
        self.order = list(range(place.parts - 1, -1, -1))

    def start(self, copy):
        copy.start()
        self.started.append(copy)

    def fetch(self, off, d):
        return pltpu.make_async_copy(
            self.acc.at[self.place.index(off, d)], self.own.at[off, d // 2], self.local.at[off, d // 2]
        )

    def open(self):
        place = self.place
        for d in sorted(range(0, place.ranks, 2), key=lambda d: lowest(d, place.ranks)):
            for off in self.order:
                self.fetch(off, d).start()

    def begin(self):
        place = self.place
        for d in sorted(range(1, place.ranks, 2), key=lambda d: lowest(d - 1, place.ranks)):
            for off in self.order:
                for h in range(PIECES):
                    self.start(
                        remote(
                            piece_of(self.acc.at[place.index(off, d)], h),
                            piece_of(self.got.at[off, d], h),
                            self.send.at[off, d, h],
                            self.recv.at[off, d, h],
                            place.device(0, 1),
                        )
                    )

    def value(self, off, d, h):
        place = self.place
        if h == 0:
            self.fetch(off, d).wait()
        total = piece_of(self.own.at[off, d // 2], h)[...].astype(jnp.float32)
        for bit in place.bits:
            if bit < lowest(d, place.ranks):
                piece = piece_of(self.got.at[off, d | bit], h)
                remote(
                    piece, piece, self.send.at[off, d | bit, h], self.recv.at[off, d | bit, h], place.device(0, bit)
                ).wait_recv()
                total = total + piece[...].astype(jnp.float32)
        return total

    def run(self):
        place = self.place
        for level in place.bits[1:] + [place.ranks]:
            ds = [d for d in range(0, place.ranks, 2) if lowest(d, place.ranks) == level]
            for d, off, h in itertools.product(ds, self.order, range(PIECES)):
                piece = piece_of(self.sent.at[off, d // 2], h)
                piece[...] = self.value(off, d, h).astype(self.sent.dtype)
                if d == 0 and off == 0:
                    continue
                bit = lowest(d, 0)
                self.start(
                    remote(
                        piece,
                        piece_of(self.got.at[off, d] if d else self.zgot.at[off], h),
                        self.send.at[off, d, h],
                        self.recv.at[off, d, h],
                        place.device(0, bit) if d else place.device(off, 0),
                    )
                )

    def slices(self, h):
        place = self.place
        yield 0, piece_of(self.sent.at[0, 0], h)[...]
        for off in range(1, place.parts):
            piece = piece_of(self.zgot.at[off], h)
            remote(
                piece, piece, self.send.at[off, 0, h], self.recv.at[off, 0, h], place.device(off, 0)
            ).wait_recv()
            yield off, piece[...]

    def close(self):
        for copy in self.started:
            copy.wait_send()


def settle(place, acc, wsum, noisy, cube, out, own, got, sent, zgot, wgot, local, send, recv, wsend, wrecv, then=None):
    held = noisy.shape[0]
    collect = Collect(place, acc, own, got, sent, zgot, local, send, recv)
    collect.open()
    place.greet()
    collect.begin()
    for d in range(1, place.ranks):
        collect.start(
            remote(wsum.at[flip(place.rank, d)], wgot.at[d], wsend.at[d], wrecv.at[d], place.device(0, d))
        )
    collect.run()
    denom = wsum[place.rank]
    for d in range(1, place.ranks):
        remote(wgot.at[d], wgot.at[d], wsend.at[d], wrecv.at[d], place.device(0, d)).wait_recv()
        denom = denom + wgot[d]
    size = held // PIECES
    for h in range(PIECES):
        numer = prior_weight * noisy[pl.ds(h * size, size), :].astype(jnp.float32)
        for off, part in collect.slices(h):
            rows = pl.ds(pl.multiple_of(flip(place.part, off) * LANES, LANES), LANES)
            numer = numer + jnp.dot(part, cube[rows, :], preferred_element_type=jnp.float32)
        for j in range(size // LANES):
            row = h * (size // LANES) + j
            spread = jnp.broadcast_to(denom[row : row + 1, :], (LANES, LANES))
            column = jnp.sum(jnp.where(diagonal(LANES), spread, 0.0), axis=1, keepdims=True)
            out[pl.ds(row * LANES, LANES), :] = (
                numer[j * LANES : (j + 1) * LANES, :] / (column + prior_weight)
            ).astype(out.dtype)
        if then is not None:
            then(h)
    return collect


def settle_scratch(count, parts, held, dtype):
    ranks = count // parts
    half = (parts, ranks // 2, held, LANES)
    return [
        pltpu.VMEM(half, dtype),
        pltpu.VMEM((parts, ranks, held, LANES), dtype),
        pltpu.VMEM(half, dtype),
        pltpu.VMEM((parts, held, LANES), dtype),
        pltpu.VMEM((ranks, SUBS, LANES), jnp.float32),
        SEMS((parts, ranks // 2)),
        SEMS((parts, ranks, PIECES)),
        SEMS((parts, ranks, PIECES)),
        SEMS((ranks,)),
        SEMS((ranks,)),
    ]


def second_kernel(count, some, acc, wsum, noisy, cube, cube_t, sigma, lists_v, turned, coeffs_in, basic, back, weights, *scratch):
    stage, got, table, send, recv = scratch[:5]
    members, same, energy, ebuf, egot, esend, erecv = scratch[5:12]
    coeffs, csem, lsem = scratch[12:15]
    group = members.shape[0]
    scalars = scratch[15 : 15 + group]
    size = noisy.shape[0] // PIECES
    parts = stage.shape[0]
    place = Place(count, parts)
    fetch = pltpu.make_async_copy(coeffs_in, coeffs, csem.at[0])
    fetch.start()
    copies = to_scalars(turned, scalars, lsem)
    spread = Spread(place, stage, got, table, send, recv)
    ebuf[...] = jnp.zeros(ebuf.shape, ebuf.dtype)
    collect = settle(
        place,
        acc,
        wsum,
        noisy,
        cube,
        basic,
        *scratch[15 + group :],
        then=lambda h: spread.begin(h, basic[h * size : (h + 1) * size, :], cube_t),
    )
    spread.finish()
    for copy in copies:
        copy.wait()
    pick_rows(table, scalars, members, some)
    fetch.wait()
    shrink_groups(
        place, True, noisy.shape[1], some, sigma, members, coeffs, back, lists_v, same, energy, ebuf, egot, weights, esend, erecv
    )
    collect.close()
    spread.close()


def third_kernel(count, parts, acc, wsum, noisy, cube, out, *scratch):
    settle(Place(count, parts), acc, wsum, noisy, cube, out, *scratch).close()


def add_kernel(count, some, carried, turned, weights, back, *refs):
    group, refs_here = back.shape[:2]
    parts = refs_here // some
    kept = refs[:carried]
    acc, wsum = refs[carried : carried + 2]
    outs = refs[carried + 2 : 2 * carried + 2]
    members, ksem, lsem = refs[2 * carried + 2 : 2 * carried + 5]
    scalars = refs[2 * carried + 5 : 2 * carried + 5 + group]
    sums = refs[2 * carried + 5 + group :]
    place = Place(count, parts)
    blocks, held = acc.shape[:2]
    copies = to_scalars(turned, scalars, lsem)
    moves = [pltpu.make_async_copy(src, dst, ksem.at[i]) for i, (src, dst) in enumerate(zip(kept, outs))]
    for move in moves:
        move.start()

    def clear(i, carry):
        rows = pl.ds(pl.multiple_of(i * LANES, LANES), LANES)
        for each in sums:
            each[rows, :] = jnp.zeros((LANES, LANES), jnp.float32)
        return carry

    lax.fori_loop(0, blocks * held // LANES, clear, 0)
    for src in range(parts):
        row = jnp.broadcast_to(weights[src : src + 1, :], (some, LANES))
        column = jnp.sum(jnp.where(diagonal(some), row, 0.0), axis=1, keepdims=True)
        spread = jnp.broadcast_to(column, (some, LANES))
        rows = pl.ds(src * some, some)

        def scale(m, carry):
            members[m, rows, :] = back[m, rows, :].astype(jnp.float32) * spread
            return carry

        lax.fori_loop(0, group, scale, 0)

    many = wsum.shape[0] * (held // LANES)
    lane = lax.broadcasted_iota(jnp.int32, (1, LANES), 1)
    heavy = [jnp.where(lane < some, weights[src : src + 1, :], 0.0) for src in range(parts)]
    tall = lax.broadcasted_iota(jnp.int32, (many, LANES), 0)
    low = lax.broadcasted_iota(jnp.int32, (LANES, LANES), 0)
    first = place.part * (many * LANES)

    def weigh(m, total):
        ones, loads = [], []
        for src in range(parts):
            spots = turned[m, src : src + 1, :] - first
            loads.append(jnp.where((spots >> 7) == tall, heavy[src], 0.0).astype(jnp.bfloat16))
            ones.append(jnp.where((spots & (LANES - 1)) == low, 1.0, 0.0).astype(jnp.bfloat16))
        return total + lax.dot_general(
            jnp.concatenate(loads, axis=1),
            jnp.concatenate(ones, axis=1),
            (((1,), (1,)), ((), ())),
            preferred_element_type=jnp.float32,
        )

    total = lax.fori_loop(0, group, weigh, jnp.zeros((many, LANES), jnp.float32), unroll=True)
    per = held // LANES
    for b in range(wsum.shape[0]):
        wsum[b, :per, :] = total[b * per : (b + 1) * per, :]
        if per < SUBS:
            wsum[b, per:, :] = jnp.zeros((SUBS - per, LANES), jnp.float32)

    together = group // STREAMS
    for copy in copies:
        copy.wait()

    def step(t, carry):
        src, row = t // (some // SUBS), lax.rem(t, some // SUBS)
        for q in range(SUBS):
            spots, news = [], []
            for m in range(group):
                spot = scalars[m][src, row * SUBS + q]
                spots.append(spot)
                news.append(sums[m // together][pl.ds(spot, 1), :] + members[m, pl.ds(t * SUBS + q, 1), :])
            for m in range(group):
                sums[m // together][pl.ds(spots[m], 1), :] = news[m]
        return carry

    lax.fori_loop(0, refs_here // SUBS, step, 0)

    def store(b, carry):
        for i in range(held // LANES):
            rows = pl.ds(pl.multiple_of(b * held + i * LANES, LANES), LANES)
            whole = sums[0][rows, :]
            for each in sums[1:]:
                whole = whole + each[rows, :]
            acc[b, i * LANES : (i + 1) * LANES, :] = whole.astype(acc.dtype)
        return carry

    lax.fori_loop(0, blocks, store, 0)
    for move in moves:
        move.wait()


def shape(*dims, dtype=jnp.float32):
    return jax.ShapeDtypeStruct(dims, dtype)


def params(rows, collective_id=None):
    limit = 5 * rows * LANES * 4 + (10 << 20)
    return pltpu.CompilerParams(
        collective_id=collective_id, has_side_effects=collective_id is not None, vmem_limit_bytes=limit
    )


def add_up(count, some, held, turned, weights, back, *kept):
    group, refs = back.shape[:2]
    ranks = count // (refs // some)
    return pl.pallas_call(
        functools.partial(add_kernel, count, some, len(kept)),
        out_shape=[shape(count, held, LANES, dtype=back.dtype), shape(ranks, SUBS, LANES)]
        + [shape(*each.shape, dtype=each.dtype) for each in kept],
        in_specs=[VMEM, VMEM, VMEM] + [VMEM] * len(kept),
        out_specs=[VMEM, VMEM] + [HBM] * len(kept),
        scratch_shapes=[pltpu.VMEM((group, refs, LANES), jnp.float32), SEMS((1,)), SEMS((group,))]
        + [pltpu.SMEM((SUBS, LANES), jnp.int32)] * group
        + [pltpu.VMEM((count * held, LANES), jnp.float32)] * STREAMS,
        compiler_params=params(count * held),
        name="add_up",
    )(turned, weights, back, *kept)


def body(noisy, matches, cube_home, sigma_coef):
    count = lax.axis_size("space")
    some, group = matches.shape
    held, width = noisy.shape
    parts = width // LANES
    refs = parts * some
    cube, cube_t = cube_tables()
    sigma = sigma_coef[None, :]
    dtype = noisy.dtype
    shared = spread_scratch(count, parts, held, dtype) + shrink_scratch(parts, group, refs)
    coeffs, back, weights, lists, turned = pl.pallas_call(
        functools.partial(first_kernel, count),
        out_shape=[
            shape(group, refs, LANES),
            shape(group, refs, LANES, dtype=dtype),
            shape(SUBS, LANES),
            shape(parts, group, LANES, dtype=jnp.int32),
            shape(group, SUBS, LANES, dtype=jnp.int32),
        ],
        in_specs=[HBM] * 5,
        out_specs=[HBM] + [VMEM] * 4,
        scratch_shapes=shared
        + [
            pltpu.VMEM(noisy.shape, dtype),
            pltpu.VMEM(cube_t.shape, dtype),
            pltpu.VMEM(sigma.shape, jnp.float32),
            pltpu.SMEM((group, some), jnp.int32),
            SEMS((5,)),
            pltpu.VMEM((group, refs, LANES), jnp.float32),
            SEMS((1,)),
            pltpu.SMEM(cube_home.shape, jnp.int32),
            pltpu.SMEM((group, LANES), jnp.int32),
            pltpu.VMEM((parts, group, LANES), jnp.int32),
            SEMS((parts,)),
            SEMS((parts,)),
            SEMS((group,)),
        ]
        + [pltpu.SMEM((SUBS, LANES), jnp.int32)] * group,
        compiler_params=params(count * held, 0),
        name="shrink",
    )(*[pltpu.with_memory_space_constraint(v, pltpu.HBM) for v in (noisy, cube_home, matches.T, sigma, jnp.asarray(cube_t))])
    acc, wsum = add_up(count, some, held, turned, weights, back)
    basic, back, weights = pl.pallas_call(
        functools.partial(second_kernel, count, some),
        out_shape=[
            shape(held, width, dtype=dtype),
            shape(group, refs, LANES, dtype=dtype),
            shape(SUBS, LANES),
        ],
        in_specs=[HBM] + [VMEM] * 7 + [HBM],
        out_specs=[VMEM] * 3,
        scratch_shapes=shared
        + [pltpu.VMEM((group, refs, LANES), jnp.float32), SEMS((1,)), SEMS((group,))]
        + [pltpu.SMEM((SUBS, LANES), jnp.int32)] * group
        + settle_scratch(count, parts, held, dtype),
        compiler_params=params(count * held, 1),
        name="wiener",
    )(acc, wsum, noisy, cube, cube_t, sigma, lists, turned, coeffs)
    acc, wsum, basic = add_up(count, some, held, turned, weights, back, basic)
    final = pl.pallas_call(
        functools.partial(third_kernel, count, parts),
        out_shape=shape(held, width, dtype=dtype),
        in_specs=[HBM] + [VMEM] * 3,
        out_specs=VMEM,
        scratch_shapes=settle_scratch(count, parts, held, dtype),
        compiler_params=params(count * held, 2),
        name="settle",
    )(acc, wsum, noisy, cube)
    return basic, final


def solution(mesh):
    in_specs = (P(("groups", "space"), None), P(("groups", "space"), None), P("groups"), P())
    out_specs = (P(("groups", "space"), None), P(("groups", "space"), None))
    return jax.shard_map(body, mesh=mesh, in_specs=in_specs, out_specs=out_specs, check_vma=False)
```

```python
import functools
import itertools

import jax
import jax.numpy as jnp
import numpy as np
from jax import lax
from jax.experimental import pallas as pl
from jax.experimental.pallas import tpu as pltpu
from jax.sharding import PartitionSpec as P

shrink_level = 2.7
prior_weight = 0.5
LANES = 128
SUBS = 8
PIECES = 2
STREAMS = 4
MESH = pl.DeviceIdType.MESH
VMEM = pl.BlockSpec(memory_space=pltpu.VMEM)
SMEM = pl.BlockSpec(memory_space=pltpu.SMEM)
HBM = pl.BlockSpec(memory_space=pltpu.HBM)
SEMS = pltpu.SemaphoreType.DMA


def dct_matrix(length):
    index = np.arange(length, dtype=np.float64)
    table = np.cos(np.pi * (2.0 * index[None, :] + 1.0) * index[:, None] / (2.0 * length))
    table = table * np.sqrt(2.0 / length)
    table[0] /= np.sqrt(2.0)
    return table


def cube_tables():
    small = dct_matrix(8)
    cube = np.kron(np.kron(small, small), small).astype(np.float32)
    return cube.astype(jnp.bfloat16), cube.T.astype(jnp.bfloat16)


def half_cosines(n):
    return [float(2.0 * np.cos(np.pi * (2 * i + 1) / (2 * n))) for i in range(n // 2)]


def cosine_sums(x):
    n = len(x)
    if n == 2:
        return [x[0] + x[1], (x[0] - x[1]) * float(np.cos(np.pi / 4))]
    half = n // 2
    even = cosine_sums([x[i] + x[n - 1 - i] for i in range(half)])
    turned = cosine_sums([(x[i] - x[n - 1 - i]) * f for i, f in enumerate(half_cosines(n))])
    out = [None] * n
    for k in range(half):
        out[2 * k] = even[k]
        out[2 * k + 1] = turned[k] - out[2 * k - 1] if k else 0.5 * turned[0]
    return out


def cosine_sums_transposed(y):
    n = len(y)
    if n == 2:
        odd = y[1] * float(np.cos(np.pi / 4))
        return [y[0] + odd, y[0] - odd]
    half = n // 2
    even = cosine_sums_transposed(y[0::2])
    tail = [None] * half
    for k in reversed(range(half)):
        tail[k] = y[2 * k + 1] - tail[k + 1] if k + 1 < half else y[2 * k + 1]
    tail[0] = 0.5 * tail[0]
    odd = [o * f for o, f in zip(cosine_sums_transposed(tail), half_cosines(n))]
    return [even[i] + odd[i] for i in range(half)] + [even[i] - odd[i] for i in reversed(range(half))]


def scales(n):
    return [float(np.sqrt((1.0 if k == 0 else 2.0) / n)) for k in range(n)]


def flip(value, mask):
    if isinstance(mask, int):
        for bit in (1 << b for b in range(mask.bit_length())):
            if mask & bit:
                value = value + bit - 2 * bit * lax.rem(value // bit, 2)
        return value
    for bit in (1, 2):
        value = value + bit * lax.rem(mask // bit, 2) * (1 - 2 * lax.rem(value // bit, 2))
    return value


def lowest(d, count):
    return d & -d if d else count


class Place:
    def __init__(self, count, parts):
        self.parts, self.ranks = parts, count // parts
        me = lax.axis_index("space")
        self.part, self.rank = me // self.ranks, lax.rem(me, self.ranks)
        self.bits = [1 << b for b in range(self.ranks.bit_length() - 1)]

    def index(self, off, d):
        return flip(self.part, off) * self.ranks + flip(self.rank, d)

    def device(self, off, d):
        return {"space": self.index(off, d)}

    def greet(self):
        barrier = pltpu.get_barrier_semaphore()
        peers = [(off, 0) for off in range(1, self.parts)] + [(0, d) for d in range(1, self.ranks)]
        for off, d in peers:
            pl.semaphore_signal(barrier, inc=1, device_id=self.device(off, d), device_id_type=MESH)
        pl.semaphore_wait(barrier, len(peers))


def remote(src, dst, send, recv, device):
    return pltpu.make_async_remote_copy(
        src_ref=src, dst_ref=dst, send_sem=send, recv_sem=recv, device_id=device, device_id_type=MESH
    )


def piece_of(ref, h):
    size = ref.shape[0] // PIECES
    return ref.at[pl.ds(h * size, size), :]


class Spread:
    def __init__(self, place, stage, got, table, send, recv):
        self.place, self.stage, self.got, self.table = place, stage, got, table
        self.send, self.recv, self.started = send, recv, []

    def block(self, off, d):
        return self.stage.at[0] if off == 0 and d == 0 else self.got.at[off, d]

    def pass_on(self, off, d, h):
        place = self.place
        for bit in reversed(place.bits):
            if bit < lowest(d, place.ranks):
                copy = remote(
                    piece_of(self.block(off, d), h),
                    piece_of(self.got.at[off, d | bit], h),
                    self.send.at[off, d | bit, h],
                    self.recv.at[off, d | bit, h],
                    place.device(0, bit),
                )
                copy.start()
                self.started.append(copy)

    def begin(self, hs, rows, cube_t):
        place = self.place
        size = rows.shape[0] // PIECES
        for off, h in itertools.product(list(range(1, place.parts)) + [0], hs):
            columns = pl.ds(pl.multiple_of(flip(place.part, off) * LANES, LANES), LANES)
            part = rows[h * size : (h + 1) * size, :]
            spec = jnp.dot(part, cube_t[:, columns], preferred_element_type=jnp.float32)
            piece = piece_of(self.stage.at[off], h)
            piece[...] = spec.astype(self.stage.dtype)
            if off == 0:
                self.pass_on(0, 0, h)
                continue
            copy = remote(
                piece,
                piece_of(self.got.at[off, 0], h),
                self.send.at[off, 0, h],
                self.recv.at[off, 0, h],
                place.device(off, 0),
            )
            copy.start()
            self.started.append(copy)

    def widen(self, off, d, h):
        source = piece_of(self.block(off, d), h)
        held = self.stage.shape[1]
        size = held // PIECES
        first = self.place.index(off, d) * held + h * size
        rows = pl.ds(pl.multiple_of(first, size), size)
        self.table[rows, :] = source[...].astype(jnp.float32)

    def finish(self, then=None):
        place = self.place

        def when(key):
            off, d, h = key
            return off + 0.5 * h + sum(2.2 if b == 1 else 1.6 for b in place.bits if d & b)

        keys = [
            (off, d, h)
            for off in range(place.parts)
            for d in range(place.ranks)
            for h in range(PIECES)
            if off or d
        ]
        for h in range(PIECES):
            self.widen(0, 0, h)
        for off, d, h in sorted(keys, key=when):
            piece = piece_of(self.got.at[off, d], h)
            remote(
                piece, piece, self.send.at[off, d, h], self.recv.at[off, d, h], place.device(off, d)
            ).wait_recv()
            self.pass_on(off, d, h)
            self.widen(off, d, h)
            if then is not None and (off, d, h) == (place.parts - 1, 0, PIECES - 1):
                then()

    def close(self):
        for copy in self.started:
            copy.wait_send()


def spread_scratch(count, parts, held, dtype):
    ranks = count // parts
    return [
        pltpu.VMEM((parts, held, LANES), dtype),
        pltpu.VMEM((parts, ranks, held, LANES), dtype),
        pltpu.VMEM((count * held, LANES), jnp.float32),
        SEMS((parts, ranks, PIECES)),
        SEMS((parts, ranks, PIECES)),
    ]


def pick_rows(table, lists, members, some):
    group = members.shape[0]

    def step(t, carry):
        src, row = t // (some // SUBS), lax.rem(t, some // SUBS)
        for q in range(SUBS):
            for m in range(group):
                spot = lists[m][src, row * SUBS + q]
                members[m, pl.ds(t * SUBS + q, 1), :] = table[pl.ds(spot, 1), :]
        return carry

    lax.fori_loop(0, members.shape[1] // SUBS, step, 0)


def to_scalars(lists, scalars, sem):
    copies = [pltpu.make_async_copy(lists.at[m], each, sem.at[m]) for m, each in enumerate(scalars)]
    for copy in copies:
        copy.start()
    return copies


def find_equals(lists, same, group, some):
    for src in range(lists.shape[0]):
        rows = lists[src]
        equal = [jnp.where(rows == pltpu.roll(rows, back, 0), 1.0, 0.0) for back in range(1, group // STREAMS)]
        equal.append(jnp.zeros((LANES - group * len(equal), LANES), jnp.float32))
        same[src * some : (src + 1) * some, :] = jnp.concatenate(equal, axis=0).T[:some, :]


def diagonal(rows):
    shape = (rows, LANES)
    return lax.broadcasted_iota(jnp.int32, shape, 0) == lax.broadcasted_iota(jnp.int32, shape, 1)


def shrink_groups(place, second, width, some, sigma, members, coeffs, back, same, energy, ebuf, egot, weights, send, recv, then=None):
    group, refs = members.shape[:2]
    factor = scales(group)
    columns = pl.ds(pl.multiple_of(place.part * LANES, LANES), LANES)
    own = sigma[:, columns]
    level = own * own if second else (shrink_level * own) * (shrink_level * own)

    def forward(b, carry):
        rows = pl.ds(pl.multiple_of(b * SUBS, SUBS), SUBS)
        values = cosine_sums([members[m, rows, :] for m in range(group)])
        total = None
        for j in range(group):
            value = values[j] * factor[j]
            square = value * value
            gain = square / (square + level)
            power = gain * gain
            total = power if total is None else total + power
            if second:
                members[j, rows, :] = gain * coeffs[j, rows, :]
            else:
                coeffs[j, rows, :] = value
                members[j, rows, :] = gain * value
        energy[rows, :] = total * level if second else total
        return carry

    lax.fori_loop(0, refs // SUBS, forward, 0)
    if then is not None:
        then()
    parts = refs // some
    for src in range(parts):
        column = jnp.sum(energy[src * some : (src + 1) * some, :], axis=1, keepdims=True)
        ebuf[src : src + 1, :] = jnp.sum(jnp.where(diagonal(some), column, 0.0), axis=0, keepdims=True)
    started = []
    for off in range(1, place.parts):
        copy = remote(ebuf, egot.at[off], send.at[off], recv.at[off], place.device(off, 0))
        copy.start()
        started.append(copy)

    def inverse(b, carry):
        rows = pl.ds(pl.multiple_of(b * 2 * SUBS, 2 * SUBS), 2 * SUBS)
        values = cosine_sums_transposed([members[j, rows, :] * factor[j] for j in range(group)])
        for m in range(group):
            merged = values[m]
            for before in range(1, m % (group // STREAMS) + 1):
                lane = (before - 1) * group + m
                merged = merged + same[rows, lane : lane + 1] * values[m - before]
            back[m, rows, :] = merged.astype(back.dtype)
        return carry

    lax.fori_loop(0, refs // (2 * SUBS), inverse, 0)
    total = ebuf[...]
    for off in range(1, place.parts):
        remote(ebuf, egot.at[off], send.at[off], recv.at[off], place.device(off, 0)).wait_recv()
        total = total + egot[off]
    weights[...] = 1.0 / (0.25 + total / (group * width))
    for copy in started:
        copy.wait_send()


def shrink_scratch(parts, group, refs):
    assert parts <= SUBS
    return [
        pltpu.VMEM((group, refs, LANES), jnp.float32),
        pltpu.VMEM((refs, LANES), jnp.float32),
        pltpu.VMEM((SUBS, LANES), jnp.float32),
        pltpu.VMEM((parts, SUBS, LANES), jnp.float32),
        SEMS((parts,)),
        SEMS((parts,)),
    ]


def first_kernel(count, x_in, home_in, ids_in, sigma_in, cube_in, coeffs_out, back, weights, same, turned, *scratch):
    stage, got, table, send, recv = scratch[:5]
    members, energy, ebuf, egot, esend, erecv = scratch[5:11]
    x, cube_t, sigma, ids, insem = scratch[11:16]
    coeffs, csem, home, named, lists_v, lsend, lrecv, lsem = scratch[16:24]
    scalars = scratch[24:]
    parts = stage.shape[0]
    group, some = ids.shape
    place = Place(count, parts)
    pairs = [(x_in, x), (cube_in, cube_t), (home_in, home), (ids_in, ids), (sigma_in, sigma)]
    fetches = [pltpu.make_async_copy(src, dst, insem.at[i]) for i, (src, dst) in enumerate(pairs)]
    for fetch in fetches:
        fetch.start()
    place.greet()
    for fetch in fetches[:2]:
        fetch.wait()
    spread = Spread(place, stage, got, table, send, recv)
    spread.begin(range(PIECES), x, cube_t)

    def look_up(row, carry):
        for q in range(SUBS):
            for m in range(group):
                named[m, row * SUBS + q] = home[ids[m, row * SUBS + q]]
        return carry

    for fetch in fetches[2:]:
        fetch.wait()
    lax.fori_loop(0, some // SUBS, look_up, 0)

    def fill(m, carry):
        for q in range(some, LANES):
            named[m, q] = 0
        return carry

    lax.fori_loop(0, group, fill, 0)

    ebuf[...] = jnp.zeros(ebuf.shape, ebuf.dtype)
    mine = pltpu.make_async_copy(named, lists_v.at[place.part], lsem.at[0])
    mine.start()
    mine.wait()
    started = []
    for off in range(1, parts):
        copy = remote(
            lists_v.at[place.part],
            lists_v.at[place.part],
            lsend.at[off],
            lrecv.at[off],
            place.device(off, 0),
        )
        copy.start()
        started.append(copy)
    copies = []

    def lists_ready():
        for off in range(1, parts):
            source = lists_v.at[flip(place.part, off)]
            remote(source, source, lsend.at[off], lrecv.at[off], place.device(off, 0)).wait_recv()
        turned[...] = jnp.zeros(turned.shape, turned.dtype)
        for m in range(group):
            for src in range(parts):
                turned[m, src : src + 1, :] = lists_v[src, m : m + 1, :]
        find_equals(lists_v, same, group, some)
        copies.extend(to_scalars(turned, scalars, lsem))

    spread.finish(lists_ready)
    for copy in copies:
        copy.wait()
    pick_rows(table, scalars, members, some)
    store = pltpu.make_async_copy(coeffs, coeffs_out, csem.at[0])
    shrink_groups(
        place, False, x.shape[1], some, sigma, members, coeffs, back, same, energy, ebuf, egot, weights, esend, erecv, store.start
    )
    store.wait()
    for copy in started:
        copy.wait_send()
    spread.close()


class Collect:
    def __init__(self, place, acc, got, sent, zgot, send, recv):
        self.place, self.acc, self.got, self.sent, self.zgot = place, acc, got, sent, zgot
        self.send, self.recv, self.started = send, recv, []
        self.order = list(range(place.parts - 1, -1, -1))

    def start(self, copy):
        copy.start()
        self.started.append(copy)

    def begin(self):
        place = self.place
        for d in sorted(range(1, place.ranks, 2), key=lambda d: lowest(d - 1, place.ranks)):
            for off in self.order:
                for h in range(PIECES):
                    self.start(
                        remote(
                            piece_of(self.acc.at[place.index(off, d)], h),
                            piece_of(self.got.at[off, d], h),
                            self.send.at[off, d, h],
                            self.recv.at[off, d, h],
                            place.device(0, 1),
                        )
                    )

    def value(self, off, d, h):
        place = self.place
        total = piece_of(self.acc.at[place.index(off, d)], h)[...].astype(jnp.float32)
        for bit in place.bits:
            if bit < lowest(d, place.ranks):
                piece = piece_of(self.got.at[off, d | bit], h)
                remote(
                    piece, piece, self.send.at[off, d | bit, h], self.recv.at[off, d | bit, h], place.device(0, bit)
                ).wait_recv()
                total = total + piece[...].astype(jnp.float32)
        return total

    def run(self):
        for level in self.place.bits[1:] + [self.place.ranks]:
            self.hand_on([d for d in range(0, self.place.ranks, 2) if lowest(d, self.place.ranks) == level])

    def hand_on(self, ds):
        place = self.place
        for d, off, h in itertools.product(ds, self.order, range(PIECES)):
            piece = piece_of(self.sent.at[off, d // 2], h)
            piece[...] = self.value(off, d, h).astype(self.sent.dtype)
            if d == 0 and off == 0:
                continue
            bit = lowest(d, 0)
            self.start(
                remote(
                    piece,
                    piece_of(self.got.at[off, d] if d else self.zgot.at[off], h),
                    self.send.at[off, d, h],
                    self.recv.at[off, d, h],
                    place.device(0, bit) if d else place.device(off, 0),
                )
            )

    def slices(self, h):
        place = self.place
        yield 0, piece_of(self.sent.at[0, 0], h)[...]
        for off in range(1, place.parts):
            piece = piece_of(self.zgot.at[off], h)
            remote(
                piece, piece, self.send.at[off, 0, h], self.recv.at[off, 0, h], place.device(off, 0)
            ).wait_recv()
            yield off, piece[...]

    def close(self):
        for copy in self.started:
            copy.wait_send()


def settle(place, acc, wsum, noisy, cube, out, got, sent, zgot, wgot, send, recv, wsend, wrecv, then=None):
    held = noisy.shape[0]
    collect = Collect(place, acc, got, sent, zgot, send, recv)
    place.greet()
    collect.begin()
    for d in range(1, place.ranks):
        collect.start(
            remote(wsum.at[flip(place.rank, d)], wgot.at[d], wsend.at[d], wrecv.at[d], place.device(0, d))
        )
    collect.run()
    denom = wsum[place.rank]
    for d in range(1, place.ranks):
        remote(wgot.at[d], wgot.at[d], wsend.at[d], wrecv.at[d], place.device(0, d)).wait_recv()
        denom = denom + wgot[d]
    size = held // PIECES
    for h in range(PIECES):
        numer = prior_weight * noisy[pl.ds(h * size, size), :].astype(jnp.float32)
        for off, part in collect.slices(h):
            rows = pl.ds(pl.multiple_of(flip(place.part, off) * LANES, LANES), LANES)
            numer = numer + jnp.dot(part, cube[rows, :], preferred_element_type=jnp.float32)
        for j in range(size // LANES):
            row = h * (size // LANES) + j
            spread = jnp.broadcast_to(denom[row : row + 1, :], (LANES, LANES))
            column = jnp.sum(jnp.where(diagonal(LANES), spread, 0.0), axis=1, keepdims=True)
            out[pl.ds(row * LANES, LANES), :] = (
                numer[j * LANES : (j + 1) * LANES, :] / (column + prior_weight)
            ).astype(out.dtype)
        if then is not None:
            then(h)
    return collect


def settle_scratch(count, parts, held, dtype):
    ranks = count // parts
    half = (parts, ranks // 2, held, LANES)
    return [
        pltpu.VMEM((parts, ranks, held, LANES), dtype),
        pltpu.VMEM(half, dtype),
        pltpu.VMEM((parts, held, LANES), dtype),
        pltpu.VMEM((ranks, SUBS, LANES), jnp.float32),
        SEMS((parts, ranks, PIECES)),
        SEMS((parts, ranks, PIECES)),
        SEMS((ranks,)),
        SEMS((ranks,)),
    ]


def second_kernel(count, some, acc, wsum, noisy, cube, cube_t, sigma, turned, same, coeffs_in, basic, back, weights, *scratch):
    stage, got, table, send, recv = scratch[:5]
    members, energy, ebuf, egot, esend, erecv = scratch[5:11]
    coeffs, csem, lsem = scratch[11:14]
    group = members.shape[0]
    scalars = scratch[14 : 14 + group]
    parts = stage.shape[0]
    place = Place(count, parts)
    fetch = pltpu.make_async_copy(coeffs_in, coeffs, csem.at[0])
    fetch.start()
    copies = to_scalars(turned, scalars, lsem)
    spread = Spread(place, stage, got, table, send, recv)
    ebuf[...] = jnp.zeros(ebuf.shape, ebuf.dtype)
    collect = settle(
        place,
        acc,
        wsum,
        noisy,
        cube,
        basic,
        *scratch[14 + group :],
        then=lambda h: spread.begin([h], basic, cube_t),
    )
    spread.finish()
    for copy in copies:
        copy.wait()
    pick_rows(table, scalars, members, some)
    fetch.wait()
    shrink_groups(
        place, True, noisy.shape[1], some, sigma, members, coeffs, back, same, energy, ebuf, egot, weights, esend, erecv
    )
    collect.close()
    spread.close()


def third_kernel(count, parts, acc, wsum, noisy, cube, out, *scratch):
    settle(Place(count, parts), acc, wsum, noisy, cube, out, *scratch).close()


def add_kernel(count, some, carried, turned, weights, back, *refs):
    group, refs_here = back.shape[:2]
    parts = refs_here // some
    kept = refs[:carried]
    acc, wsum = refs[carried : carried + 2]
    outs = refs[carried + 2 : 2 * carried + 2]
    members, ksem, lsem = refs[2 * carried + 2 : 2 * carried + 5]
    scalars = refs[2 * carried + 5 : 2 * carried + 5 + group]
    sums = refs[2 * carried + 5 + group :]
    place = Place(count, parts)
    blocks, held = acc.shape[:2]
    copies = to_scalars(turned, scalars, lsem)
    moves = [pltpu.make_async_copy(src, dst, ksem.at[i]) for i, (src, dst) in enumerate(zip(kept, outs))]
    for move in moves:
        move.start()

    def clear(i, carry):
        rows = pl.ds(pl.multiple_of(i * LANES, LANES), LANES)
        for each in sums:
            each[rows, :] = jnp.zeros((LANES, LANES), jnp.float32)
        return carry

    lax.fori_loop(0, blocks * held // LANES, clear, 0)
    for src in range(parts):
        row = jnp.broadcast_to(weights[src : src + 1, :], (some, LANES))
        column = jnp.sum(jnp.where(diagonal(some), row, 0.0), axis=1, keepdims=True)
        spread = jnp.broadcast_to(column, (some, LANES))
        rows = pl.ds(src * some, some)

        def scale(m, carry):
            members[m, rows, :] = back[m, rows, :].astype(jnp.float32) * spread
            return carry

        lax.fori_loop(0, group, scale, 0)

    many = wsum.shape[0] * (held // LANES)
    lane = lax.broadcasted_iota(jnp.int32, (1, LANES), 1)
    heavy = [jnp.where(lane < some, weights[src : src + 1, :], 0.0) for src in range(parts)]
    tall = lax.broadcasted_iota(jnp.int32, (many, LANES), 0)
    low = lax.broadcasted_iota(jnp.int32, (LANES, LANES), 0)
    first = place.part * (many * LANES)

    def weigh(m, total):
        ones, loads = [], []
        for src in range(parts):
            spots = turned[m, src : src + 1, :] - first
            loads.append(jnp.where((spots >> 7) == tall, heavy[src], 0.0).astype(jnp.bfloat16))
            ones.append(jnp.where((spots & (LANES - 1)) == low, 1.0, 0.0).astype(jnp.bfloat16))
        return total + lax.dot_general(
            jnp.concatenate(loads, axis=1),
            jnp.concatenate(ones, axis=1),
            (((1,), (1,)), ((), ())),
            preferred_element_type=jnp.float32,
        )

    total = lax.fori_loop(0, group, weigh, jnp.zeros((many, LANES), jnp.float32), unroll=True)
    per = held // LANES
    for b in range(wsum.shape[0]):
        wsum[b, :per, :] = total[b * per : (b + 1) * per, :]
        if per < SUBS:
            wsum[b, per:, :] = jnp.zeros((SUBS - per, LANES), jnp.float32)

    together = group // STREAMS
    for copy in copies:
        copy.wait()

    def step(t, carry):
        src, row = t // (some // SUBS), lax.rem(t, some // SUBS)
        for q in range(SUBS):
            spots, news = [], []
            for m in range(group):
                spot = scalars[m][src, row * SUBS + q]
                spots.append(spot)
                news.append(sums[m // together][pl.ds(spot, 1), :] + members[m, pl.ds(t * SUBS + q, 1), :])
            for m in range(group):
                sums[m // together][pl.ds(spots[m], 1), :] = news[m]
        return carry

    lax.fori_loop(0, refs_here // SUBS, step, 0)

    def store(b, carry):
        for i in range(held // LANES):
            rows = pl.ds(pl.multiple_of(b * held + i * LANES, LANES), LANES)
            whole = sums[0][rows, :]
            for each in sums[1:]:
                whole = whole + each[rows, :]
            acc[b, i * LANES : (i + 1) * LANES, :] = whole.astype(acc.dtype)
        return carry

    lax.fori_loop(0, blocks, store, 0)
    for move in moves:
        move.wait()


def shape(*dims, dtype=jnp.float32):
    return jax.ShapeDtypeStruct(dims, dtype)


def params(rows, collective_id=None):
    limit = 5 * rows * LANES * 4 + (10 << 20)
    return pltpu.CompilerParams(
        collective_id=collective_id, has_side_effects=collective_id is not None, vmem_limit_bytes=limit
    )


def add_up(count, some, held, turned, weights, back, *kept):
    group, refs = back.shape[:2]
    ranks = count // (refs // some)
    return pl.pallas_call(
        functools.partial(add_kernel, count, some, len(kept)),
        out_shape=[shape(count, held, LANES, dtype=back.dtype), shape(ranks, SUBS, LANES)]
        + [shape(*each.shape, dtype=each.dtype) for each in kept],
        in_specs=[VMEM] * (3 + len(kept)),
        out_specs=[VMEM, VMEM] + [HBM] * len(kept),
        scratch_shapes=[pltpu.VMEM((group, refs, LANES), jnp.float32), SEMS((1,)), SEMS((group,))]
        + [pltpu.SMEM((SUBS, LANES), jnp.int32)] * group
        + [pltpu.VMEM((count * held, LANES), jnp.float32)] * STREAMS,
        compiler_params=params(count * held),
        name="add_up",
    )(turned, weights, back, *kept)


def body(noisy, matches, cube_home, sigma_coef):
    count = lax.axis_size("space")
    some, group = matches.shape
    held, width = noisy.shape
    parts = width // LANES
    refs = parts * some
    cube, cube_t = cube_tables()
    sigma = sigma_coef[None, :]
    dtype = noisy.dtype
    shared = spread_scratch(count, parts, held, dtype) + shrink_scratch(parts, group, refs)
    coeffs, back, weights, same, turned = pl.pallas_call(
        functools.partial(first_kernel, count),
        out_shape=[
            shape(group, refs, LANES),
            shape(group, refs, LANES, dtype=dtype),
            shape(SUBS, LANES),
            shape(refs, LANES),
            shape(group, SUBS, LANES, dtype=jnp.int32),
        ],
        in_specs=[HBM] * 5,
        out_specs=[HBM] + [VMEM] * 4,
        scratch_shapes=shared
        + [
            pltpu.VMEM(noisy.shape, dtype),
            pltpu.VMEM(cube_t.shape, dtype),
            pltpu.VMEM(sigma.shape, jnp.float32),
            pltpu.SMEM((group, some), jnp.int32),
            SEMS((5,)),
            pltpu.VMEM((group, refs, LANES), jnp.float32),
            SEMS((1,)),
            pltpu.SMEM(cube_home.shape, jnp.int32),
            pltpu.SMEM((group, LANES), jnp.int32),
            pltpu.VMEM((parts, group, LANES), jnp.int32),
            SEMS((parts,)),
            SEMS((parts,)),
            SEMS((group,)),
        ]
        + [pltpu.SMEM((SUBS, LANES), jnp.int32)] * group,
        compiler_params=params(count * held, 0),
        name="shrink",
    )(*[pltpu.with_memory_space_constraint(v, pltpu.HBM) for v in (noisy, cube_home, matches.T, sigma, jnp.asarray(cube_t))])
    acc, wsum = add_up(count, some, held, turned, weights, back)
    basic, back, weights = pl.pallas_call(
        functools.partial(second_kernel, count, some),
        out_shape=[
            shape(held, width, dtype=dtype),
            shape(group, refs, LANES, dtype=dtype),
            shape(SUBS, LANES),
        ],
        in_specs=[VMEM] * 8 + [HBM],
        out_specs=[VMEM] * 3,
        scratch_shapes=shared
        + [pltpu.VMEM((group, refs, LANES), jnp.float32), SEMS((1,)), SEMS((group,))]
        + [pltpu.SMEM((SUBS, LANES), jnp.int32)] * group
        + settle_scratch(count, parts, held, dtype),
        compiler_params=params(count * held, 1),
        name="wiener",
    )(acc, wsum, noisy, cube, cube_t, sigma, turned, same, coeffs)
    acc, wsum, basic = add_up(count, some, held, turned, weights, back, basic)
    final = pl.pallas_call(
        functools.partial(third_kernel, count, parts),
        out_shape=shape(held, width, dtype=dtype),
        in_specs=[VMEM] * 4,
        out_specs=VMEM,
        scratch_shapes=settle_scratch(count, parts, held, dtype),
        compiler_params=params(count * held, 2),
        name="settle",
    )(acc, wsum, noisy, cube)
    return basic, final


def solution(mesh):
    in_specs = (P(("groups", "space"), None), P(("groups", "space"), None), P("groups"), P())
    out_specs = (P(("groups", "space"), None), P(("groups", "space"), None))
    return jax.shard_map(body, mesh=mesh, in_specs=in_specs, out_specs=out_specs, check_vma=False)
```

```python
import functools
import itertools

import jax
import jax.numpy as jnp
import numpy as np
from jax import lax
from jax.experimental import pallas as pl
from jax.experimental.pallas import tpu as pltpu
from jax.sharding import PartitionSpec as P

shrink_level = 2.7
prior_weight = 0.5
LANES = 128
SUBS = 8
PIECES = 2
STREAMS = 4
MESH = pl.DeviceIdType.MESH
VMEM = pl.BlockSpec(memory_space=pltpu.VMEM)
SMEM = pl.BlockSpec(memory_space=pltpu.SMEM)
HBM = pl.BlockSpec(memory_space=pltpu.HBM)
SEMS = pltpu.SemaphoreType.DMA


def dct_matrix(length):
    index = np.arange(length, dtype=np.float64)
    table = np.cos(np.pi * (2.0 * index[None, :] + 1.0) * index[:, None] / (2.0 * length))
    table = table * np.sqrt(2.0 / length)
    table[0] /= np.sqrt(2.0)
    return table


def cube_tables():
    small = dct_matrix(8)
    cube = np.kron(np.kron(small, small), small).astype(np.float32)
    return cube.astype(jnp.bfloat16), cube.T.astype(jnp.bfloat16)


def half_cosines(n):
    return [float(2.0 * np.cos(np.pi * (2 * i + 1) / (2 * n))) for i in range(n // 2)]


def cosine_sums(x):
    n = len(x)
    if n == 2:
        return [x[0] + x[1], (x[0] - x[1]) * float(np.cos(np.pi / 4))]
    half = n // 2
    even = cosine_sums([x[i] + x[n - 1 - i] for i in range(half)])
    turned = cosine_sums([(x[i] - x[n - 1 - i]) * f for i, f in enumerate(half_cosines(n))])
    out = [None] * n
    for k in range(half):
        out[2 * k] = even[k]
        out[2 * k + 1] = turned[k] - out[2 * k - 1] if k else 0.5 * turned[0]
    return out


def cosine_sums_transposed(y):
    n = len(y)
    if n == 2:
        odd = y[1] * float(np.cos(np.pi / 4))
        return [y[0] + odd, y[0] - odd]
    half = n // 2
    even = cosine_sums_transposed(y[0::2])
    tail = [None] * half
    for k in reversed(range(half)):
        tail[k] = y[2 * k + 1] - tail[k + 1] if k + 1 < half else y[2 * k + 1]
    tail[0] = 0.5 * tail[0]
    odd = [o * f for o, f in zip(cosine_sums_transposed(tail), half_cosines(n))]
    return [even[i] + odd[i] for i in range(half)] + [even[i] - odd[i] for i in reversed(range(half))]


def scales(n):
    return [float(np.sqrt((1.0 if k == 0 else 2.0) / n)) for k in range(n)]


def flip(value, mask):
    if isinstance(mask, int):
        for bit in (1 << b for b in range(mask.bit_length())):
            if mask & bit:
                value = value + bit - 2 * bit * lax.rem(value // bit, 2)
        return value
    for bit in (1, 2):
        value = value + bit * lax.rem(mask // bit, 2) * (1 - 2 * lax.rem(value // bit, 2))
    return value


def lowest(d, count):
    return d & -d if d else count


class Place:
    def __init__(self, count, parts):
        self.parts, self.ranks = parts, count // parts
        me = lax.axis_index("space")
        self.part, self.rank = me // self.ranks, lax.rem(me, self.ranks)
        self.bits = [1 << b for b in range(self.ranks.bit_length() - 1)]

    def index(self, off, d):
        return flip(self.part, off) * self.ranks + flip(self.rank, d)

    def device(self, off, d):
        return {"space": self.index(off, d)}

    def peers(self):
        return [(off, 0) for off in range(1, self.parts)] + [(0, d) for d in range(1, self.ranks)]

    def greet(self):
        barrier = pltpu.get_barrier_semaphore()
        for off, d in self.peers():
            pl.semaphore_signal(barrier, inc=1, device_id=self.device(off, d), device_id_type=MESH)

    def meet(self):
        pl.semaphore_wait(pltpu.get_barrier_semaphore(), len(self.peers()))


def remote(src, dst, send, recv, device):
    return pltpu.make_async_remote_copy(
        src_ref=src, dst_ref=dst, send_sem=send, recv_sem=recv, device_id=device, device_id_type=MESH
    )


def piece_of(ref, h):
    size = ref.shape[0] // PIECES
    return ref.at[pl.ds(h * size, size), :]


class Spread:
    def __init__(self, place, stage, got, table, send, recv):
        self.place, self.stage, self.got, self.table = place, stage, got, table
        self.send, self.recv, self.started = send, recv, []

    def block(self, off, d):
        return self.stage.at[0] if off == 0 and d == 0 else self.got.at[off, d]

    def pass_on(self, off, d, h):
        place = self.place
        for bit in reversed(place.bits):
            if bit < lowest(d, place.ranks):
                copy = remote(
                    piece_of(self.block(off, d), h),
                    piece_of(self.got.at[off, d | bit], h),
                    self.send.at[off, d | bit, h],
                    self.recv.at[off, d | bit, h],
                    place.device(0, bit),
                )
                copy.start()
                self.started.append(copy)

    def orders(self, hs):
        return itertools.product(list(range(1, self.place.parts)) + [0], hs)

    def transform(self, hs, rows, cube_t):
        size = rows.shape[0] // PIECES
        for off, h in self.orders(hs):
            columns = pl.ds(pl.multiple_of(flip(self.place.part, off) * LANES, LANES), LANES)
            part = rows[h * size : (h + 1) * size, :]
            spec = jnp.dot(part, cube_t[:, columns], preferred_element_type=jnp.float32)
            piece_of(self.stage.at[off], h)[...] = spec.astype(self.stage.dtype)

    def begin(self, hs):
        for off, h in self.orders(hs):
            if off == 0:
                self.pass_on(0, 0, h)
                continue
            copy = remote(
                piece_of(self.stage.at[off], h),
                piece_of(self.got.at[off, 0], h),
                self.send.at[off, 0, h],
                self.recv.at[off, 0, h],
                self.place.device(off, 0),
            )
            copy.start()
            self.started.append(copy)

    def widen(self, off, d, h):
        source = piece_of(self.block(off, d), h)
        held = self.stage.shape[1]
        size = held // PIECES
        first = self.place.index(off, d) * held + h * size
        rows = pl.ds(pl.multiple_of(first, size), size)
        self.table[rows, :] = source[...].astype(jnp.float32)

    def finish(self, then=None):
        place = self.place

        def when(key):
            off, d, h = key
            return off + 0.5 * h + sum(2.2 if b == 1 else 1.6 for b in place.bits if d & b)

        keys = [
            (off, d, h)
            for off in range(place.parts)
            for d in range(place.ranks)
            for h in range(PIECES)
            if off or d
        ]
        for h in range(PIECES):
            self.widen(0, 0, h)
        for off, d, h in sorted(keys, key=when):
            piece = piece_of(self.got.at[off, d], h)
            remote(
                piece, piece, self.send.at[off, d, h], self.recv.at[off, d, h], place.device(off, d)
            ).wait_recv()
            self.pass_on(off, d, h)
            self.widen(off, d, h)
            if then is not None and (off, d, h) == (place.parts - 1, 0, PIECES - 1):
                then()

    def close(self):
        for copy in self.started:
            copy.wait_send()


def spread_scratch(count, parts, held, dtype):
    ranks = count // parts
    return [
        pltpu.VMEM((parts, held, LANES), dtype),
        pltpu.VMEM((parts, ranks, held, LANES), dtype),
        pltpu.VMEM((count * held, LANES), jnp.float32),
        SEMS((parts, ranks, PIECES)),
        SEMS((parts, ranks, PIECES)),
    ]


def pick_rows(table, lists, members, some):
    group = members.shape[0]

    def step(t, carry):
        src, row = t // (some // SUBS), lax.rem(t, some // SUBS)
        for q in range(SUBS):
            for m in range(group):
                spot = lists[m][src, row * SUBS + q]
                members[m, pl.ds(t * SUBS + q, 1), :] = table[pl.ds(spot, 1), :]
        return carry

    lax.fori_loop(0, members.shape[1] // SUBS, step, 0)


def to_scalars(lists, scalars, sem):
    copies = [pltpu.make_async_copy(lists.at[m], each, sem.at[m]) for m, each in enumerate(scalars)]
    for copy in copies:
        copy.start()
    return copies


def find_equals(lists, same, group, some):
    for src in range(lists.shape[0]):
        rows = lists[src]
        equal = [jnp.where(rows == pltpu.roll(rows, back, 0), 1.0, 0.0) for back in range(1, group // STREAMS)]
        equal.append(jnp.zeros((LANES - group * len(equal), LANES), jnp.float32))
        same[src * some : (src + 1) * some, :] = jnp.concatenate(equal, axis=0).T[:some, :]


def diagonal(rows):
    shape = (rows, LANES)
    return lax.broadcasted_iota(jnp.int32, shape, 0) == lax.broadcasted_iota(jnp.int32, shape, 1)


def shrink_groups(place, second, width, some, sigma, members, coeffs, back, same, energy, ebuf, egot, weights, send, recv, then=None):
    group, refs = members.shape[:2]
    factor = scales(group)
    columns = pl.ds(pl.multiple_of(place.part * LANES, LANES), LANES)
    own = sigma[:, columns]
    level = own * own if second else (shrink_level * own) * (shrink_level * own)

    def forward(b, carry):
        rows = pl.ds(pl.multiple_of(b * SUBS, SUBS), SUBS)
        values = cosine_sums([members[m, rows, :] for m in range(group)])
        total = None
        for j in range(group):
            value = values[j] * factor[j]
            square = value * value
            gain = square / (square + level)
            power = gain * gain
            total = power if total is None else total + power
            if second:
                members[j, rows, :] = gain * coeffs[j, rows, :]
            else:
                coeffs[j, rows, :] = value
                members[j, rows, :] = gain * value
        energy[rows, :] = total * level if second else total
        return carry

    lax.fori_loop(0, refs // SUBS, forward, 0)
    if then is not None:
        then()
    parts = refs // some
    for src in range(parts):
        column = jnp.sum(energy[src * some : (src + 1) * some, :], axis=1, keepdims=True)
        ebuf[src : src + 1, :] = jnp.sum(jnp.where(diagonal(some), column, 0.0), axis=0, keepdims=True)
    started = []
    for off in range(1, place.parts):
        copy = remote(ebuf, egot.at[off], send.at[off], recv.at[off], place.device(off, 0))
        copy.start()
        started.append(copy)

    def inverse(b, carry):
        rows = pl.ds(pl.multiple_of(b * SUBS, SUBS), SUBS)
        values = cosine_sums_transposed([members[j, rows, :] * factor[j] for j in range(group)])
        for m in range(group):
            merged = values[m]
            for before in range(1, m % (group // STREAMS) + 1):
                lane = (before - 1) * group + m
                merged = merged + same[rows, lane : lane + 1] * values[m - before]
            back[m, rows, :] = merged.astype(back.dtype)
        return carry

    lax.fori_loop(0, refs // SUBS, inverse, 0)
    total = ebuf[...]
    for off in range(1, place.parts):
        remote(ebuf, egot.at[off], send.at[off], recv.at[off], place.device(off, 0)).wait_recv()
        total = total + egot[off]
    weights[...] = 1.0 / (0.25 + total / (group * width))
    for copy in started:
        copy.wait_send()


def shrink_scratch(parts, group, refs):
    assert parts <= SUBS
    return [
        pltpu.VMEM((group, refs, LANES), jnp.float32),
        pltpu.VMEM((refs, LANES), jnp.float32),
        pltpu.VMEM((SUBS, LANES), jnp.float32),
        pltpu.VMEM((parts, SUBS, LANES), jnp.float32),
        SEMS((parts,)),
        SEMS((parts,)),
    ]


def first_kernel(count, x_in, home_in, ids_in, sigma_in, cube_in, coeffs_out, back, weights, same, turned, *scratch):
    stage, got, table, send, recv = scratch[:5]
    members, energy, ebuf, egot, esend, erecv = scratch[5:11]
    x, cube_t, sigma, ids, insem = scratch[11:16]
    coeffs, csem, home, named, lists_v, lsend, lrecv, lsem = scratch[16:24]
    scalars = scratch[24:]
    parts = stage.shape[0]
    group, some = ids.shape
    place = Place(count, parts)
    pairs = [(x_in, x), (cube_in, cube_t), (home_in, home), (ids_in, ids), (sigma_in, sigma)]
    fetches = [pltpu.make_async_copy(src, dst, insem.at[i]) for i, (src, dst) in enumerate(pairs)]
    for fetch in fetches:
        fetch.start()
    place.greet()
    for fetch in fetches[:2]:
        fetch.wait()
    spread = Spread(place, stage, got, table, send, recv)
    spread.transform(range(PIECES), x, cube_t)
    place.meet()
    spread.begin(range(PIECES))

    def look_up(row, carry):
        for q in range(SUBS):
            for m in range(group):
                named[m, row * SUBS + q] = home[ids[m, row * SUBS + q]]
        return carry

    for fetch in fetches[2:]:
        fetch.wait()
    lax.fori_loop(0, some // SUBS, look_up, 0)

    def fill(m, carry):
        for q in range(some, LANES):
            named[m, q] = 0
        return carry

    lax.fori_loop(0, group, fill, 0)

    ebuf[...] = jnp.zeros(ebuf.shape, ebuf.dtype)
    mine = pltpu.make_async_copy(named, lists_v.at[place.part], lsem.at[0])
    mine.start()
    mine.wait()
    started = []
    for off in range(1, parts):
        copy = remote(
            lists_v.at[place.part],
            lists_v.at[place.part],
            lsend.at[off],
            lrecv.at[off],
            place.device(off, 0),
        )
        copy.start()
        started.append(copy)
    copies = []

    def lists_ready():
        for off in range(1, parts):
            source = lists_v.at[flip(place.part, off)]
            remote(source, source, lsend.at[off], lrecv.at[off], place.device(off, 0)).wait_recv()
        turned[...] = jnp.zeros(turned.shape, turned.dtype)
        for m in range(group):
            for src in range(parts):
                turned[m, src : src + 1, :] = lists_v[src, m : m + 1, :]
        find_equals(lists_v, same, group, some)
        copies.extend(to_scalars(turned, scalars, lsem))

    spread.finish(lists_ready)
    for copy in copies:
        copy.wait()
    pick_rows(table, scalars, members, some)
    store = pltpu.make_async_copy(coeffs, coeffs_out, csem.at[0])
    shrink_groups(
        place, False, x.shape[1], some, sigma, members, coeffs, back, same, energy, ebuf, egot, weights, esend, erecv, store.start
    )
    store.wait()
    for copy in started:
        copy.wait_send()
    spread.close()


class Collect:
    def __init__(self, place, acc, got, sent, zgot, send, recv):
        self.place, self.acc, self.got, self.sent, self.zgot = place, acc, got, sent, zgot
        self.send, self.recv, self.started = send, recv, []
        self.order = list(range(place.parts - 1, -1, -1))

    def start(self, copy):
        copy.start()
        self.started.append(copy)

    def begin(self):
        place = self.place
        for d in sorted(range(1, place.ranks, 2), key=lambda d: lowest(d - 1, place.ranks)):
            for off in self.order:
                for h in range(PIECES):
                    self.start(
                        remote(
                            piece_of(self.acc.at[place.index(off, d)], h),
                            piece_of(self.got.at[off, d], h),
                            self.send.at[off, d, h],
                            self.recv.at[off, d, h],
                            place.device(0, 1),
                        )
                    )

    def value(self, off, d, h):
        place = self.place
        total = piece_of(self.acc.at[place.index(off, d)], h)[...].astype(jnp.float32)
        for bit in place.bits:
            if bit < lowest(d, place.ranks):
                piece = piece_of(self.got.at[off, d | bit], h)
                remote(
                    piece, piece, self.send.at[off, d | bit, h], self.recv.at[off, d | bit, h], place.device(0, bit)
                ).wait_recv()
                total = total + piece[...].astype(jnp.float32)
        return total

    def run(self):
        for level in self.place.bits[1:] + [self.place.ranks]:
            self.hand_on([d for d in range(0, self.place.ranks, 2) if lowest(d, self.place.ranks) == level])

    def hand_on(self, ds):
        place = self.place
        for d, off, h in itertools.product(ds, self.order, range(PIECES)):
            piece = piece_of(self.sent.at[off, d // 2], h)
            piece[...] = self.value(off, d, h).astype(self.sent.dtype)
            if d == 0 and off == 0:
                continue
            bit = lowest(d, 0)
            self.start(
                remote(
                    piece,
                    piece_of(self.got.at[off, d] if d else self.zgot.at[off], h),
                    self.send.at[off, d, h],
                    self.recv.at[off, d, h],
                    place.device(0, bit) if d else place.device(off, 0),
                )
            )

    def slices(self, h):
        place = self.place
        yield 0, piece_of(self.sent.at[0, 0], h)[...]
        for off in range(1, place.parts):
            piece = piece_of(self.zgot.at[off], h)
            remote(
                piece, piece, self.send.at[off, 0, h], self.recv.at[off, 0, h], place.device(off, 0)
            ).wait_recv()
            yield off, piece[...]

    def close(self):
        for copy in self.started:
            copy.wait_send()


def weigh_rows(place, some, held, turned, weights, wsum):
    parts = place.parts
    group = turned.shape[0]
    many = wsum.shape[0] * (held // LANES)
    lane = lax.broadcasted_iota(jnp.int32, (1, LANES), 1)
    heavy = [jnp.where(lane < some, weights[src : src + 1, :], 0.0) for src in range(parts)]
    tall = lax.broadcasted_iota(jnp.int32, (many, LANES), 0)
    low = lax.broadcasted_iota(jnp.int32, (LANES, LANES), 0)
    first = place.part * (many * LANES)

    def weigh(m, total):
        ones, loads = [], []
        for src in range(parts):
            spots = turned[m, src : src + 1, :] - first
            loads.append(jnp.where((spots >> 7) == tall, heavy[src], 0.0).astype(jnp.bfloat16))
            ones.append(jnp.where((spots & (LANES - 1)) == low, 1.0, 0.0).astype(jnp.bfloat16))
        return total + lax.dot_general(
            jnp.concatenate(loads, axis=1),
            jnp.concatenate(ones, axis=1),
            (((1,), (1,)), ((), ())),
            preferred_element_type=jnp.float32,
        )

    total = lax.fori_loop(0, group, weigh, jnp.zeros((many, LANES), jnp.float32), unroll=True)
    per = held // LANES
    for b in range(wsum.shape[0]):
        wsum[b, :per, :] = total[b * per : (b + 1) * per, :]
        if per < SUBS:
            wsum[b, per:, :] = jnp.zeros((SUBS - per, LANES), jnp.float32)


def settle(place, some, turned, weights, acc, noisy, cube, out, wsum, got, sent, zgot, wgot, send, recv, wsend, wrecv, then=None):
    held = noisy.shape[0]
    collect = Collect(place, acc, got, sent, zgot, send, recv)
    place.greet()
    weigh_rows(place, some, held, turned, weights, wsum)
    place.meet()
    collect.begin()
    for d in range(1, place.ranks):
        collect.start(
            remote(wsum.at[flip(place.rank, d)], wgot.at[d], wsend.at[d], wrecv.at[d], place.device(0, d))
        )
    collect.run()
    denom = wsum[place.rank]
    for d in range(1, place.ranks):
        remote(wgot.at[d], wgot.at[d], wsend.at[d], wrecv.at[d], place.device(0, d)).wait_recv()
        denom = denom + wgot[d]
    size = held // PIECES
    for h in range(PIECES):
        numer = prior_weight * noisy[pl.ds(h * size, size), :].astype(jnp.float32)
        for off, part in collect.slices(h):
            rows = pl.ds(pl.multiple_of(flip(place.part, off) * LANES, LANES), LANES)
            numer = numer + jnp.dot(part, cube[rows, :], preferred_element_type=jnp.float32)
        for j in range(size // LANES):
            row = h * (size // LANES) + j
            spread = jnp.broadcast_to(denom[row : row + 1, :], (LANES, LANES))
            column = jnp.sum(jnp.where(diagonal(LANES), spread, 0.0), axis=1, keepdims=True)
            out[pl.ds(row * LANES, LANES), :] = (
                numer[j * LANES : (j + 1) * LANES, :] / (column + prior_weight)
            ).astype(out.dtype)
        if then is not None:
            then(h)
    return collect


def settle_scratch(count, parts, held, dtype):
    ranks = count // parts
    half = (parts, ranks // 2, held, LANES)
    return [
        pltpu.VMEM((ranks, SUBS, LANES), jnp.float32),
        pltpu.VMEM((parts, ranks, held, LANES), dtype),
        pltpu.VMEM(half, dtype),
        pltpu.VMEM((parts, held, LANES), dtype),
        pltpu.VMEM((ranks, SUBS, LANES), jnp.float32),
        SEMS((parts, ranks, PIECES)),
        SEMS((parts, ranks, PIECES)),
        SEMS((ranks,)),
        SEMS((ranks,)),
    ]


def second_kernel(count, some, acc, weights_in, noisy, cube, cube_t, sigma, turned, same, coeffs_in, basic, back, weights, *scratch):
    stage, got, table, send, recv = scratch[:5]
    members, energy, ebuf, egot, esend, erecv = scratch[5:11]
    coeffs, csem, lsem = scratch[11:14]
    group = members.shape[0]
    scalars = scratch[14 : 14 + group]
    parts = stage.shape[0]
    place = Place(count, parts)
    fetch = pltpu.make_async_copy(coeffs_in, coeffs, csem.at[0])
    fetch.start()
    copies = to_scalars(turned, scalars, lsem)
    spread = Spread(place, stage, got, table, send, recv)
    ebuf[...] = jnp.zeros(ebuf.shape, ebuf.dtype)
    def spread_piece(h):
        spread.transform([h], basic, cube_t)
        spread.begin([h])

    collect = settle(
        place,
        some,
        turned,
        weights_in,
        acc,
        noisy,
        cube,
        basic,
        *scratch[14 + group :],
        then=spread_piece,
    )
    spread.finish()
    for copy in copies:
        copy.wait()
    pick_rows(table, scalars, members, some)
    fetch.wait()
    shrink_groups(
        place, True, noisy.shape[1], some, sigma, members, coeffs, back, same, energy, ebuf, egot, weights, esend, erecv
    )
    collect.close()
    spread.close()


def third_kernel(count, parts, some, acc, weights, noisy, cube, turned, out, *scratch):
    settle(Place(count, parts), some, turned, weights, acc, noisy, cube, out, *scratch).close()


def add_kernel(some, carried, turned, weights, back, *refs):
    group, refs_here = back.shape[:2]
    parts = refs_here // some
    kept = refs[:carried]
    acc = refs[carried]
    outs = refs[carried + 1 : 2 * carried + 1]
    heavy, ksem, lsem = refs[2 * carried + 1 : 2 * carried + 4]
    scalars = refs[2 * carried + 4 : 2 * carried + 4 + group]
    sums = refs[2 * carried + 4 + group :]
    blocks, held = acc.shape[:2]
    copies = to_scalars(turned, scalars, lsem)
    moves = [pltpu.make_async_copy(src, dst, ksem.at[i]) for i, (src, dst) in enumerate(zip(kept, outs))]
    for move in moves:
        move.start()

    def clear(i, carry):
        rows = pl.ds(pl.multiple_of(i * LANES, LANES), LANES)
        for each in sums:
            each[rows, :] = jnp.zeros((LANES, LANES), jnp.float32)
        return carry

    lax.fori_loop(0, blocks * held // LANES, clear, 0)
    for src in range(parts):
        row = jnp.broadcast_to(weights[src : src + 1, :], (some, LANES))
        column = jnp.sum(jnp.where(diagonal(some), row, 0.0), axis=1, keepdims=True)
        heavy[src * some : (src + 1) * some, :] = jnp.broadcast_to(column, (some, LANES))
    together = group // STREAMS
    for copy in copies:
        copy.wait()

    def step(t, carry):
        src, row = t // (some // SUBS), lax.rem(t, some // SUBS)
        for q in range(SUBS):
            spots, news = [], []
            weight = heavy[pl.ds(t * SUBS + q, 1), :]
            for m in range(group):
                spot = scalars[m][src, row * SUBS + q]
                spots.append(spot)
                each = weight * back[m, pl.ds(t * SUBS + q, 1), :]
                news.append(sums[m // together][pl.ds(spot, 1), :] + each)
            for m in range(group):
                sums[m // together][pl.ds(spots[m], 1), :] = news[m]
        return carry

    lax.fori_loop(0, refs_here // SUBS, step, 0)

    def store(b, carry):
        for i in range(held // LANES):
            rows = pl.ds(pl.multiple_of(b * held + i * LANES, LANES), LANES)
            whole = sums[0][rows, :]
            for each in sums[1:]:
                whole = whole + each[rows, :]
            acc[b, i * LANES : (i + 1) * LANES, :] = whole.astype(acc.dtype)
        return carry

    lax.fori_loop(0, blocks, store, 0)
    for move in moves:
        move.wait()


def shape(*dims, dtype=jnp.float32):
    return jax.ShapeDtypeStruct(dims, dtype)


def params(rows, collective_id=None):
    limit = 5 * rows * LANES * 4 + (10 << 20)
    return pltpu.CompilerParams(
        collective_id=collective_id, has_side_effects=collective_id is not None, vmem_limit_bytes=limit
    )


def add_up(count, some, held, dtype, turned, weights, back, *kept):
    group, refs = back.shape[:2]
    return pl.pallas_call(
        functools.partial(add_kernel, some, len(kept)),
        out_shape=[shape(count, held, LANES, dtype=dtype)]
        + [shape(*each.shape, dtype=each.dtype) for each in kept],
        in_specs=[VMEM] * (3 + len(kept)),
        out_specs=[VMEM] + [HBM] * len(kept),
        scratch_shapes=[pltpu.VMEM((refs, LANES), jnp.float32), SEMS((1,)), SEMS((group,))]
        + [pltpu.SMEM((SUBS, LANES), jnp.int32)] * group
        + [pltpu.VMEM((count * held, LANES), jnp.float32)] * STREAMS,
        compiler_params=params(count * held),
        name="add_up",
    )(turned, weights, back, *kept)


def body(noisy, matches, cube_home, sigma_coef):
    count = lax.axis_size("space")
    some, group = matches.shape
    held, width = noisy.shape
    parts = width // LANES
    refs = parts * some
    cube, cube_t = cube_tables()
    sigma = sigma_coef[None, :]
    dtype = noisy.dtype
    shared = spread_scratch(count, parts, held, dtype) + shrink_scratch(parts, group, refs)
    coeffs, back, weights, same, turned = pl.pallas_call(
        functools.partial(first_kernel, count),
        out_shape=[
            shape(group, refs, LANES),
            shape(group, refs, LANES),
            shape(SUBS, LANES),
            shape(refs, LANES),
            shape(group, SUBS, LANES, dtype=jnp.int32),
        ],
        in_specs=[HBM] * 5,
        out_specs=[HBM] + [VMEM] * 4,
        scratch_shapes=shared
        + [
            pltpu.VMEM(noisy.shape, dtype),
            pltpu.VMEM(cube_t.shape, dtype),
            pltpu.VMEM(sigma.shape, jnp.float32),
            pltpu.SMEM((group, some), jnp.int32),
            SEMS((5,)),
            pltpu.VMEM((group, refs, LANES), jnp.float32),
            SEMS((1,)),
            pltpu.SMEM(cube_home.shape, jnp.int32),
            pltpu.SMEM((group, LANES), jnp.int32),
            pltpu.VMEM((parts, group, LANES), jnp.int32),
            SEMS((parts,)),
            SEMS((parts,)),
            SEMS((group,)),
        ]
        + [pltpu.SMEM((SUBS, LANES), jnp.int32)] * group,
        compiler_params=params(count * held, 0),
        name="shrink",
    )(*[pltpu.with_memory_space_constraint(v, pltpu.HBM) for v in (noisy, cube_home, matches.T, sigma, jnp.asarray(cube_t))])
    (acc,) = add_up(count, some, held, dtype, turned, weights, back)
    basic, back, weights = pl.pallas_call(
        functools.partial(second_kernel, count, some),
        out_shape=[
            shape(held, width, dtype=dtype),
            shape(group, refs, LANES),
            shape(SUBS, LANES),
        ],
        in_specs=[VMEM] * 8 + [HBM],
        out_specs=[VMEM] * 3,
        scratch_shapes=shared
        + [pltpu.VMEM((group, refs, LANES), jnp.float32), SEMS((1,)), SEMS((group,))]
        + [pltpu.SMEM((SUBS, LANES), jnp.int32)] * group
        + settle_scratch(count, parts, held, dtype),
        compiler_params=params(count * held, 1),
        name="wiener",
    )(acc, weights, noisy, cube, cube_t, sigma, turned, same, coeffs)
    acc, basic = add_up(count, some, held, dtype, turned, weights, back, basic)
    final = pl.pallas_call(
        functools.partial(third_kernel, count, parts, some),
        out_shape=shape(held, width, dtype=dtype),
        in_specs=[VMEM] * 5,
        out_specs=VMEM,
        scratch_shapes=settle_scratch(count, parts, held, dtype),
        compiler_params=params(count * held, 2),
        name="settle",
    )(acc, weights, noisy, cube, turned)
    return basic, final


def solution(mesh):
    in_specs = (P(("groups", "space"), None), P(("groups", "space"), None), P("groups"), P())
    out_specs = (P(("groups", "space"), None), P(("groups", "space"), None))
    return jax.shard_map(body, mesh=mesh, in_specs=in_specs, out_specs=out_specs, check_vma=False)
```

```python
import functools
import itertools

import jax
import jax.numpy as jnp
import numpy as np
from jax import lax
from jax.experimental import pallas as pl
from jax.experimental.pallas import tpu as pltpu
from jax.sharding import PartitionSpec as P

shrink_level = 2.7
prior_weight = 0.5
LANES = 128
SUBS = 8
PIECES = 2
STREAMS = 4
MESH = pl.DeviceIdType.MESH
VMEM = pl.BlockSpec(memory_space=pltpu.VMEM)
SMEM = pl.BlockSpec(memory_space=pltpu.SMEM)
HBM = pl.BlockSpec(memory_space=pltpu.HBM)
SEMS = pltpu.SemaphoreType.DMA


def dct_matrix(length):
    index = np.arange(length, dtype=np.float64)
    table = np.cos(np.pi * (2.0 * index[None, :] + 1.0) * index[:, None] / (2.0 * length))
    table = table * np.sqrt(2.0 / length)
    table[0] /= np.sqrt(2.0)
    return table


def cube_tables():
    small = dct_matrix(8)
    cube = np.kron(np.kron(small, small), small).astype(np.float32)
    return cube.astype(jnp.bfloat16), cube.T.astype(jnp.bfloat16)


def half_cosines(n):
    return [float(2.0 * np.cos(np.pi * (2 * i + 1) / (2 * n))) for i in range(n // 2)]


def cosine_sums(x):
    n = len(x)
    if n == 2:
        return [x[0] + x[1], (x[0] - x[1]) * float(np.cos(np.pi / 4))]
    half = n // 2
    even = cosine_sums([x[i] + x[n - 1 - i] for i in range(half)])
    turned = cosine_sums([(x[i] - x[n - 1 - i]) * f for i, f in enumerate(half_cosines(n))])
    out = [None] * n
    for k in range(half):
        out[2 * k] = even[k]
        out[2 * k + 1] = turned[k] - out[2 * k - 1] if k else 0.5 * turned[0]
    return out


def cosine_sums_transposed(y):
    n = len(y)
    if n == 2:
        odd = y[1] * float(np.cos(np.pi / 4))
        return [y[0] + odd, y[0] - odd]
    half = n // 2
    even = cosine_sums_transposed(y[0::2])
    tail = [None] * half
    for k in reversed(range(half)):
        tail[k] = y[2 * k + 1] - tail[k + 1] if k + 1 < half else y[2 * k + 1]
    tail[0] = 0.5 * tail[0]
    odd = [o * f for o, f in zip(cosine_sums_transposed(tail), half_cosines(n))]
    return [even[i] + odd[i] for i in range(half)] + [even[i] - odd[i] for i in reversed(range(half))]


def scales(n):
    return [float(np.sqrt((1.0 if k == 0 else 2.0) / n)) for k in range(n)]


def flip(value, mask):
    if isinstance(mask, int):
        for bit in (1 << b for b in range(mask.bit_length())):
            if mask & bit:
                value = value + bit - 2 * bit * lax.rem(value // bit, 2)
        return value
    for bit in (1, 2):
        value = value + bit * lax.rem(mask // bit, 2) * (1 - 2 * lax.rem(value // bit, 2))
    return value


def lowest(d, count):
    return d & -d if d else count


class Place:
    def __init__(self, count, parts):
        self.parts, self.ranks = parts, count // parts
        me = lax.axis_index("space")
        self.part, self.rank = me // self.ranks, lax.rem(me, self.ranks)
        self.bits = [1 << b for b in range(self.ranks.bit_length() - 1)]

    def index(self, off, d):
        return flip(self.part, off) * self.ranks + flip(self.rank, d)

    def device(self, off, d):
        return {"space": self.index(off, d)}

    def peers(self):
        return [(off, 0) for off in range(1, self.parts)] + [(0, d) for d in range(1, self.ranks)]

    def greet(self):
        barrier = pltpu.get_barrier_semaphore()
        for off, d in self.peers():
            pl.semaphore_signal(barrier, inc=1, device_id=self.device(off, d), device_id_type=MESH)

    def meet(self):
        pl.semaphore_wait(pltpu.get_barrier_semaphore(), len(self.peers()))


def remote(src, dst, send, recv, device):
    return pltpu.make_async_remote_copy(
        src_ref=src, dst_ref=dst, send_sem=send, recv_sem=recv, device_id=device, device_id_type=MESH
    )


def piece_of(ref, h):
    size = ref.shape[0] // PIECES
    return ref.at[pl.ds(h * size, size), :]


class Spread:
    def __init__(self, place, stage, got, table, send, recv):
        self.place, self.stage, self.got, self.table = place, stage, got, table
        self.send, self.recv, self.started = send, recv, []

    def block(self, off, d):
        return self.stage.at[0] if off == 0 and d == 0 else self.got.at[off, d]

    def pass_on(self, off, d, h):
        place = self.place
        for bit in reversed(place.bits):
            if bit < lowest(d, place.ranks):
                copy = remote(
                    piece_of(self.block(off, d), h),
                    piece_of(self.got.at[off, d | bit], h),
                    self.send.at[off, d | bit, h],
                    self.recv.at[off, d | bit, h],
                    place.device(0, bit),
                )
                copy.start()
                self.started.append(copy)

    def orders(self, hs):
        return itertools.product(list(range(1, self.place.parts)) + [0], hs)

    def transform(self, hs, rows, cube_t):
        size = rows.shape[0] // PIECES
        for off, h in self.orders(hs):
            columns = pl.ds(pl.multiple_of(flip(self.place.part, off) * LANES, LANES), LANES)
            part = rows[h * size : (h + 1) * size, :]
            spec = jnp.dot(part, cube_t[:, columns], preferred_element_type=jnp.float32)
            piece_of(self.stage.at[off], h)[...] = spec.astype(self.stage.dtype)

    def begin(self, hs):
        for off, h in self.orders(hs):
            if off == 0:
                self.pass_on(0, 0, h)
                continue
            copy = remote(
                piece_of(self.stage.at[off], h),
                piece_of(self.got.at[off, 0], h),
                self.send.at[off, 0, h],
                self.recv.at[off, 0, h],
                self.place.device(off, 0),
            )
            copy.start()
            self.started.append(copy)

    def widen(self, off, d, h):
        source = piece_of(self.block(off, d), h)
        held = self.stage.shape[1]
        size = held // PIECES
        first = self.place.index(off, d) * held + h * size
        rows = pl.ds(pl.multiple_of(first, size), size)
        self.table[rows, :] = source[...].astype(jnp.float32)

    def finish(self, then=None):
        place = self.place

        def when(key):
            off, d, h = key
            return off + 0.5 * h + sum(2.2 if b == 1 else 1.6 for b in place.bits if d & b)

        keys = [
            (off, d, h)
            for off in range(place.parts)
            for d in range(place.ranks)
            for h in range(PIECES)
            if off or d
        ]
        for h in range(PIECES):
            self.widen(0, 0, h)
        for off, d, h in sorted(keys, key=when):
            piece = piece_of(self.got.at[off, d], h)
            remote(
                piece, piece, self.send.at[off, d, h], self.recv.at[off, d, h], place.device(off, d)
            ).wait_recv()
            self.pass_on(off, d, h)
            self.widen(off, d, h)
            if then is not None and (off, d, h) == (place.parts - 1, 0, PIECES - 1):
                then()

    def close(self):
        for copy in self.started:
            copy.wait_send()


def spread_scratch(count, parts, held, dtype):
    ranks = count // parts
    return [
        pltpu.VMEM((parts, held, LANES), dtype),
        pltpu.VMEM((parts, ranks, held, LANES), dtype),
        pltpu.VMEM((count * held, LANES), jnp.float32),
        SEMS((parts, ranks, PIECES)),
        SEMS((parts, ranks, PIECES)),
    ]


def pick_rows(table, lists, t, some, picked):
    src, row = t // (some // SUBS), lax.rem(t, some // SUBS)
    for q in range(SUBS):
        for m in range(picked.shape[0]):
            spot = lists[m][src, row * SUBS + q]
            picked[m, q : q + 1, :] = table[pl.ds(spot, 1), :]


def to_scalars(lists, scalars, sem):
    copies = [pltpu.make_async_copy(lists.at[m], each, sem.at[m]) for m, each in enumerate(scalars)]
    for copy in copies:
        copy.start()
    return copies


def find_equals(lists, same, group, some):
    for src in range(lists.shape[0]):
        rows = lists[src]
        equal = [jnp.where(rows == pltpu.roll(rows, back, 0), 1.0, 0.0) for back in range(1, group // STREAMS)]
        equal.append(jnp.zeros((LANES - group * len(equal), LANES), jnp.float32))
        same[src * some : (src + 1) * some, :] = jnp.concatenate(equal, axis=0).T[:some, :]


def diagonal(rows):
    shape = (rows, LANES)
    return lax.broadcasted_iota(jnp.int32, shape, 0) == lax.broadcasted_iota(jnp.int32, shape, 1)


def shrink_groups(place, second, width, some, table, lists, sigma, first, other, members, coeffs, back, same, energy, ebuf, egot, weights, send, recv, then=None):
    group, refs = members.shape[:2]
    factor = scales(group)
    columns = pl.ds(pl.multiple_of(place.part * LANES, LANES), LANES)
    own = sigma[:, columns]
    level = own * own if second else (shrink_level * own) * (shrink_level * own)

    def forward(b, picked):
        rows = pl.ds(pl.multiple_of(b * SUBS, SUBS), SUBS)
        values = cosine_sums([picked[m] for m in range(group)])
        total = None
        for j in range(group):
            value = values[j] * factor[j]
            square = value * value
            gain = square / (square + level)
            power = gain * gain
            total = power if total is None else total + power
            if second:
                members[j, rows, :] = gain * coeffs[j, rows, :]
            else:
                coeffs[j, rows, :] = value
                members[j, rows, :] = gain * value
        energy[rows, :] = total * level if second else total

    blocks = refs // SUBS
    pick_rows(table, lists, 0, some, first)

    def pair(i, carry):
        pick_rows(table, lists, 2 * i + 1, some, other)
        forward(2 * i, first)
        pick_rows(table, lists, jnp.minimum(2 * i + 2, blocks - 1), some, first)
        forward(2 * i + 1, other)
        return carry

    lax.fori_loop(0, blocks // 2, pair, 0)
    if then is not None:
        then()
    parts = refs // some
    for src in range(parts):
        column = jnp.sum(energy[src * some : (src + 1) * some, :], axis=1, keepdims=True)
        ebuf[src : src + 1, :] = jnp.sum(jnp.where(diagonal(some), column, 0.0), axis=0, keepdims=True)
    started = []
    for off in range(1, place.parts):
        copy = remote(ebuf, egot.at[off], send.at[off], recv.at[off], place.device(off, 0))
        copy.start()
        started.append(copy)

    def inverse(b, carry):
        rows = pl.ds(pl.multiple_of(b * 2 * SUBS, 2 * SUBS), 2 * SUBS)
        values = cosine_sums_transposed([members[j, rows, :] * factor[j] for j in range(group)])
        for m in range(group):
            merged = values[m]
            for before in range(1, m % (group // STREAMS) + 1):
                lane = (before - 1) * group + m
                merged = merged + same[rows, lane : lane + 1] * values[m - before]
            back[m, rows, :] = merged.astype(back.dtype)
        return carry

    lax.fori_loop(0, refs // (2 * SUBS), inverse, 0)
    total = ebuf[...]
    for off in range(1, place.parts):
        remote(ebuf, egot.at[off], send.at[off], recv.at[off], place.device(off, 0)).wait_recv()
        total = total + egot[off]
    weights[...] = 1.0 / (0.25 + total / (group * width))
    for copy in started:
        copy.wait_send()


def shrink_scratch(parts, group, refs):
    assert parts <= SUBS
    return [
        pltpu.VMEM((group, SUBS, LANES), jnp.float32),
        pltpu.VMEM((group, SUBS, LANES), jnp.float32),
        pltpu.VMEM((group, refs, LANES), jnp.float32),
        pltpu.VMEM((refs, LANES), jnp.float32),
        pltpu.VMEM((SUBS, LANES), jnp.float32),
        pltpu.VMEM((parts, SUBS, LANES), jnp.float32),
        SEMS((parts,)),
        SEMS((parts,)),
    ]


def first_kernel(count, x_in, home_in, ids_in, sigma_in, cube_in, coeffs_out, back, weights, same, turned, *scratch):
    stage, got, table, send, recv = scratch[:5]
    first, other, members, energy, ebuf, egot, esend, erecv = scratch[5:13]
    x, cube_t, sigma, ids, insem = scratch[13:18]
    coeffs, csem, home, named, lists_v, lsend, lrecv, lsem = scratch[18:26]
    scalars = scratch[26:]
    parts = stage.shape[0]
    group, some = ids.shape
    place = Place(count, parts)
    pairs = [(x_in, x), (cube_in, cube_t), (home_in, home), (ids_in, ids), (sigma_in, sigma)]
    fetches = [pltpu.make_async_copy(src, dst, insem.at[i]) for i, (src, dst) in enumerate(pairs)]
    for fetch in fetches:
        fetch.start()
    place.greet()
    for fetch in fetches[:2]:
        fetch.wait()
    spread = Spread(place, stage, got, table, send, recv)
    spread.transform(range(PIECES), x, cube_t)
    place.meet()
    spread.begin(range(PIECES))

    def look_up(row, carry):
        for q in range(SUBS):
            for m in range(group):
                named[m, row * SUBS + q] = home[ids[m, row * SUBS + q]]
        return carry

    for fetch in fetches[2:]:
        fetch.wait()
    lax.fori_loop(0, some // SUBS, look_up, 0)

    def fill(m, carry):
        for q in range(some, LANES):
            named[m, q] = 0
        return carry

    lax.fori_loop(0, group, fill, 0)

    ebuf[...] = jnp.zeros(ebuf.shape, ebuf.dtype)
    mine = pltpu.make_async_copy(named, lists_v.at[place.part], lsem.at[0])
    mine.start()
    mine.wait()
    started = []
    for off in range(1, parts):
        copy = remote(
            lists_v.at[place.part],
            lists_v.at[place.part],
            lsend.at[off],
            lrecv.at[off],
            place.device(off, 0),
        )
        copy.start()
        started.append(copy)
    copies = []

    def lists_ready():
        for off in range(1, parts):
            source = lists_v.at[flip(place.part, off)]
            remote(source, source, lsend.at[off], lrecv.at[off], place.device(off, 0)).wait_recv()
        turned[...] = jnp.zeros(turned.shape, turned.dtype)
        for m in range(group):
            for src in range(parts):
                turned[m, src : src + 1, :] = lists_v[src, m : m + 1, :]
        find_equals(lists_v, same, group, some)
        copies.extend(to_scalars(turned, scalars, lsem))

    spread.finish(lists_ready)
    for copy in copies:
        copy.wait()
    store = pltpu.make_async_copy(coeffs, coeffs_out, csem.at[0])
    shrink_groups(
        place, False, x.shape[1], some, table, scalars, sigma, first, other, members, coeffs, back, same, energy, ebuf, egot, weights, esend, erecv, store.start
    )
    store.wait()
    for copy in started:
        copy.wait_send()
    spread.close()


class Collect:
    def __init__(self, place, acc, got, sent, zgot, send, recv):
        self.place, self.acc, self.got, self.sent, self.zgot = place, acc, got, sent, zgot
        self.send, self.recv, self.started = send, recv, []
        self.order = list(range(place.parts - 1, -1, -1))

    def start(self, copy):
        copy.start()
        self.started.append(copy)

    def begin(self):
        place = self.place
        for d in sorted(range(1, place.ranks, 2), key=lambda d: lowest(d - 1, place.ranks)):
            for off in self.order:
                for h in range(PIECES):
                    self.start(
                        remote(
                            piece_of(self.acc.at[place.index(off, d)], h),
                            piece_of(self.got.at[off, d], h),
                            self.send.at[off, d, h],
                            self.recv.at[off, d, h],
                            place.device(0, 1),
                        )
                    )

    def value(self, off, d, h):
        place = self.place
        total = piece_of(self.acc.at[place.index(off, d)], h)[...].astype(jnp.float32)
        for bit in place.bits:
            if bit < lowest(d, place.ranks):
                piece = piece_of(self.got.at[off, d | bit], h)
                remote(
                    piece, piece, self.send.at[off, d | bit, h], self.recv.at[off, d | bit, h], place.device(0, bit)
                ).wait_recv()
                total = total + piece[...].astype(jnp.float32)
        return total

    def run(self):
        for level in self.place.bits[1:] + [self.place.ranks]:
            self.hand_on([d for d in range(0, self.place.ranks, 2) if lowest(d, self.place.ranks) == level])

    def hand_on(self, ds):
        place = self.place
        for d, off, h in itertools.product(ds, self.order, range(PIECES)):
            piece = piece_of(self.sent.at[off, d // 2], h)
            piece[...] = self.value(off, d, h).astype(self.sent.dtype)
            if d == 0 and off == 0:
                continue
            bit = lowest(d, 0)
            self.start(
                remote(
                    piece,
                    piece_of(self.got.at[off, d] if d else self.zgot.at[off], h),
                    self.send.at[off, d, h],
                    self.recv.at[off, d, h],
                    place.device(0, bit) if d else place.device(off, 0),
                )
            )

    def slices(self, h):
        place = self.place
        yield 0, piece_of(self.sent.at[0, 0], h)[...]
        for off in range(1, place.parts):
            piece = piece_of(self.zgot.at[off], h)
            remote(
                piece, piece, self.send.at[off, 0, h], self.recv.at[off, 0, h], place.device(off, 0)
            ).wait_recv()
            yield off, piece[...]

    def close(self):
        for copy in self.started:
            copy.wait_send()


def weigh_rows(place, some, held, turned, weights, wsum):
    parts = place.parts
    group = turned.shape[0]
    many = wsum.shape[0] * (held // LANES)
    lane = lax.broadcasted_iota(jnp.int32, (1, LANES), 1)
    heavy = [jnp.where(lane < some, weights[src : src + 1, :], 0.0) for src in range(parts)]
    tall = lax.broadcasted_iota(jnp.int32, (many, LANES), 0)
    low = lax.broadcasted_iota(jnp.int32, (LANES, LANES), 0)
    first = place.part * (many * LANES)

    def weigh(m, total):
        ones, loads = [], []
        for src in range(parts):
            spots = turned[m, src : src + 1, :] - first
            loads.append(jnp.where((spots >> 7) == tall, heavy[src], 0.0).astype(jnp.bfloat16))
            ones.append(jnp.where((spots & (LANES - 1)) == low, 1.0, 0.0).astype(jnp.bfloat16))
        return total + lax.dot_general(
            jnp.concatenate(loads, axis=1),
            jnp.concatenate(ones, axis=1),
            (((1,), (1,)), ((), ())),
            preferred_element_type=jnp.float32,
        )

    total = lax.fori_loop(0, group, weigh, jnp.zeros((many, LANES), jnp.float32), unroll=True)
    per = held // LANES
    for b in range(wsum.shape[0]):
        wsum[b, :per, :] = total[b * per : (b + 1) * per, :]
        if per < SUBS:
            wsum[b, per:, :] = jnp.zeros((SUBS - per, LANES), jnp.float32)


def settle(place, some, turned, weights, acc, noisy, cube, out, wsum, got, sent, zgot, wgot, send, recv, wsend, wrecv, then=None):
    held = noisy.shape[0]
    collect = Collect(place, acc, got, sent, zgot, send, recv)
    place.greet()
    weigh_rows(place, some, held, turned, weights, wsum)
    place.meet()
    collect.begin()
    for d in range(1, place.ranks):
        collect.start(
            remote(wsum.at[flip(place.rank, d)], wgot.at[d], wsend.at[d], wrecv.at[d], place.device(0, d))
        )
    collect.run()
    denom = wsum[place.rank]
    for d in range(1, place.ranks):
        remote(wgot.at[d], wgot.at[d], wsend.at[d], wrecv.at[d], place.device(0, d)).wait_recv()
        denom = denom + wgot[d]
    size = held // PIECES
    for h in range(PIECES):
        numer = prior_weight * noisy[pl.ds(h * size, size), :].astype(jnp.float32)
        for off, part in collect.slices(h):
            rows = pl.ds(pl.multiple_of(flip(place.part, off) * LANES, LANES), LANES)
            numer = numer + jnp.dot(part, cube[rows, :], preferred_element_type=jnp.float32)
        for j in range(size // LANES):
            row = h * (size // LANES) + j
            spread = jnp.broadcast_to(denom[row : row + 1, :], (LANES, LANES))
            column = jnp.sum(jnp.where(diagonal(LANES), spread, 0.0), axis=1, keepdims=True)
            out[pl.ds(row * LANES, LANES), :] = (
                numer[j * LANES : (j + 1) * LANES, :] / (column + prior_weight)
            ).astype(out.dtype)
        if then is not None:
            then(h)
    return collect


def settle_scratch(count, parts, held, dtype):
    ranks = count // parts
    half = (parts, ranks // 2, held, LANES)
    return [
        pltpu.VMEM((ranks, SUBS, LANES), jnp.float32),
        pltpu.VMEM((parts, ranks, held, LANES), dtype),
        pltpu.VMEM(half, dtype),
        pltpu.VMEM((parts, held, LANES), dtype),
        pltpu.VMEM((ranks, SUBS, LANES), jnp.float32),
        SEMS((parts, ranks, PIECES)),
        SEMS((parts, ranks, PIECES)),
        SEMS((ranks,)),
        SEMS((ranks,)),
    ]


def second_kernel(count, some, acc, weights_in, noisy, cube, cube_t, sigma, turned, same, coeffs_in, basic, back, weights, *scratch):
    stage, got, table, send, recv = scratch[:5]
    first, other, members, energy, ebuf, egot, esend, erecv = scratch[5:13]
    coeffs, csem, lsem = scratch[13:16]
    group = members.shape[0]
    scalars = scratch[16 : 16 + group]
    parts = stage.shape[0]
    place = Place(count, parts)
    fetch = pltpu.make_async_copy(coeffs_in, coeffs, csem.at[0])
    fetch.start()
    copies = to_scalars(turned, scalars, lsem)
    spread = Spread(place, stage, got, table, send, recv)
    ebuf[...] = jnp.zeros(ebuf.shape, ebuf.dtype)
    def spread_piece(h):
        spread.transform([h], basic, cube_t)
        spread.begin([h])

    collect = settle(
        place,
        some,
        turned,
        weights_in,
        acc,
        noisy,
        cube,
        basic,
        *scratch[16 + group :],
        then=spread_piece,
    )
    spread.finish()
    for copy in copies:
        copy.wait()
    fetch.wait()
    shrink_groups(
        place, True, noisy.shape[1], some, table, scalars, sigma, first, other, members, coeffs, back, same, energy, ebuf, egot, weights, esend, erecv
    )
    collect.close()
    spread.close()


def third_kernel(count, parts, some, acc, weights, noisy, cube, turned, out, *scratch):
    settle(Place(count, parts), some, turned, weights, acc, noisy, cube, out, *scratch).close()


def add_kernel(some, carried, turned, weights, back, *refs):
    group, refs_here = back.shape[:2]
    parts = refs_here // some
    kept = refs[:carried]
    acc = refs[carried]
    outs = refs[carried + 1 : 2 * carried + 1]
    heavy, ksem, lsem = refs[2 * carried + 1 : 2 * carried + 4]
    scalars = refs[2 * carried + 4 : 2 * carried + 4 + group]
    sums = refs[2 * carried + 4 + group :]
    blocks, held = acc.shape[:2]
    copies = to_scalars(turned, scalars, lsem)
    moves = [pltpu.make_async_copy(src, dst, ksem.at[i]) for i, (src, dst) in enumerate(zip(kept, outs))]
    for move in moves:
        move.start()

    def clear(i, carry):
        rows = pl.ds(pl.multiple_of(i * LANES, LANES), LANES)
        for each in sums:
            each[rows, :] = jnp.zeros((LANES, LANES), jnp.float32)
        return carry

    lax.fori_loop(0, blocks * held // LANES, clear, 0)
    for src in range(parts):
        row = jnp.broadcast_to(weights[src : src + 1, :], (some, LANES))
        column = jnp.sum(jnp.where(diagonal(some), row, 0.0), axis=1, keepdims=True)
        heavy[src * some : (src + 1) * some, :] = jnp.broadcast_to(column, (some, LANES))
    together = group // STREAMS
    for copy in copies:
        copy.wait()

    def step(t, carry):
        src, row = t // (some // SUBS), lax.rem(t, some // SUBS)
        for q in range(SUBS):
            spots, news = [], []
            weight = heavy[pl.ds(t * SUBS + q, 1), :]
            for m in range(group):
                spot = scalars[m][src, row * SUBS + q]
                spots.append(spot)
                each = weight * back[m, pl.ds(t * SUBS + q, 1), :]
                news.append(sums[m // together][pl.ds(spot, 1), :] + each)
            for m in range(group):
                sums[m // together][pl.ds(spots[m], 1), :] = news[m]
        return carry

    lax.fori_loop(0, refs_here // SUBS, step, 0)

    def store(b, carry):
        for i in range(held // LANES):
            rows = pl.ds(pl.multiple_of(b * held + i * LANES, LANES), LANES)
            whole = sums[0][rows, :]
            for each in sums[1:]:
                whole = whole + each[rows, :]
            acc[b, i * LANES : (i + 1) * LANES, :] = whole.astype(acc.dtype)
        return carry

    lax.fori_loop(0, blocks, store, 0)
    for move in moves:
        move.wait()


def shape(*dims, dtype=jnp.float32):
    return jax.ShapeDtypeStruct(dims, dtype)


def params(rows, collective_id=None):
    limit = 5 * rows * LANES * 4 + (10 << 20)
    return pltpu.CompilerParams(
        collective_id=collective_id, has_side_effects=collective_id is not None, vmem_limit_bytes=limit
    )


def add_up(count, some, held, dtype, turned, weights, back, *kept):
    group, refs = back.shape[:2]
    return pl.pallas_call(
        functools.partial(add_kernel, some, len(kept)),
        out_shape=[shape(count, held, LANES, dtype=dtype)]
        + [shape(*each.shape, dtype=each.dtype) for each in kept],
        in_specs=[VMEM] * (3 + len(kept)),
        out_specs=[VMEM] + [HBM] * len(kept),
        scratch_shapes=[pltpu.VMEM((refs, LANES), jnp.float32), SEMS((1,)), SEMS((group,))]
        + [pltpu.SMEM((SUBS, LANES), jnp.int32)] * group
        + [pltpu.VMEM((count * held, LANES), jnp.float32)] * STREAMS,
        compiler_params=params(count * held),
        name="add_up",
    )(turned, weights, back, *kept)


def body(noisy, matches, cube_home, sigma_coef):
    count = lax.axis_size("space")
    some, group = matches.shape
    held, width = noisy.shape
    parts = width // LANES
    refs = parts * some
    cube, cube_t = cube_tables()
    sigma = sigma_coef[None, :]
    dtype = noisy.dtype
    shared = spread_scratch(count, parts, held, dtype) + shrink_scratch(parts, group, refs)
    coeffs, back, weights, same, turned = pl.pallas_call(
        functools.partial(first_kernel, count),
        out_shape=[
            shape(group, refs, LANES),
            shape(group, refs, LANES),
            shape(SUBS, LANES),
            shape(refs, LANES),
            shape(group, SUBS, LANES, dtype=jnp.int32),
        ],
        in_specs=[HBM] * 5,
        out_specs=[HBM] + [VMEM] * 4,
        scratch_shapes=shared
        + [
            pltpu.VMEM(noisy.shape, dtype),
            pltpu.VMEM(cube_t.shape, dtype),
            pltpu.VMEM(sigma.shape, jnp.float32),
            pltpu.SMEM((group, some), jnp.int32),
            SEMS((5,)),
            pltpu.VMEM((group, refs, LANES), jnp.float32),
            SEMS((1,)),
            pltpu.SMEM(cube_home.shape, jnp.int32),
            pltpu.SMEM((group, LANES), jnp.int32),
            pltpu.VMEM((parts, group, LANES), jnp.int32),
            SEMS((parts,)),
            SEMS((parts,)),
            SEMS((group,)),
        ]
        + [pltpu.SMEM((SUBS, LANES), jnp.int32)] * group,
        compiler_params=params(count * held, 0),
        name="shrink",
    )(*[pltpu.with_memory_space_constraint(v, pltpu.HBM) for v in (noisy, cube_home, matches.T, sigma, jnp.asarray(cube_t))])
    (acc,) = add_up(count, some, held, dtype, turned, weights, back)
    basic, back, weights = pl.pallas_call(
        functools.partial(second_kernel, count, some),
        out_shape=[
            shape(held, width, dtype=dtype),
            shape(group, refs, LANES),
            shape(SUBS, LANES),
        ],
        in_specs=[VMEM] * 8 + [HBM],
        out_specs=[VMEM] * 3,
        scratch_shapes=shared
        + [pltpu.VMEM((group, refs, LANES), jnp.float32), SEMS((1,)), SEMS((group,))]
        + [pltpu.SMEM((SUBS, LANES), jnp.int32)] * group
        + settle_scratch(count, parts, held, dtype),
        compiler_params=params(count * held, 1),
        name="wiener",
    )(acc, weights, noisy, cube, cube_t, sigma, turned, same, coeffs)
    acc, basic = add_up(count, some, held, dtype, turned, weights, back, basic)
    final = pl.pallas_call(
        functools.partial(third_kernel, count, parts, some),
        out_shape=shape(held, width, dtype=dtype),
        in_specs=[VMEM] * 5,
        out_specs=VMEM,
        scratch_shapes=settle_scratch(count, parts, held, dtype),
        compiler_params=params(count * held, 2),
        name="settle",
    )(acc, weights, noisy, cube, turned)
    return basic, final


def solution(mesh):
    in_specs = (P(("groups", "space"), None), P(("groups", "space"), None), P("groups"), P())
    out_specs = (P(("groups", "space"), None), P(("groups", "space"), None))
    return jax.shard_map(body, mesh=mesh, in_specs=in_specs, out_specs=out_specs, check_vma=False)
```

```python
import functools
import itertools

import jax
import jax.numpy as jnp
import numpy as np
from jax import lax
from jax.experimental import pallas as pl
from jax.experimental.pallas import tpu as pltpu
from jax.sharding import PartitionSpec as P

shrink_level = 2.7
prior_weight = 0.5
LANES = 128
SUBS = 8
PIECES = 2
STREAMS = 4
MESH = pl.DeviceIdType.MESH
VMEM = pl.BlockSpec(memory_space=pltpu.VMEM)
SMEM = pl.BlockSpec(memory_space=pltpu.SMEM)
HBM = pl.BlockSpec(memory_space=pltpu.HBM)
SEMS = pltpu.SemaphoreType.DMA


def dct_matrix(length):
    index = np.arange(length, dtype=np.float64)
    table = np.cos(np.pi * (2.0 * index[None, :] + 1.0) * index[:, None] / (2.0 * length))
    table = table * np.sqrt(2.0 / length)
    table[0] /= np.sqrt(2.0)
    return table


def cube_tables():
    small = dct_matrix(8)
    cube = np.kron(np.kron(small, small), small).astype(np.float32)
    return cube.astype(jnp.bfloat16), cube.T.astype(jnp.bfloat16)


def half_cosines(n):
    return [float(2.0 * np.cos(np.pi * (2 * i + 1) / (2 * n))) for i in range(n // 2)]


def cosine_sums(x):
    n = len(x)
    if n == 2:
        return [x[0] + x[1], (x[0] - x[1]) * float(np.cos(np.pi / 4))]
    half = n // 2
    even = cosine_sums([x[i] + x[n - 1 - i] for i in range(half)])
    turned = cosine_sums([(x[i] - x[n - 1 - i]) * f for i, f in enumerate(half_cosines(n))])
    out = [None] * n
    for k in range(half):
        out[2 * k] = even[k]
        out[2 * k + 1] = turned[k] - out[2 * k - 1] if k else 0.5 * turned[0]
    return out


def cosine_sums_transposed(y):
    n = len(y)
    if n == 2:
        odd = y[1] * float(np.cos(np.pi / 4))
        return [y[0] + odd, y[0] - odd]
    half = n // 2
    even = cosine_sums_transposed(y[0::2])
    tail = [None] * half
    for k in reversed(range(half)):
        tail[k] = y[2 * k + 1] - tail[k + 1] if k + 1 < half else y[2 * k + 1]
    tail[0] = 0.5 * tail[0]
    odd = [o * f for o, f in zip(cosine_sums_transposed(tail), half_cosines(n))]
    return [even[i] + odd[i] for i in range(half)] + [even[i] - odd[i] for i in reversed(range(half))]


def scales(n):
    return [float(np.sqrt((1.0 if k == 0 else 2.0) / n)) for k in range(n)]


def flip(value, mask):
    if isinstance(mask, int):
        for bit in (1 << b for b in range(mask.bit_length())):
            if mask & bit:
                value = value + bit - 2 * bit * lax.rem(value // bit, 2)
        return value
    for bit in (1, 2):
        value = value + bit * lax.rem(mask // bit, 2) * (1 - 2 * lax.rem(value // bit, 2))
    return value


def lowest(d, count):
    return d & -d if d else count


class Place:
    def __init__(self, count, parts):
        self.parts, self.ranks = parts, count // parts
        me = lax.axis_index("space")
        self.part, self.rank = me // self.ranks, lax.rem(me, self.ranks)
        self.bits = [1 << b for b in range(self.ranks.bit_length() - 1)]

    def index(self, off, d):
        return flip(self.part, off) * self.ranks + flip(self.rank, d)

    def device(self, off, d):
        return {"space": self.index(off, d)}

    def peers(self):
        return [(off, 0) for off in range(1, self.parts)] + [(0, d) for d in range(1, self.ranks)]

    def greet(self):
        barrier = pltpu.get_barrier_semaphore()
        for off, d in self.peers():
            pl.semaphore_signal(barrier, inc=1, device_id=self.device(off, d), device_id_type=MESH)

    def meet(self):
        pl.semaphore_wait(pltpu.get_barrier_semaphore(), len(self.peers()))


def remote(src, dst, send, recv, device):
    return pltpu.make_async_remote_copy(
        src_ref=src, dst_ref=dst, send_sem=send, recv_sem=recv, device_id=device, device_id_type=MESH
    )


def piece_of(ref, h):
    size = ref.shape[0] // PIECES
    return ref.at[pl.ds(h * size, size), :]


class Spread:
    def __init__(self, place, stage, got, table, send, recv):
        self.place, self.stage, self.got, self.table = place, stage, got, table
        self.send, self.recv, self.started = send, recv, []

    def block(self, off, d):
        return self.stage.at[0] if off == 0 and d == 0 else self.got.at[off, d]

    def pass_on(self, off, d, h):
        place = self.place
        for bit in reversed(place.bits):
            if bit < lowest(d, place.ranks):
                copy = remote(
                    piece_of(self.block(off, d), h),
                    piece_of(self.got.at[off, d | bit], h),
                    self.send.at[off, d | bit, h],
                    self.recv.at[off, d | bit, h],
                    place.device(0, bit),
                )
                copy.start()
                self.started.append(copy)

    def orders(self, hs):
        return itertools.product(list(range(1, self.place.parts)) + [0], hs)

    def transform(self, hs, rows, cube_t):
        size = rows.shape[0] // PIECES
        for off, h in self.orders(hs):
            columns = pl.ds(pl.multiple_of(flip(self.place.part, off) * LANES, LANES), LANES)
            part = rows[h * size : (h + 1) * size, :]
            spec = jnp.dot(part, cube_t[:, columns], preferred_element_type=jnp.float32)
            piece_of(self.stage.at[off], h)[...] = spec.astype(self.stage.dtype)

    def begin(self, hs):
        for off, h in self.orders(hs):
            if off == 0:
                self.pass_on(0, 0, h)
                continue
            copy = remote(
                piece_of(self.stage.at[off], h),
                piece_of(self.got.at[off, 0], h),
                self.send.at[off, 0, h],
                self.recv.at[off, 0, h],
                self.place.device(off, 0),
            )
            copy.start()
            self.started.append(copy)

    def widen(self, off, d, h):
        source = piece_of(self.block(off, d), h)
        held = self.stage.shape[1]
        size = held // PIECES
        first = self.place.index(off, d) * held + h * size
        rows = pl.ds(pl.multiple_of(first, size), size)
        self.table[rows, :] = source[...].astype(jnp.float32)

    def finish(self, then=None):
        place = self.place

        def when(key):
            off, d, h = key
            return off + 0.5 * h + sum(2.2 if b == 1 else 1.6 for b in place.bits if d & b)

        keys = [
            (off, d, h)
            for off in range(place.parts)
            for d in range(place.ranks)
            for h in range(PIECES)
            if off or d
        ]
        for h in range(PIECES):
            self.widen(0, 0, h)
        for off, d, h in sorted(keys, key=when):
            piece = piece_of(self.got.at[off, d], h)
            remote(
                piece, piece, self.send.at[off, d, h], self.recv.at[off, d, h], place.device(off, d)
            ).wait_recv()
            self.pass_on(off, d, h)
            self.widen(off, d, h)
            if then is not None and (off, d, h) == (place.parts - 1, 0, PIECES - 1):
                then()

    def close(self):
        for copy in self.started:
            copy.wait_send()


def spread_scratch(count, parts, held, dtype):
    ranks = count // parts
    return [
        pltpu.VMEM((parts, held, LANES), dtype),
        pltpu.VMEM((parts, ranks, held, LANES), dtype),
        pltpu.VMEM((count * held, LANES), jnp.float32),
        SEMS((parts, ranks, PIECES)),
        SEMS((parts, ranks, PIECES)),
    ]


def pick_rows(table, lists, t, some, picked):
    src, row = t // (some // SUBS), lax.rem(t, some // SUBS)
    for q in range(SUBS):
        for m in range(picked.shape[0]):
            spot = lists[m][src, row * SUBS + q]
            picked[m, q : q + 1, :] = table[pl.ds(spot, 1), :]


def to_scalars(lists, scalars, sem):
    copies = [pltpu.make_async_copy(lists.at[m], each, sem.at[m]) for m, each in enumerate(scalars)]
    for copy in copies:
        copy.start()
    return copies


def find_equals(lists, same, group, some):
    for src in range(lists.shape[0]):
        rows = lists[src]
        equal = [jnp.where(rows == pltpu.roll(rows, back, 0), 1.0, 0.0) for back in range(1, group // STREAMS)]
        equal.append(jnp.zeros((LANES - group * len(equal), LANES), jnp.float32))
        same[src * some : (src + 1) * some, :] = jnp.concatenate(equal, axis=0).T[:some, :]


def diagonal(rows):
    shape = (rows, LANES)
    return lax.broadcasted_iota(jnp.int32, shape, 0) == lax.broadcasted_iota(jnp.int32, shape, 1)


def shrink_groups(place, second, width, some, table, lists, sigma, first, other, members, coeffs, back, same, energy, ebuf, egot, weights, send, recv, then=None):
    group, refs = members.shape[:2]
    factor = scales(group)
    columns = pl.ds(pl.multiple_of(place.part * LANES, LANES), LANES)
    own = sigma[:, columns]
    level = own * own if second else (shrink_level * own) * (shrink_level * own)

    def forward(b, picked):
        rows = pl.ds(pl.multiple_of(b * SUBS, SUBS), SUBS)
        values = cosine_sums([picked[m] for m in range(group)])
        total = None
        for j in range(group):
            value = values[j] * factor[j]
            square = value * value
            gain = square / (square + level)
            power = gain * gain
            total = power if total is None else total + power
            if second:
                members[j, rows, :] = gain * coeffs[j, rows, :]
            else:
                coeffs[j, rows, :] = value
                members[j, rows, :] = gain * value
        energy[rows, :] = total * level if second else total

    blocks = refs // SUBS
    pick_rows(table, lists, 0, some, first)

    def pair(i, carry):
        pick_rows(table, lists, 2 * i + 1, some, other)
        forward(2 * i, first)
        pick_rows(table, lists, jnp.minimum(2 * i + 2, blocks - 1), some, first)
        forward(2 * i + 1, other)
        return carry

    lax.fori_loop(0, blocks // 2, pair, 0, unroll=2)
    if then is not None:
        then()
    parts = refs // some
    for src in range(parts):
        column = jnp.sum(energy[src * some : (src + 1) * some, :], axis=1, keepdims=True)
        ebuf[src : src + 1, :] = jnp.sum(jnp.where(diagonal(some), column, 0.0), axis=0, keepdims=True)
    started = []
    for off in range(1, place.parts):
        copy = remote(ebuf, egot.at[off], send.at[off], recv.at[off], place.device(off, 0))
        copy.start()
        started.append(copy)

    def inverse(b, carry):
        rows = pl.ds(pl.multiple_of(b * 2 * SUBS, 2 * SUBS), 2 * SUBS)
        values = cosine_sums_transposed([members[j, rows, :] * factor[j] for j in range(group)])
        for m in range(group):
            merged = values[m]
            for before in range(1, m % (group // STREAMS) + 1):
                lane = (before - 1) * group + m
                merged = merged + same[rows, lane : lane + 1] * values[m - before]
            back[m, rows, :] = merged.astype(back.dtype)
        return carry

    lax.fori_loop(0, refs // (2 * SUBS), inverse, 0)
    total = ebuf[...]
    for off in range(1, place.parts):
        remote(ebuf, egot.at[off], send.at[off], recv.at[off], place.device(off, 0)).wait_recv()
        total = total + egot[off]
    weights[...] = 1.0 / (0.25 + total / (group * width))
    for copy in started:
        copy.wait_send()


def shrink_scratch(parts, group, refs):
    assert parts <= SUBS
    return [
        pltpu.VMEM((group, SUBS, LANES), jnp.float32),
        pltpu.VMEM((group, SUBS, LANES), jnp.float32),
        pltpu.VMEM((group, refs, LANES), jnp.float32),
        pltpu.VMEM((refs, LANES), jnp.float32),
        pltpu.VMEM((SUBS, LANES), jnp.float32),
        pltpu.VMEM((parts, SUBS, LANES), jnp.float32),
        SEMS((parts,)),
        SEMS((parts,)),
    ]


def first_kernel(count, x_in, home_in, ids_in, sigma_in, cube_in, coeffs_out, back, weights, same, turned, *scratch):
    stage, got, table, send, recv = scratch[:5]
    first, other, members, energy, ebuf, egot, esend, erecv = scratch[5:13]
    x, cube_t, sigma, ids, insem = scratch[13:18]
    coeffs, csem, home, named, lists_v, lsend, lrecv, lsem = scratch[18:26]
    scalars = scratch[26:]
    parts = stage.shape[0]
    group, some = ids.shape
    place = Place(count, parts)
    pairs = [(x_in, x), (cube_in, cube_t), (home_in, home), (ids_in, ids), (sigma_in, sigma)]
    fetches = [pltpu.make_async_copy(src, dst, insem.at[i]) for i, (src, dst) in enumerate(pairs)]
    for fetch in fetches:
        fetch.start()
    place.greet()
    for fetch in fetches[:2]:
        fetch.wait()
    spread = Spread(place, stage, got, table, send, recv)
    spread.transform(range(PIECES), x, cube_t)
    place.meet()
    spread.begin(range(PIECES))

    def look_up(row, carry):
        for q in range(SUBS):
            for m in range(group):
                named[m, row * SUBS + q] = home[ids[m, row * SUBS + q]]
        return carry

    for fetch in fetches[2:]:
        fetch.wait()
    lax.fori_loop(0, some // SUBS, look_up, 0)

    def fill(m, carry):
        for q in range(some, LANES):
            named[m, q] = 0
        return carry

    lax.fori_loop(0, group, fill, 0)

    ebuf[...] = jnp.zeros(ebuf.shape, ebuf.dtype)
    mine = pltpu.make_async_copy(named, lists_v.at[place.part], lsem.at[0])
    mine.start()
    mine.wait()
    started = []
    for off in range(1, parts):
        copy = remote(
            lists_v.at[place.part],
            lists_v.at[place.part],
            lsend.at[off],
            lrecv.at[off],
            place.device(off, 0),
        )
        copy.start()
        started.append(copy)
    copies = []

    def lists_ready():
        for off in range(1, parts):
            source = lists_v.at[flip(place.part, off)]
            remote(source, source, lsend.at[off], lrecv.at[off], place.device(off, 0)).wait_recv()
        turned[...] = jnp.zeros(turned.shape, turned.dtype)
        for m in range(group):
            for src in range(parts):
                turned[m, src : src + 1, :] = lists_v[src, m : m + 1, :]
        find_equals(lists_v, same, group, some)
        copies.extend(to_scalars(turned, scalars, lsem))

    spread.finish(lists_ready)
    for copy in copies:
        copy.wait()
    store = pltpu.make_async_copy(coeffs, coeffs_out, csem.at[0])
    shrink_groups(
        place, False, x.shape[1], some, table, scalars, sigma, first, other, members, coeffs, back, same, energy, ebuf, egot, weights, esend, erecv, store.start
    )
    store.wait()
    for copy in started:
        copy.wait_send()
    spread.close()


class Collect:
    def __init__(self, place, acc, got, sent, zgot, send, recv):
        self.place, self.acc, self.got, self.sent, self.zgot = place, acc, got, sent, zgot
        self.send, self.recv, self.started = send, recv, []
        self.order = sorted(range(1, place.parts), key=lambda off: (off % 2, off)) + [0]

    def start(self, copy):
        copy.start()
        self.started.append(copy)

    def begin(self):
        place = self.place
        for d in sorted(range(1, place.ranks, 2), key=lambda d: lowest(d - 1, place.ranks)):
            for off in self.order:
                for h in range(PIECES):
                    self.start(
                        remote(
                            piece_of(self.acc.at[place.index(off, d)], h),
                            piece_of(self.got.at[off, d], h),
                            self.send.at[off, d, h],
                            self.recv.at[off, d, h],
                            place.device(0, 1),
                        )
                    )

    def value(self, off, d, h):
        place = self.place
        total = piece_of(self.acc.at[place.index(off, d)], h)[...].astype(jnp.float32)
        for bit in place.bits:
            if bit < lowest(d, place.ranks):
                piece = piece_of(self.got.at[off, d | bit], h)
                remote(
                    piece, piece, self.send.at[off, d | bit, h], self.recv.at[off, d | bit, h], place.device(0, bit)
                ).wait_recv()
                total = total + piece[...].astype(jnp.float32)
        return total

    def run(self):
        for level in self.place.bits[1:] + [self.place.ranks]:
            self.hand_on([d for d in range(0, self.place.ranks, 2) if lowest(d, self.place.ranks) == level])

    def hand_on(self, ds):
        place = self.place
        for d, off, h in itertools.product(ds, self.order, range(PIECES)):
            piece = piece_of(self.sent.at[off, d // 2], h)
            piece[...] = self.value(off, d, h).astype(self.sent.dtype)
            if d == 0 and off == 0:
                continue
            bit = lowest(d, 0)
            self.start(
                remote(
                    piece,
                    piece_of(self.got.at[off, d] if d else self.zgot.at[off], h),
                    self.send.at[off, d, h],
                    self.recv.at[off, d, h],
                    place.device(0, bit) if d else place.device(off, 0),
                )
            )

    def slices(self, h):
        place = self.place
        yield 0, piece_of(self.sent.at[0, 0], h)[...]
        for off in range(1, place.parts):
            piece = piece_of(self.zgot.at[off], h)
            remote(
                piece, piece, self.send.at[off, 0, h], self.recv.at[off, 0, h], place.device(off, 0)
            ).wait_recv()
            yield off, piece[...]

    def close(self):
        for copy in self.started:
            copy.wait_send()


def weigh_rows(place, some, held, turned, weights, wsum):
    parts = place.parts
    group = turned.shape[0]
    many = wsum.shape[0] * (held // LANES)
    lane = lax.broadcasted_iota(jnp.int32, (1, LANES), 1)
    heavy = [jnp.where(lane < some, weights[src : src + 1, :], 0.0) for src in range(parts)]
    tall = lax.broadcasted_iota(jnp.int32, (many, LANES), 0)
    low = lax.broadcasted_iota(jnp.int32, (LANES, LANES), 0)
    first = place.part * (many * LANES)

    def weigh(m, total):
        ones, loads = [], []
        for src in range(parts):
            spots = turned[m, src : src + 1, :] - first
            loads.append(jnp.where((spots >> 7) == tall, heavy[src], 0.0).astype(jnp.bfloat16))
            ones.append(jnp.where((spots & (LANES - 1)) == low, 1.0, 0.0).astype(jnp.bfloat16))
        return total + lax.dot_general(
            jnp.concatenate(loads, axis=1),
            jnp.concatenate(ones, axis=1),
            (((1,), (1,)), ((), ())),
            preferred_element_type=jnp.float32,
        )

    total = lax.fori_loop(0, group, weigh, jnp.zeros((many, LANES), jnp.float32), unroll=True)
    per = held // LANES
    for b in range(wsum.shape[0]):
        wsum[b, :per, :] = total[b * per : (b + 1) * per, :]
        if per < SUBS:
            wsum[b, per:, :] = jnp.zeros((SUBS - per, LANES), jnp.float32)


def settle(place, some, turned, weights, acc, noisy, cube, out, wsum, got, sent, zgot, wgot, send, recv, wsend, wrecv, then=None):
    held = noisy.shape[0]
    collect = Collect(place, acc, got, sent, zgot, send, recv)
    place.greet()
    weigh_rows(place, some, held, turned, weights, wsum)
    place.meet()
    collect.begin()
    for d in range(1, place.ranks):
        collect.start(
            remote(wsum.at[flip(place.rank, d)], wgot.at[d], wsend.at[d], wrecv.at[d], place.device(0, d))
        )
    collect.run()
    denom = wsum[place.rank]
    for d in range(1, place.ranks):
        remote(wgot.at[d], wgot.at[d], wsend.at[d], wrecv.at[d], place.device(0, d)).wait_recv()
        denom = denom + wgot[d]
    size = held // PIECES
    for h in range(PIECES):
        numer = prior_weight * noisy[pl.ds(h * size, size), :].astype(jnp.float32)
        for off, part in collect.slices(h):
            rows = pl.ds(pl.multiple_of(flip(place.part, off) * LANES, LANES), LANES)
            numer = numer + jnp.dot(part, cube[rows, :], preferred_element_type=jnp.float32)
        for j in range(size // LANES):
            row = h * (size // LANES) + j
            spread = jnp.broadcast_to(denom[row : row + 1, :], (LANES, LANES))
            column = jnp.sum(jnp.where(diagonal(LANES), spread, 0.0), axis=1, keepdims=True)
            out[pl.ds(row * LANES, LANES), :] = (
                numer[j * LANES : (j + 1) * LANES, :] / (column + prior_weight)
            ).astype(out.dtype)
        if then is not None:
            then(h)
    return collect


def settle_scratch(count, parts, held, dtype):
    ranks = count // parts
    half = (parts, ranks // 2, held, LANES)
    return [
        pltpu.VMEM((ranks, SUBS, LANES), jnp.float32),
        pltpu.VMEM((parts, ranks, held, LANES), dtype),
        pltpu.VMEM(half, dtype),
        pltpu.VMEM((parts, held, LANES), dtype),
        pltpu.VMEM((ranks, SUBS, LANES), jnp.float32),
        SEMS((parts, ranks, PIECES)),
        SEMS((parts, ranks, PIECES)),
        SEMS((ranks,)),
        SEMS((ranks,)),
    ]


def second_kernel(count, some, acc, weights_in, noisy, cube, cube_t, sigma, turned, same, coeffs_in, basic, back, weights, *scratch):
    stage, got, table, send, recv = scratch[:5]
    first, other, members, energy, ebuf, egot, esend, erecv = scratch[5:13]
    coeffs, csem, lsem = scratch[13:16]
    group = members.shape[0]
    scalars = scratch[16 : 16 + group]
    parts = stage.shape[0]
    place = Place(count, parts)
    fetch = pltpu.make_async_copy(coeffs_in, coeffs, csem.at[0])
    fetch.start()
    copies = to_scalars(turned, scalars, lsem)
    spread = Spread(place, stage, got, table, send, recv)
    ebuf[...] = jnp.zeros(ebuf.shape, ebuf.dtype)
    def spread_piece(h):
        spread.transform([h], basic, cube_t)
        spread.begin([h])

    collect = settle(
        place,
        some,
        turned,
        weights_in,
        acc,
        noisy,
        cube,
        basic,
        *scratch[16 + group :],
        then=spread_piece,
    )
    spread.finish()
    for copy in copies:
        copy.wait()
    fetch.wait()
    shrink_groups(
        place, True, noisy.shape[1], some, table, scalars, sigma, first, other, members, coeffs, back, same, energy, ebuf, egot, weights, esend, erecv
    )
    collect.close()
    spread.close()


def third_kernel(count, parts, some, acc, weights, noisy, cube, turned, out, *scratch):
    settle(Place(count, parts), some, turned, weights, acc, noisy, cube, out, *scratch).close()


def add_kernel(some, carried, turned, weights, back, *refs):
    group, refs_here = back.shape[:2]
    parts = refs_here // some
    kept = refs[:carried]
    acc = refs[carried]
    outs = refs[carried + 1 : 2 * carried + 1]
    heavy, ksem, lsem = refs[2 * carried + 1 : 2 * carried + 4]
    scalars = refs[2 * carried + 4 : 2 * carried + 4 + group]
    sums = refs[2 * carried + 4 + group :]
    blocks, held = acc.shape[:2]
    copies = to_scalars(turned, scalars, lsem)
    moves = [pltpu.make_async_copy(src, dst, ksem.at[i]) for i, (src, dst) in enumerate(zip(kept, outs))]
    for move in moves:
        move.start()

    def clear(i, carry):
        rows = pl.ds(pl.multiple_of(i * LANES, LANES), LANES)
        for each in sums:
            each[rows, :] = jnp.zeros((LANES, LANES), jnp.float32)
        return carry

    lax.fori_loop(0, blocks * held // LANES, clear, 0)
    for src in range(parts):
        row = jnp.broadcast_to(weights[src : src + 1, :], (some, LANES))
        column = jnp.sum(jnp.where(diagonal(some), row, 0.0), axis=1, keepdims=True)
        heavy[src * some : (src + 1) * some, :] = jnp.broadcast_to(column, (some, LANES))
    together = group // STREAMS
    for copy in copies:
        copy.wait()

    def step(t, carry):
        src, row = t // (some // SUBS), lax.rem(t, some // SUBS)
        for q in range(SUBS):
            spots, news = [], []
            weight = heavy[pl.ds(t * SUBS + q, 1), :]
            for m in range(group):
                spot = scalars[m][src, row * SUBS + q]
                spots.append(spot)
                each = weight * back[m, pl.ds(t * SUBS + q, 1), :]
                news.append(sums[m // together][pl.ds(spot, 1), :] + each)
            for m in range(group):
                sums[m // together][pl.ds(spots[m], 1), :] = news[m]
        return carry

    lax.fori_loop(0, refs_here // SUBS, step, 0)

    def store(b, carry):
        for i in range(held // LANES):
            rows = pl.ds(pl.multiple_of(b * held + i * LANES, LANES), LANES)
            whole = sums[0][rows, :]
            for each in sums[1:]:
                whole = whole + each[rows, :]
            acc[b, i * LANES : (i + 1) * LANES, :] = whole.astype(acc.dtype)
        return carry

    lax.fori_loop(0, blocks, store, 0)
    for move in moves:
        move.wait()


def shape(*dims, dtype=jnp.float32):
    return jax.ShapeDtypeStruct(dims, dtype)


def params(rows, collective_id=None):
    limit = 5 * rows * LANES * 4 + (10 << 20)
    return pltpu.CompilerParams(
        collective_id=collective_id, has_side_effects=collective_id is not None, vmem_limit_bytes=limit
    )


def add_up(count, some, held, dtype, turned, weights, back, *kept):
    group, refs = back.shape[:2]
    return pl.pallas_call(
        functools.partial(add_kernel, some, len(kept)),
        out_shape=[shape(count, held, LANES, dtype=dtype)]
        + [shape(*each.shape, dtype=each.dtype) for each in kept],
        in_specs=[VMEM] * (3 + len(kept)),
        out_specs=[VMEM] + [HBM] * len(kept),
        scratch_shapes=[pltpu.VMEM((refs, LANES), jnp.float32), SEMS((1,)), SEMS((group,))]
        + [pltpu.SMEM((SUBS, LANES), jnp.int32)] * group
        + [pltpu.VMEM((count * held, LANES), jnp.float32)] * STREAMS,
        compiler_params=params(count * held),
        name="add_up",
    )(turned, weights, back, *kept)


def body(noisy, matches, cube_home, sigma_coef):
    count = lax.axis_size("space")
    some, group = matches.shape
    held, width = noisy.shape
    parts = width // LANES
    refs = parts * some
    cube, cube_t = cube_tables()
    sigma = sigma_coef[None, :]
    dtype = noisy.dtype
    shared = spread_scratch(count, parts, held, dtype) + shrink_scratch(parts, group, refs)
    coeffs, back, weights, same, turned = pl.pallas_call(
        functools.partial(first_kernel, count),
        out_shape=[
            shape(group, refs, LANES),
            shape(group, refs, LANES),
            shape(SUBS, LANES),
            shape(refs, LANES),
            shape(group, SUBS, LANES, dtype=jnp.int32),
        ],
        in_specs=[HBM] * 5,
        out_specs=[HBM] + [VMEM] * 4,
        scratch_shapes=shared
        + [
            pltpu.VMEM(noisy.shape, dtype),
            pltpu.VMEM(cube_t.shape, dtype),
            pltpu.VMEM(sigma.shape, jnp.float32),
            pltpu.SMEM((group, some), jnp.int32),
            SEMS((5,)),
            pltpu.VMEM((group, refs, LANES), jnp.float32),
            SEMS((1,)),
            pltpu.SMEM(cube_home.shape, jnp.int32),
            pltpu.SMEM((group, LANES), jnp.int32),
            pltpu.VMEM((parts, group, LANES), jnp.int32),
            SEMS((parts,)),
            SEMS((parts,)),
            SEMS((group,)),
        ]
        + [pltpu.SMEM((SUBS, LANES), jnp.int32)] * group,
        compiler_params=params(count * held, 0),
        name="shrink",
    )(*[pltpu.with_memory_space_constraint(v, pltpu.HBM) for v in (noisy, cube_home, matches.T, sigma, jnp.asarray(cube_t))])
    (acc,) = add_up(count, some, held, dtype, turned, weights, back)
    basic, back, weights = pl.pallas_call(
        functools.partial(second_kernel, count, some),
        out_shape=[
            shape(held, width, dtype=dtype),
            shape(group, refs, LANES),
            shape(SUBS, LANES),
        ],
        in_specs=[VMEM] * 8 + [HBM],
        out_specs=[VMEM] * 3,
        scratch_shapes=shared
        + [pltpu.VMEM((group, refs, LANES), jnp.float32), SEMS((1,)), SEMS((group,))]
        + [pltpu.SMEM((SUBS, LANES), jnp.int32)] * group
        + settle_scratch(count, parts, held, dtype),
        compiler_params=params(count * held, 1),
        name="wiener",
    )(acc, weights, noisy, cube, cube_t, sigma, turned, same, coeffs)
    acc, basic = add_up(count, some, held, dtype, turned, weights, back, basic)
    final = pl.pallas_call(
        functools.partial(third_kernel, count, parts, some),
        out_shape=shape(held, width, dtype=dtype),
        in_specs=[VMEM] * 5,
        out_specs=VMEM,
        scratch_shapes=settle_scratch(count, parts, held, dtype),
        compiler_params=params(count * held, 2),
        name="settle",
    )(acc, weights, noisy, cube, turned)
    return basic, final


def solution(mesh):
    in_specs = (P(("groups", "space"), None), P(("groups", "space"), None), P("groups"), P())
    out_specs = (P(("groups", "space"), None), P(("groups", "space"), None))
    return jax.shard_map(body, mesh=mesh, in_specs=in_specs, out_specs=out_specs, check_vma=False)
```

```python
import functools
import itertools

import jax
import jax.numpy as jnp
import numpy as np
from jax import lax
from jax.experimental import pallas as pl
from jax.experimental.pallas import tpu as pltpu
from jax.sharding import PartitionSpec as P

shrink_level = 2.7
prior_weight = 0.5
LANES = 128
SUBS = 8
PIECES = 2
STREAMS = 4
MESH = pl.DeviceIdType.MESH
VMEM = pl.BlockSpec(memory_space=pltpu.VMEM)
SMEM = pl.BlockSpec(memory_space=pltpu.SMEM)
HBM = pl.BlockSpec(memory_space=pltpu.HBM)
SEMS = pltpu.SemaphoreType.DMA


def dct_matrix(length):
    index = np.arange(length, dtype=np.float64)
    table = np.cos(np.pi * (2.0 * index[None, :] + 1.0) * index[:, None] / (2.0 * length))
    table = table * np.sqrt(2.0 / length)
    table[0] /= np.sqrt(2.0)
    return table


def cube_tables():
    small = dct_matrix(8)
    cube = np.kron(np.kron(small, small), small).astype(np.float32)
    return cube.astype(jnp.bfloat16), cube.T.astype(jnp.bfloat16)


def half_cosines(n):
    return [float(2.0 * np.cos(np.pi * (2 * i + 1) / (2 * n))) for i in range(n // 2)]


def cosine_sums(x):
    n = len(x)
    if n == 2:
        return [x[0] + x[1], (x[0] - x[1]) * float(np.cos(np.pi / 4))]
    half = n // 2
    even = cosine_sums([x[i] + x[n - 1 - i] for i in range(half)])
    turned = cosine_sums([(x[i] - x[n - 1 - i]) * f for i, f in enumerate(half_cosines(n))])
    out = [None] * n
    for k in range(half):
        out[2 * k] = even[k]
        out[2 * k + 1] = turned[k] - out[2 * k - 1] if k else 0.5 * turned[0]
    return out


def cosine_sums_transposed(y):
    n = len(y)
    if n == 2:
        odd = y[1] * float(np.cos(np.pi / 4))
        return [y[0] + odd, y[0] - odd]
    half = n // 2
    even = cosine_sums_transposed(y[0::2])
    tail = [None] * half
    for k in reversed(range(half)):
        tail[k] = y[2 * k + 1] - tail[k + 1] if k + 1 < half else y[2 * k + 1]
    tail[0] = 0.5 * tail[0]
    odd = [o * f for o, f in zip(cosine_sums_transposed(tail), half_cosines(n))]
    return [even[i] + odd[i] for i in range(half)] + [even[i] - odd[i] for i in reversed(range(half))]


def scales(n):
    return [float(np.sqrt((1.0 if k == 0 else 2.0) / n)) for k in range(n)]


def flip(value, mask):
    if isinstance(mask, int):
        for bit in (1 << b for b in range(mask.bit_length())):
            if mask & bit:
                value = value + bit - 2 * bit * lax.rem(value // bit, 2)
        return value
    for bit in (1, 2):
        value = value + bit * lax.rem(mask // bit, 2) * (1 - 2 * lax.rem(value // bit, 2))
    return value


def lowest(d, count):
    return d & -d if d else count


class Place:
    def __init__(self, count, parts):
        self.parts, self.ranks = parts, count // parts
        me = lax.axis_index("space")
        self.part, self.rank = me // self.ranks, lax.rem(me, self.ranks)
        self.bits = [1 << b for b in range(self.ranks.bit_length() - 1)]

    def index(self, off, d):
        return flip(self.part, off) * self.ranks + flip(self.rank, d)

    def device(self, off, d):
        return {"space": self.index(off, d)}

    def peers(self):
        return [(off, 0) for off in range(1, self.parts)] + [(0, d) for d in range(1, self.ranks)]

    def greet(self):
        barrier = pltpu.get_barrier_semaphore()
        for off, d in self.peers():
            pl.semaphore_signal(barrier, inc=1, device_id=self.device(off, d), device_id_type=MESH)

    def meet(self):
        pl.semaphore_wait(pltpu.get_barrier_semaphore(), len(self.peers()))


def remote(src, dst, send, recv, device):
    return pltpu.make_async_remote_copy(
        src_ref=src, dst_ref=dst, send_sem=send, recv_sem=recv, device_id=device, device_id_type=MESH
    )


def piece_of(ref, h):
    size = ref.shape[0] // PIECES
    return ref.at[pl.ds(h * size, size), :]


class Spread:
    def __init__(self, place, stage, got, table, send, recv):
        self.place, self.stage, self.got, self.table = place, stage, got, table
        self.send, self.recv, self.started = send, recv, []

    def block(self, off, d):
        return self.stage.at[0] if off == 0 and d == 0 else self.got.at[off, d]

    def pass_on(self, off, d, h):
        place = self.place
        for bit in reversed(place.bits):
            if bit < lowest(d, place.ranks):
                copy = remote(
                    piece_of(self.block(off, d), h),
                    piece_of(self.got.at[off, d | bit], h),
                    self.send.at[off, d | bit, h],
                    self.recv.at[off, d | bit, h],
                    place.device(0, bit),
                )
                copy.start()
                self.started.append(copy)

    def orders(self, hs):
        return itertools.product(range(self.place.parts), hs)

    def transform(self, hs, rows, cube_t):
        size = rows.shape[0] // PIECES
        for off, h in self.orders(hs):
            columns = pl.ds(pl.multiple_of(flip(self.place.part, off) * LANES, LANES), LANES)
            part = rows[h * size : (h + 1) * size, :]
            spec = jnp.dot(part, cube_t[:, columns], preferred_element_type=jnp.float32)
            piece_of(self.stage.at[off], h)[...] = spec.astype(self.stage.dtype)

    def begin(self, hs):
        for off, h in self.orders(hs):
            if off == 0:
                self.pass_on(0, 0, h)
                continue
            copy = remote(
                piece_of(self.stage.at[off], h),
                piece_of(self.got.at[off, 0], h),
                self.send.at[off, 0, h],
                self.recv.at[off, 0, h],
                self.place.device(off, 0),
            )
            copy.start()
            self.started.append(copy)

    def widen(self, off, d, h):
        source = piece_of(self.block(off, d), h)
        held = self.stage.shape[1]
        size = held // PIECES
        first = self.place.index(off, d) * held + h * size
        rows = pl.ds(pl.multiple_of(first, size), size)
        self.table[rows, :] = source[...].astype(jnp.float32)

    def finish(self, then=None):
        place = self.place

        def when(key):
            off, d, h = key
            return off + 0.5 * h + sum(2.2 if b == 1 else 1.6 for b in place.bits if d & b)

        keys = [
            (off, d, h)
            for off in range(place.parts)
            for d in range(place.ranks)
            for h in range(PIECES)
            if off or d
        ]
        for h in range(PIECES):
            self.widen(0, 0, h)
        for off, d, h in sorted(keys, key=when):
            piece = piece_of(self.got.at[off, d], h)
            remote(
                piece, piece, self.send.at[off, d, h], self.recv.at[off, d, h], place.device(off, d)
            ).wait_recv()
            self.pass_on(off, d, h)
            self.widen(off, d, h)
            if then is not None and (off, d, h) == (place.parts - 1, 0, PIECES - 1):
                then()

    def close(self):
        for copy in self.started:
            copy.wait_send()


def spread_scratch(count, parts, held, dtype):
    ranks = count // parts
    return [
        pltpu.VMEM((parts, held, LANES), dtype),
        pltpu.VMEM((parts, ranks, held, LANES), dtype),
        pltpu.VMEM((count * held, LANES), jnp.float32),
        SEMS((parts, ranks, PIECES)),
        SEMS((parts, ranks, PIECES)),
    ]


def pick_rows(table, lists, t, some, picked):
    src, row = t // (some // SUBS), lax.rem(t, some // SUBS)
    for q in range(SUBS):
        for m in range(picked.shape[0]):
            spot = lists[m][src, row * SUBS + q]
            picked[m, q : q + 1, :] = table[pl.ds(spot, 1), :]


def to_scalars(lists, scalars, sem):
    copies = [pltpu.make_async_copy(lists.at[m], each, sem.at[m]) for m, each in enumerate(scalars)]
    for copy in copies:
        copy.start()
    return copies


def find_equals(lists, same, group, some):
    for src in range(lists.shape[0]):
        rows = lists[src]
        equal = [jnp.where(rows == pltpu.roll(rows, back, 0), 1.0, 0.0) for back in range(1, group // STREAMS)]
        equal.append(jnp.zeros((LANES - group * len(equal), LANES), jnp.float32))
        same[src * some : (src + 1) * some, :] = jnp.concatenate(equal, axis=0).T[:some, :]


def diagonal(rows):
    shape = (rows, LANES)
    return lax.broadcasted_iota(jnp.int32, shape, 0) == lax.broadcasted_iota(jnp.int32, shape, 1)


def shrink_groups(place, second, width, some, table, lists, sigma, first, other, members, coeffs, back, same, energy, ebuf, egot, weights, send, recv, then=None):
    group, refs = members.shape[:2]
    factor = scales(group)
    columns = pl.ds(pl.multiple_of(place.part * LANES, LANES), LANES)
    own = sigma[:, columns]
    level = own * own if second else (shrink_level * own) * (shrink_level * own)

    def forward(b, picked):
        rows = pl.ds(pl.multiple_of(b * SUBS, SUBS), SUBS)
        values = cosine_sums([picked[m] for m in range(group)])
        total = None
        for j in range(group):
            value = values[j] * factor[j]
            square = value * value
            gain = square / (square + level)
            power = gain * gain
            total = power if total is None else total + power
            if second:
                members[j, rows, :] = gain * coeffs[j, rows, :]
            else:
                coeffs[j, rows, :] = value
                members[j, rows, :] = gain * value
        energy[rows, :] = total * level if second else total

    blocks = refs // SUBS
    pick_rows(table, lists, 0, some, first)

    def pair(i, carry):
        pick_rows(table, lists, 2 * i + 1, some, other)
        forward(2 * i, first)
        pick_rows(table, lists, jnp.minimum(2 * i + 2, blocks - 1), some, first)
        forward(2 * i + 1, other)
        return carry

    lax.fori_loop(0, blocks // 2, pair, 0, unroll=2)
    if then is not None:
        then()
    parts = refs // some
    for src in range(parts):
        column = jnp.sum(energy[src * some : (src + 1) * some, :], axis=1, keepdims=True)
        ebuf[src : src + 1, :] = jnp.sum(jnp.where(diagonal(some), column, 0.0), axis=0, keepdims=True)
    started = []
    for off in range(1, place.parts):
        copy = remote(ebuf, egot.at[off], send.at[off], recv.at[off], place.device(off, 0))
        copy.start()
        started.append(copy)

    def inverse(b, carry):
        rows = pl.ds(pl.multiple_of(b * 2 * SUBS, 2 * SUBS), 2 * SUBS)
        values = cosine_sums_transposed([members[j, rows, :] * factor[j] for j in range(group)])
        for m in range(group):
            merged = values[m]
            for before in range(1, m % (group // STREAMS) + 1):
                lane = (before - 1) * group + m
                merged = merged + same[rows, lane : lane + 1] * values[m - before]
            back[m, rows, :] = merged.astype(back.dtype)
        return carry

    lax.fori_loop(0, refs // (2 * SUBS), inverse, 0)
    total = ebuf[...]
    for off in range(1, place.parts):
        remote(ebuf, egot.at[off], send.at[off], recv.at[off], place.device(off, 0)).wait_recv()
        total = total + egot[off]
    weights[...] = 1.0 / (0.25 + total / (group * width))
    for copy in started:
        copy.wait_send()


def shrink_scratch(parts, group, refs):
    assert parts <= SUBS
    return [
        pltpu.VMEM((group, SUBS, LANES), jnp.float32),
        pltpu.VMEM((group, SUBS, LANES), jnp.float32),
        pltpu.VMEM((group, refs, LANES), jnp.float32),
        pltpu.VMEM((refs, LANES), jnp.float32),
        pltpu.VMEM((SUBS, LANES), jnp.float32),
        pltpu.VMEM((parts, SUBS, LANES), jnp.float32),
        SEMS((parts,)),
        SEMS((parts,)),
    ]


def first_kernel(count, x_in, home_in, ids_in, sigma_in, cube_in, coeffs_out, back, weights, same, turned, *scratch):
    stage, got, table, send, recv = scratch[:5]
    first, other, members, energy, ebuf, egot, esend, erecv = scratch[5:13]
    x, cube_t, sigma, ids, insem = scratch[13:18]
    coeffs, csem, home, named, lists_v, lsend, lrecv, lsem = scratch[18:26]
    scalars = scratch[26:]
    parts = stage.shape[0]
    group, some = ids.shape
    place = Place(count, parts)
    pairs = [(x_in, x), (cube_in, cube_t), (home_in, home), (ids_in, ids), (sigma_in, sigma)]
    fetches = [pltpu.make_async_copy(src, dst, insem.at[i]) for i, (src, dst) in enumerate(pairs)]
    for fetch in fetches:
        fetch.start()
    place.greet()
    for fetch in fetches[:2]:
        fetch.wait()
    spread = Spread(place, stage, got, table, send, recv)
    spread.transform(range(PIECES), x, cube_t)
    place.meet()
    spread.begin(range(PIECES))

    def look_up(row, carry):
        for q in range(SUBS):
            for m in range(group):
                named[m, row * SUBS + q] = home[ids[m, row * SUBS + q]]
        return carry

    for fetch in fetches[2:]:
        fetch.wait()
    lax.fori_loop(0, some // SUBS, look_up, 0)

    def fill(m, carry):
        for q in range(some, LANES):
            named[m, q] = 0
        return carry

    lax.fori_loop(0, group, fill, 0)

    ebuf[...] = jnp.zeros(ebuf.shape, ebuf.dtype)
    mine = pltpu.make_async_copy(named, lists_v.at[place.part], lsem.at[0])
    mine.start()
    mine.wait()
    started = []
    for off in range(1, parts):
        copy = remote(
            lists_v.at[place.part],
            lists_v.at[place.part],
            lsend.at[off],
            lrecv.at[off],
            place.device(off, 0),
        )
        copy.start()
        started.append(copy)
    copies = []

    def lists_ready():
        for off in range(1, parts):
            source = lists_v.at[flip(place.part, off)]
            remote(source, source, lsend.at[off], lrecv.at[off], place.device(off, 0)).wait_recv()
        turned[...] = jnp.zeros(turned.shape, turned.dtype)
        for m in range(group):
            for src in range(parts):
                turned[m, src : src + 1, :] = lists_v[src, m : m + 1, :]
        find_equals(lists_v, same, group, some)
        copies.extend(to_scalars(turned, scalars, lsem))

    spread.finish(lists_ready)
    for copy in copies:
        copy.wait()
    store = pltpu.make_async_copy(coeffs, coeffs_out, csem.at[0])
    shrink_groups(
        place, False, x.shape[1], some, table, scalars, sigma, first, other, members, coeffs, back, same, energy, ebuf, egot, weights, esend, erecv, store.start
    )
    store.wait()
    for copy in started:
        copy.wait_send()
    spread.close()


class Collect:
    def __init__(self, place, acc, got, sent, zgot, send, recv):
        self.place, self.acc, self.got, self.sent, self.zgot = place, acc, got, sent, zgot
        self.send, self.recv, self.started = send, recv, []
        self.order = sorted(range(1, place.parts), key=lambda off: (off % 2, off)) + [0]

    def start(self, copy):
        copy.start()
        self.started.append(copy)

    def begin(self):
        place = self.place
        for d in sorted(range(1, place.ranks, 2), key=lambda d: lowest(d - 1, place.ranks)):
            for off in self.order:
                for h in range(PIECES):
                    self.start(
                        remote(
                            piece_of(self.acc.at[place.index(off, d)], h),
                            piece_of(self.got.at[off, d], h),
                            self.send.at[off, d, h],
                            self.recv.at[off, d, h],
                            place.device(0, 1),
                        )
                    )

    def value(self, off, d, h):
        place = self.place
        total = piece_of(self.acc.at[place.index(off, d)], h)[...].astype(jnp.float32)
        for bit in place.bits:
            if bit < lowest(d, place.ranks):
                piece = piece_of(self.got.at[off, d | bit], h)
                remote(
                    piece, piece, self.send.at[off, d | bit, h], self.recv.at[off, d | bit, h], place.device(0, bit)
                ).wait_recv()
                total = total + piece[...].astype(jnp.float32)
        return total

    def run(self):
        for level in self.place.bits[1:] + [self.place.ranks]:
            self.hand_on([d for d in range(0, self.place.ranks, 2) if lowest(d, self.place.ranks) == level])

    def hand_on(self, ds):
        place = self.place
        for d, off, h in itertools.product(ds, self.order, range(PIECES)):
            piece = piece_of(self.sent.at[off, d // 2], h)
            piece[...] = self.value(off, d, h).astype(self.sent.dtype)
            if d == 0 and off == 0:
                continue
            bit = lowest(d, 0)
            self.start(
                remote(
                    piece,
                    piece_of(self.got.at[off, d] if d else self.zgot.at[off], h),
                    self.send.at[off, d, h],
                    self.recv.at[off, d, h],
                    place.device(0, bit) if d else place.device(off, 0),
                )
            )

    def slices(self, h):
        place = self.place
        yield 0, piece_of(self.sent.at[0, 0], h)[...]
        for off in range(1, place.parts):
            piece = piece_of(self.zgot.at[off], h)
            remote(
                piece, piece, self.send.at[off, 0, h], self.recv.at[off, 0, h], place.device(off, 0)
            ).wait_recv()
            yield off, piece[...]

    def close(self):
        for copy in self.started:
            copy.wait_send()


def weigh_rows(place, some, held, turned, weights, wsum):
    parts = place.parts
    group = turned.shape[0]
    many = wsum.shape[0] * (held // LANES)
    lane = lax.broadcasted_iota(jnp.int32, (1, LANES), 1)
    heavy = [jnp.where(lane < some, weights[src : src + 1, :], 0.0) for src in range(parts)]
    tall = lax.broadcasted_iota(jnp.int32, (many, LANES), 0)
    low = lax.broadcasted_iota(jnp.int32, (LANES, LANES), 0)
    first = place.part * (many * LANES)

    def weigh(m, total):
        ones, loads = [], []
        for src in range(parts):
            spots = turned[m, src : src + 1, :] - first
            loads.append(jnp.where((spots >> 7) == tall, heavy[src], 0.0).astype(jnp.bfloat16))
            ones.append(jnp.where((spots & (LANES - 1)) == low, 1.0, 0.0).astype(jnp.bfloat16))
        return total + lax.dot_general(
            jnp.concatenate(loads, axis=1),
            jnp.concatenate(ones, axis=1),
            (((1,), (1,)), ((), ())),
            preferred_element_type=jnp.float32,
        )

    total = lax.fori_loop(0, group, weigh, jnp.zeros((many, LANES), jnp.float32), unroll=True)
    per = held // LANES
    for b in range(wsum.shape[0]):
        wsum[b, :per, :] = total[b * per : (b + 1) * per, :]
        if per < SUBS:
            wsum[b, per:, :] = jnp.zeros((SUBS - per, LANES), jnp.float32)


def settle(place, some, turned, weights, acc, noisy, cube, out, wsum, got, sent, zgot, wgot, send, recv, wsend, wrecv, then=None):
    held = noisy.shape[0]
    collect = Collect(place, acc, got, sent, zgot, send, recv)
    place.greet()
    weigh_rows(place, some, held, turned, weights, wsum)
    place.meet()
    collect.begin()
    for d in range(1, place.ranks):
        collect.start(
            remote(wsum.at[flip(place.rank, d)], wgot.at[d], wsend.at[d], wrecv.at[d], place.device(0, d))
        )
    collect.run()
    denom = wsum[place.rank]
    for d in range(1, place.ranks):
        remote(wgot.at[d], wgot.at[d], wsend.at[d], wrecv.at[d], place.device(0, d)).wait_recv()
        denom = denom + wgot[d]
    size = held // PIECES
    for h in range(PIECES):
        numer = prior_weight * noisy[pl.ds(h * size, size), :].astype(jnp.float32)
        for off, part in collect.slices(h):
            rows = pl.ds(pl.multiple_of(flip(place.part, off) * LANES, LANES), LANES)
            numer = numer + jnp.dot(part, cube[rows, :], preferred_element_type=jnp.float32)
        for j in range(size // LANES):
            row = h * (size // LANES) + j
            spread = jnp.broadcast_to(denom[row : row + 1, :], (LANES, LANES))
            column = jnp.sum(jnp.where(diagonal(LANES), spread, 0.0), axis=1, keepdims=True)
            out[pl.ds(row * LANES, LANES), :] = (
                numer[j * LANES : (j + 1) * LANES, :] / (column + prior_weight)
            ).astype(out.dtype)
        if then is not None:
            then(h)
    return collect


def settle_scratch(count, parts, held, dtype):
    ranks = count // parts
    half = (parts, ranks // 2, held, LANES)
    return [
        pltpu.VMEM((ranks, SUBS, LANES), jnp.float32),
        pltpu.VMEM((parts, ranks, held, LANES), dtype),
        pltpu.VMEM(half, dtype),
        pltpu.VMEM((parts, held, LANES), dtype),
        pltpu.VMEM((ranks, SUBS, LANES), jnp.float32),
        SEMS((parts, ranks, PIECES)),
        SEMS((parts, ranks, PIECES)),
        SEMS((ranks,)),
        SEMS((ranks,)),
    ]


def second_kernel(count, some, acc, weights_in, noisy, cube, cube_t, sigma, turned, same, coeffs_in, basic, back, weights, *scratch):
    stage, got, table, send, recv = scratch[:5]
    first, other, members, energy, ebuf, egot, esend, erecv = scratch[5:13]
    coeffs, csem, lsem = scratch[13:16]
    group = members.shape[0]
    scalars = scratch[16 : 16 + group]
    parts = stage.shape[0]
    place = Place(count, parts)
    fetch = pltpu.make_async_copy(coeffs_in, coeffs, csem.at[0])
    fetch.start()
    copies = to_scalars(turned, scalars, lsem)
    spread = Spread(place, stage, got, table, send, recv)
    ebuf[...] = jnp.zeros(ebuf.shape, ebuf.dtype)
    def spread_piece(h):
        spread.transform([h], basic, cube_t)
        spread.begin([h])

    collect = settle(
        place,
        some,
        turned,
        weights_in,
        acc,
        noisy,
        cube,
        basic,
        *scratch[16 + group :],
        then=spread_piece,
    )
    spread.finish()
    for copy in copies:
        copy.wait()
    fetch.wait()
    shrink_groups(
        place, True, noisy.shape[1], some, table, scalars, sigma, first, other, members, coeffs, back, same, energy, ebuf, egot, weights, esend, erecv
    )
    collect.close()
    spread.close()


def third_kernel(count, parts, some, acc, weights, noisy, cube, turned, out, *scratch):
    settle(Place(count, parts), some, turned, weights, acc, noisy, cube, out, *scratch).close()


def add_kernel(some, carried, turned, weights, back, *refs):
    group, refs_here = back.shape[:2]
    parts = refs_here // some
    kept = refs[:carried]
    acc = refs[carried]
    outs = refs[carried + 1 : 2 * carried + 1]
    heavy, ksem, lsem = refs[2 * carried + 1 : 2 * carried + 4]
    scalars = refs[2 * carried + 4 : 2 * carried + 4 + group]
    sums = refs[2 * carried + 4 + group :]
    blocks, held = acc.shape[:2]
    copies = to_scalars(turned, scalars, lsem)
    moves = [pltpu.make_async_copy(src, dst, ksem.at[i]) for i, (src, dst) in enumerate(zip(kept, outs))]
    for move in moves:
        move.start()

    def clear(i, carry):
        rows = pl.ds(pl.multiple_of(i * LANES, LANES), LANES)
        for each in sums:
            each[rows, :] = jnp.zeros((LANES, LANES), jnp.float32)
        return carry

    lax.fori_loop(0, blocks * held // LANES, clear, 0)
    for src in range(parts):
        row = jnp.broadcast_to(weights[src : src + 1, :], (some, LANES))
        column = jnp.sum(jnp.where(diagonal(some), row, 0.0), axis=1, keepdims=True)
        heavy[src * some : (src + 1) * some, :] = jnp.broadcast_to(column, (some, LANES))
    together = group // STREAMS
    for copy in copies:
        copy.wait()

    def step(t, carry):
        src, row = t // (some // SUBS), lax.rem(t, some // SUBS)
        for q in range(SUBS):
            spots, news = [], []
            weight = heavy[pl.ds(t * SUBS + q, 1), :]
            for m in range(group):
                spot = scalars[m][src, row * SUBS + q]
                spots.append(spot)
                each = weight * back[m, pl.ds(t * SUBS + q, 1), :]
                news.append(sums[m // together][pl.ds(spot, 1), :] + each)
            for m in range(group):
                sums[m // together][pl.ds(spots[m], 1), :] = news[m]
        return carry

    lax.fori_loop(0, refs_here // SUBS, step, 0)

    def store(b, carry):
        for i in range(held // LANES):
            rows = pl.ds(pl.multiple_of(b * held + i * LANES, LANES), LANES)
            whole = sums[0][rows, :]
            for each in sums[1:]:
                whole = whole + each[rows, :]
            acc[b, i * LANES : (i + 1) * LANES, :] = whole.astype(acc.dtype)
        return carry

    lax.fori_loop(0, blocks, store, 0)
    for move in moves:
        move.wait()


def shape(*dims, dtype=jnp.float32):
    return jax.ShapeDtypeStruct(dims, dtype)


def params(rows, collective_id=None):
    limit = 5 * rows * LANES * 4 + (10 << 20)
    return pltpu.CompilerParams(
        collective_id=collective_id, has_side_effects=collective_id is not None, vmem_limit_bytes=limit
    )


def add_up(count, some, held, dtype, turned, weights, back, *kept):
    group, refs = back.shape[:2]
    return pl.pallas_call(
        functools.partial(add_kernel, some, len(kept)),
        out_shape=[shape(count, held, LANES, dtype=dtype)]
        + [shape(*each.shape, dtype=each.dtype) for each in kept],
        in_specs=[VMEM] * (3 + len(kept)),
        out_specs=[VMEM] + [HBM] * len(kept),
        scratch_shapes=[pltpu.VMEM((refs, LANES), jnp.float32), SEMS((1,)), SEMS((group,))]
        + [pltpu.SMEM((SUBS, LANES), jnp.int32)] * group
        + [pltpu.VMEM((count * held, LANES), jnp.float32)] * STREAMS,
        compiler_params=params(count * held),
        name="add_up",
    )(turned, weights, back, *kept)


def body(noisy, matches, cube_home, sigma_coef):
    count = lax.axis_size("space")
    some, group = matches.shape
    held, width = noisy.shape
    parts = width // LANES
    refs = parts * some
    cube, cube_t = cube_tables()
    sigma = sigma_coef[None, :]
    dtype = noisy.dtype
    shared = spread_scratch(count, parts, held, dtype) + shrink_scratch(parts, group, refs)
    coeffs, back, weights, same, turned = pl.pallas_call(
        functools.partial(first_kernel, count),
        out_shape=[
            shape(group, refs, LANES),
            shape(group, refs, LANES),
            shape(SUBS, LANES),
            shape(refs, LANES),
            shape(group, SUBS, LANES, dtype=jnp.int32),
        ],
        in_specs=[HBM] * 5,
        out_specs=[HBM] + [VMEM] * 4,
        scratch_shapes=shared
        + [
            pltpu.VMEM(noisy.shape, dtype),
            pltpu.VMEM(cube_t.shape, dtype),
            pltpu.VMEM(sigma.shape, jnp.float32),
            pltpu.SMEM((group, some), jnp.int32),
            SEMS((5,)),
            pltpu.VMEM((group, refs, LANES), jnp.float32),
            SEMS((1,)),
            pltpu.SMEM(cube_home.shape, jnp.int32),
            pltpu.SMEM((group, LANES), jnp.int32),
            pltpu.VMEM((parts, group, LANES), jnp.int32),
            SEMS((parts,)),
            SEMS((parts,)),
            SEMS((group,)),
        ]
        + [pltpu.SMEM((SUBS, LANES), jnp.int32)] * group,
        compiler_params=params(count * held, 0),
        name="shrink",
    )(*[pltpu.with_memory_space_constraint(v, pltpu.HBM) for v in (noisy, cube_home, matches.T, sigma, jnp.asarray(cube_t))])
    (acc,) = add_up(count, some, held, dtype, turned, weights, back)
    basic, back, weights = pl.pallas_call(
        functools.partial(second_kernel, count, some),
        out_shape=[
            shape(held, width, dtype=dtype),
            shape(group, refs, LANES),
            shape(SUBS, LANES),
        ],
        in_specs=[VMEM] * 8 + [HBM],
        out_specs=[VMEM] * 3,
        scratch_shapes=shared
        + [pltpu.VMEM((group, refs, LANES), jnp.float32), SEMS((1,)), SEMS((group,))]
        + [pltpu.SMEM((SUBS, LANES), jnp.int32)] * group
        + settle_scratch(count, parts, held, dtype),
        compiler_params=params(count * held, 1),
        name="wiener",
    )(acc, weights, noisy, cube, cube_t, sigma, turned, same, coeffs)
    acc, basic = add_up(count, some, held, dtype, turned, weights, back, basic)
    final = pl.pallas_call(
        functools.partial(third_kernel, count, parts, some),
        out_shape=shape(held, width, dtype=dtype),
        in_specs=[VMEM] * 5,
        out_specs=VMEM,
        scratch_shapes=settle_scratch(count, parts, held, dtype),
        compiler_params=params(count * held, 2),
        name="settle",
    )(acc, weights, noisy, cube, turned)
    return basic, final


def solution(mesh):
    in_specs = (P(("groups", "space"), None), P(("groups", "space"), None), P("groups"), P())
    out_specs = (P(("groups", "space"), None), P(("groups", "space"), None))
    return jax.shard_map(body, mesh=mesh, in_specs=in_specs, out_specs=out_specs, check_vma=False)
```
